32 devices in a mesh: dp: 8 (over z, x), expert: 4 (over y, core).
Axes of the slice: x: 2, y: 2, z: 4, core: 2. Of those that a mesh axis runs over, the one named last changes fastest.
Arguments:
- layer_input: bfloat16 [2, 32, 96, 1152], P(None, ('dp', 'expert')), may hold values from -6 to 6
- segments: int32 [2, 32, 96], P(None, ('dp', 'expert')), may hold values from 0 to 1, never falling along the last dimension, each value on 1 to 72 neighbouring positions
- routes: int32 [2, 32, 96, 1], P(None, ('dp', 'expert')), may hold values from 0 to 3
- cotangent: bfloat16 [2, 32, 96, 1152], P(None, ('dp', 'expert')), may hold values from -6 to 6
- norm1_gain: bfloat16 [1152], replicated, may hold values from 0.5 to 1.5
- in_weight: bfloat16 [4608, 1152], P('dp'), may hold values from -0.1875 to 0.1875
- conv_weight: bfloat16 [4, 2304], P(None, ('dp', 'expert')), may hold values from -0.5 to 0.5
- conv_bias: bfloat16 [2304], P(('dp', 'expert')), may hold values from -0.5 to 0.5
- xproj_weight: bfloat16 [2304, 104], P(('dp', 'expert')), may hold values from -0.5 to 0.5
- dtproj_weight: bfloat16 [72, 2304], P(None, ('dp', 'expert')), may hold values from -0.75 to 0.75
- dt_bias: bfloat16 [2304], P(('dp', 'expert')), may hold values from -5 to -1.5
- a_log: bfloat16 [16, 2304], P(None, ('dp', 'expert')), may hold values from 0 to 2.765625
- skip_gain: bfloat16 [2304], P(('dp', 'expert')), may hold values from 0.5 to 1.5
- out_weight: bfloat16 [2304, 1152], P('dp'), may hold values from -0.375 to 0.375
- norm2_gain: bfloat16 [1152], replicated, may hold values from 0.5 to 1.5
- router_weight: bfloat16 [1152, 4], replicated, may hold values from -0.125 to 0.125
- up_weight: bfloat16 [4, 3072, 1152], P('expert', 'dp'), may hold values from -0.1875 to 0.1875
- down_weight: bfloat16 [4, 3072, 1152], P('expert', 'dp'), may hold values from -0.875 to 0.875
Outputs:
- layer_output: bfloat16 [2, 32, 96, 1152], P(None, ('dp', 'expert'))
- input_grad: float32 [2, 32, 96, 1152], P(None, ('dp', 'expert'))
- norm1_gain_grad: float32 [1152], replicated
- in_weight_grad: float32 [4608, 1152], P('dp')
- conv_weight_grad: float32 [4, 2304], P(None, ('dp', 'expert'))
- conv_bias_grad: float32 [2304], P(('dp', 'expert'))
- xproj_weight_grad: float32 [2304, 104], P(('dp', 'expert'))
- dtproj_weight_grad: float32 [72, 2304], P(None, ('dp', 'expert'))
- dt_bias_grad: float32 [2304], P(('dp', 'expert'))
- a_log_grad: float32 [16, 2304], P(None, ('dp', 'expert'))
- skip_gain_grad: float32 [2304], P(('dp', 'expert'))
- out_weight_grad: float32 [2304, 1152], P('dp')
- norm2_gain_grad: float32 [1152], replicated
- router_weight_grad: float32 [1152, 4], replicated
- up_weight_grad: float32 [4, 3072, 1152], P('expert', 'dp')
- down_weight_grad: float32 [4, 3072, 1152], P('expert', 'dp')
The draws below stay inside these ranges and needn't reach their ends.
Inputs may be any that keep to these rules, and one draw needn't show every extreme that they name: `segments`: segment numbers of a sequence start at 0 and never fall; a document has at most 72 positions.
All inputs are finite; a program needn't handle non-finite values.
Results may differ from the reference program's by a relative error of at most 0.02.
Values may be sent and summed in bfloat16 or wider, within the bound.
No kernel may reach another device: no remote copies, remote signals or barrier semaphores. Data moves between devices by JAX's collectives and lax.ppermute only.
A program may use at most 192 MiB of HBM per device.

```python
import math
import jax
import jax.numpy as jnp
import numpy as np
from jax import lax

D = 1152
DI = 2304
NS = 16
RK = 72
KC = 4
FF = 3072
SEQ = 96
MICRO = 2
CH = 16
EXPERTS = 4
BATCH = 32
CAP = 30
DOCS = 2
DOC_MOST = 72


def block_scale(own_key, extent, cuts, least, largest):
    loudness = 1.0
    for position, blocks in cuts:
        draws = jax.random.uniform(jax.random.fold_in(jax.random.fold_in(own_key, 6), position), (blocks,), jnp.float32, least / len(cuts), largest / len(cuts))
        loudness = loudness * jnp.repeat(jnp.exp(draws), extent[position] // blocks).reshape((-1,) + (1,) * (len(extent) - 1 - position))
    return loudness


def choose_distinct(stream_key, rows, number_of, top, lift):
    order = jax.random.permutation(jax.random.fold_in(stream_key, 1), number_of)
    boost = order
    for power in range(3):
        boost = boost * boost // number_of
    boost = boost * lift // number_of
    chance = jax.random.randint(jax.random.fold_in(stream_key, 2), (rows, number_of), 0, 4096) + boost
    sure = jax.random.permutation(jax.random.fold_in(stream_key, 3), rows)[jnp.arange(number_of) % rows]
    chance = jnp.where(jnp.arange(rows)[:, None] == sure[None, :], 1 << 14, chance)
    priority = chance * number_of + jnp.arange(number_of)
    return lax.top_k(priority.astype(jnp.int32), top)[1].astype(jnp.int32)


def length_profile(count, total, reach, skew):
    portions = [(1 << 20) // math.isqrt(grade ** skew) + 1 for grade in range(2, count + 1)]
    spare, given = total - reach - (count - 1), [1] * (count - 1)
    while spare > 0:
        free = [i for i in range(count - 1) if given[i] < reach]
        whole, budget = sum([portions[i] for i in free]), spare
        for i in free:
            addition = min(reach - given[i], max(1, budget * portions[i] // whole), spare)
            given[i] = given[i] + addition
            spare = spare - addition
    return np.array([reach] + given)


def uneven_parts(stream_key, amount, total, reach, slope):
    if amount == 2:
        one = jax.random.randint(stream_key, (), max(1, total - reach), min(reach, total - 1) + 1)
        return jnp.stack([one, total - one])
    lengths = jnp.asarray(length_profile(amount, total, reach, slope), jnp.int32)
    twos = (amount - 1) // 2
    donor, receiver = lengths[1:1 + 2 * twos:2], lengths[2:2 + 2 * twos:2]
    margin = jnp.minimum(donor - 1, reach - receiver)
    moved = jax.random.randint(jax.random.fold_in(stream_key, 1), (twos,), 0, 1 << 20) % (margin + 1)
    lengths = lengths.at[1:1 + 2 * twos:2].set(donor - moved).at[2:2 + 2 * twos:2].set(receiver + moved)
    return lengths[jax.random.permutation(jax.random.fold_in(stream_key, 2), amount)]


def noise(stream_key, shape, deviation, reach, shards=(), kind=jnp.bfloat16):
    gain = block_scale(stream_key, shape, shards, -0.22, 0.18) if shards else 1.0
    values = jax.random.normal(stream_key, shape, jnp.float32) * deviation * gain
    return jnp.minimum(jnp.maximum(values, -reach), reach).astype(kind)


def setup_inputs(seed: int = 0) -> dict:
    arg_keys = jax.random.split(jax.random.key(seed), 19)
    layer_input = noise(arg_keys[0], (MICRO, BATCH, SEQ, D), 1.0, 6.0, ((1, 32),))
    segments = jax.vmap(lambda own: jnp.searchsorted(jnp.cumsum(uneven_parts(own, DOCS, SEQ, DOC_MOST, 1)), jnp.arange(SEQ), side="right"))(jax.random.split(arg_keys[1], MICRO * BATCH)).reshape((MICRO, BATCH, SEQ)).astype(jnp.int32)
    routes = choose_distinct(arg_keys[2], MICRO * BATCH * SEQ, EXPERTS, 1, 2048).reshape((MICRO, BATCH, SEQ, 1))
    cotangent = noise(arg_keys[3], (MICRO, BATCH, SEQ, D), 1.0, 6.0, ((1, 32),))
    norm1_gain = jnp.clip(1.0 + 0.1 * jax.random.normal(arg_keys[4], (D,), jnp.float32), 0.5, 1.5).astype(jnp.bfloat16)
    in_weight = noise(arg_keys[5], (2 * DI, D), D ** -0.5, 0.1875, ((0, 8),))
    conv_weight = jnp.clip(jax.random.uniform(arg_keys[6], (KC, DI), jnp.float32, -0.5, 0.5) * block_scale(arg_keys[6], (KC, DI), ((1, 32),), -0.4, 0.0), -0.5, 0.5).astype(jnp.bfloat16)
    conv_bias = jnp.clip(jax.random.uniform(arg_keys[7], (DI,), jnp.float32, -0.5, 0.5) * block_scale(arg_keys[7], (DI,), ((0, 32),), -0.4, 0.0), -0.5, 0.5).astype(jnp.bfloat16)
    xproj_weight = noise(arg_keys[8], (DI, RK + 2 * NS), (DI // 16) ** -0.5, 0.5, ((0, 32),))
    dtproj_weight = noise(arg_keys[9], (RK, DI), RK ** -0.5, 0.75, ((1, 32),))
    dt_bias = jnp.clip(-5.0 + 3.5 * jax.random.uniform(arg_keys[10], (DI,), jnp.float32) ** block_scale(arg_keys[10], (DI,), ((0, 32),), -0.2, 0.2), -5.0, -1.5).astype(jnp.bfloat16)
    a_log = jnp.clip(2.765625 * jax.random.uniform(arg_keys[11], (NS, DI), jnp.float32) ** block_scale(arg_keys[11], (NS, DI), ((1, 32),), -0.2, 0.2), 0.0, 2.765625).astype(jnp.bfloat16)
    skip_gain = jnp.clip(1.0 + 0.1 * jax.random.normal(arg_keys[12], (DI,), jnp.float32), 0.5, 1.5).astype(jnp.bfloat16)
    out_weight = noise(arg_keys[13], (DI, D), (DI // 8) ** -0.5, 0.375, ((0, 8),))
    norm2_gain = jnp.clip(1.0 + 0.1 * jax.random.normal(arg_keys[14], (D,), jnp.float32), 0.5, 1.5).astype(jnp.bfloat16)
    router_weight = noise(arg_keys[15], (D, EXPERTS), (2 * D) ** -0.5, 0.125)
    up_weight = noise(arg_keys[16], (EXPERTS, FF, D), D ** -0.5, 0.1875, ((0, 4), (1, 8)))
    down_weight = noise(arg_keys[17], (EXPERTS, FF, D), (FF // 64) ** -0.5, 0.875, ((0, 4), (1, 8)))
    return dict(layer_input=layer_input, segments=segments, routes=routes, cotangent=cotangent, norm1_gain=norm1_gain, in_weight=in_weight, conv_weight=conv_weight, conv_bias=conv_bias, xproj_weight=xproj_weight, dtproj_weight=dtproj_weight, dt_bias=dt_bias, a_log=a_log, skip_gain=skip_gain, out_weight=out_weight, norm2_gain=norm2_gain, router_weight=router_weight, up_weight=up_weight, down_weight=down_weight)


HIGHEST = lax.Precision.HIGHEST
EPSILON = 1e-05

@jax.custom_vjp
def low(v):
    return lax.optimization_barrier(v.astype(jnp.bfloat16)).astype(jnp.float32)

@jax.custom_vjp
def low_back(v):
    return v

def low_keep(v):
    return (low(v), None)

def low_pass(kept, grad):
    return (grad,)

def back_keep(v):
    return (v, None)

def back_low(kept, grad):
    return (low(grad),)
low.defvjp(low_keep, low_pass)
low_back.defvjp(back_keep, back_low)

def matmul(left_side, right_side):
    return jnp.dot(left_side, right_side, precision=HIGHEST, preferred_element_type=jnp.float32)

def rms_scale(values, gain_row):
    return values * lax.rsqrt(lax.optimization_barrier(jnp.mean(values * values, axis=-1, keepdims=True)) + EPSILON) * gain_row

def gelu_tanh(values):
    return jax.nn.gelu(values, approximate=True)

def same_doc_shift(segment, offset):
    padded = jnp.concatenate([jnp.full((offset,), -1, segment.dtype), segment])[:segment.shape[0]]
    return (padded == segment).astype(jnp.float32)

def conv_silu(inner_part, conv_taps, bias_row, segment):
    length = inner_part.shape[0]
    tap_count = conv_taps.shape[0]
    summed = jnp.zeros_like(inner_part) + bias_row
    for offset in range(tap_count):
        shifted = jnp.pad(inner_part, ((offset, 0), (0, 0)))[:length]
        summed = summed + conv_taps[tap_count - 1 - offset] * shifted * same_doc_shift(segment, offset)[:, None]
    return jax.nn.silu(summed)

def pair_combine(earlier, latter):
    return (earlier[0] * latter[0], latter[0] * earlier[1] + latter[1])

def scan_mix(conv_out, dt_part, dt_shift, b_rows, c_rows, log_rates, skip_row, gate_in, keep_row, block_len):
    delta = jax.nn.softplus(dt_part + dt_shift)
    decay_rate = -jnp.exp(log_rates)
    length = conv_out.shape[0]
    blocks = length // block_len

    def split_blocks(values):
        return values.reshape((blocks, block_len) + values.shape[1:])

    def block_step(state_now, pieces):
        delta_b, conv_b, b_blk, c_blk, keep_b = pieces
        factor = jnp.exp(delta_b[:, None, :] * decay_rate[None]) * keep_b[:, None, None]
        driven = (delta_b * conv_b)[:, None, :] * b_blk[:, :, None]
        cum_factor, local_state = lax.associative_scan(pair_combine, (factor, driven), axis=0)
        states = local_state + cum_factor * state_now[None]
        return (states[-1], lax.optimization_barrier(jnp.sum(c_blk[:, :, None] * states, axis=1)))
    initial = jnp.zeros(decay_rate.shape, jnp.float32)
    final_state, outputs = lax.scan(jax.checkpoint(block_step), initial, (split_blocks(delta), split_blocks(conv_out), split_blocks(b_rows), split_blocks(c_rows), split_blocks(keep_row)))
    mixed_out = outputs.reshape(length, -1) + skip_row * conv_out
    return mixed_out * jax.nn.silu(gate_in)

def norm_route(residual, gain_two, router_full, chosen_rows):
    normed_two = rms_scale(residual, gain_two)
    logits = jnp.dot(normed_two, router_full, precision=HIGHEST, preferred_element_type=jnp.float32)
    probabilities = jax.nn.softmax(logits, axis=-1)
    return (normed_two, lax.optimization_barrier(jnp.sum(probabilities * chosen_rows, axis=1)))

def dispatch_matrix(route_row, expert_count, capacity):
    chosen = (route_row[:, None] == jnp.arange(expert_count, dtype=jnp.int32)[None]).astype(jnp.int32)
    earlier = jnp.cumsum(chosen, axis=0) - chosen
    slot_index = lax.optimization_barrier(jnp.sum(earlier * chosen, axis=1))
    places = (slot_index[:, None] == jnp.arange(capacity, dtype=jnp.int32)[None]).astype(jnp.float32)
    return (chosen.astype(jnp.float32)[:, :, None] * places[:, None, :]).reshape(route_row.shape[0], expert_count * capacity)

def layer_seq(row_input, segment, route_row, params):
    gain_one, in_full, conv_full, convb_full, xproj_full, dtproj_full, dtb_full, alog_full, skip_full, out_full, gain_two, router_full, up_full, down_full = params
    rank_width = dtproj_full.shape[0]
    nstate = alog_full.shape[0]
    inner_width = conv_full.shape[1]
    normed_one = rms_scale(row_input, gain_one)
    joined = low_back(matmul(low(normed_one), in_full.T))
    conv_out = conv_silu(joined[:, :inner_width], conv_full, convb_full, segment)
    projected = low_back(matmul(low(conv_out), xproj_full))
    dt_part = low_back(matmul(low(projected[:, :rank_width]), dtproj_full))
    keep_row = same_doc_shift(segment, 1)
    mixed_out = scan_mix(conv_out, dt_part, dtb_full, projected[:, rank_width:rank_width + nstate], projected[:, rank_width + nstate:], alog_full, skip_full, joined[:, inner_width:], keep_row, CH)
    branch = low_back(matmul(low(mixed_out), out_full))
    residual = row_input + branch
    chosen_rows = (route_row[:, None] == jnp.arange(EXPERTS, dtype=jnp.int32)[None]).astype(jnp.float32)
    normed_two, gate_row = norm_route(residual, gain_two, router_full, chosen_rows)
    placed = dispatch_matrix(route_row, EXPERTS, CAP)
    sent_rows = low_back(low(normed_two))
    slot_rows = jnp.einsum('tk,td->kd', placed, sent_rows, precision=HIGHEST).reshape(EXPERTS, CAP, -1)
    hidden = low_back(jnp.einsum('ecd,efd->ecf', slot_rows, up_full, precision=HIGHEST))
    active = low(gelu_tanh(hidden))
    returned = low(low_back(jnp.einsum('ecf,efd->ecd', active, down_full, precision=HIGHEST)))
    gathered = jnp.einsum('tk,kd->td', placed, returned.reshape(EXPERTS * CAP, -1), precision=HIGHEST)
    return residual + gate_row[:, None] * gathered

def reference(layer_input, segments, routes, cotangent, norm1_gain, in_weight, conv_weight, conv_bias, xproj_weight, dtproj_weight, dt_bias, a_log, skip_gain, out_weight, norm2_gain, router_weight, up_weight, down_weight):
    params = tuple((weight_item.astype(jnp.float32) for weight_item in (norm1_gain, in_weight, conv_weight, conv_bias, xproj_weight, dtproj_weight, dt_bias, a_log, skip_gain, out_weight, norm2_gain, router_weight, up_weight, down_weight)))
    total_seqs = MICRO * BATCH
    group_size = math.gcd(total_seqs, max(1, 2048 // SEQ))
    group_count = total_seqs // group_size
    rows_all = layer_input.astype(jnp.float32).reshape(group_count, group_size, SEQ, D)
    segs_all = segments.reshape(group_count, group_size, SEQ)
    routes_all = routes[..., 0].reshape(group_count, group_size, SEQ)
    cots_all = cotangent.astype(jnp.float32).reshape(group_count, group_size, SEQ, D)

    def run_group(carry, pieces):
        rows_in, seg_in, route_in, cot_in = pieces

        def forward(rows_value, param_values):
            return jax.vmap(layer_seq, in_axes=(0, 0, 0, None))(rows_value, seg_in, route_in, param_values)
        outputs, pullback = jax.vjp(forward, rows_in, params)
        grad_rows, grad_params = pullback(cot_in)
        carry = jax.tree.map(lambda running, addend: running + addend, carry, grad_params)
        return (carry, (outputs.astype(jnp.bfloat16), grad_rows))
    zero_grads = jax.tree.map(jnp.zeros_like, params)
    grads, (out_all, dx_all) = lax.scan(run_group, zero_grads, (rows_all, segs_all, routes_all, cots_all))
    g_norm1, g_in, g_conv, g_convb, g_xproj, g_dtproj, g_dtb, g_alog, g_skip, g_out, g_norm2, g_router, g_up, g_down = grads
    layer_output = out_all.reshape(MICRO, BATCH, SEQ, D)
    input_grad = dx_all.reshape(MICRO, BATCH, SEQ, D)
    return (layer_output, input_grad, g_norm1, g_in, g_conv, g_convb, g_xproj, g_dtproj, g_dtb, g_alog, g_skip, g_out, g_norm2, g_router, g_up, g_down)
```

```python
import jax
import jax.numpy as jnp
from jax import lax
from jax.experimental import pallas as pl
from jax.experimental.pallas import tpu as pltpu
from jax.sharding import PartitionSpec as P

LANES = 128
ROWS = 8

def wide(tile, width):
    return jnp.concatenate([tile] * (width // LANES), axis=1)

def narrow(values):
    total = values[:, :LANES]
    for start in range(LANES, values.shape[1], LANES):
        total = total + values[:, start : start + LANES]
    return total

def fold_states(pieces, position):
    folded = []
    for piece in pieces:
        total = piece[:ROWS]
        for start in range(ROWS, piece.shape[0], ROWS):
            total = total + piece[start : start + ROWS]
        folded.append(total)
    low = (position & 4) == 0
    folded = [
        jnp.where(low, a, b) + pltpu.roll(jnp.where(low, b, a), 4, 0)
        for a, b in zip(folded[:4], folded[4:])
    ]
    for step in (2, 1):
        low = (position & step) == 0
        half = len(folded) // 2
        folded = [
            jnp.where(low, a + pltpu.roll(a, ROWS - step, 0), b + pltpu.roll(b, step, 0))
            for a, b in zip(folded[:half], folded[half:])
        ]
    return folded[0]

def scan_forward(decay_ref, drive_ref, b_ref, c_ref, rate_ref, out_ref):
    length, width = decay_ref.shape[1:]
    rate = rate_ref[...]
    position = lax.broadcasted_iota(jnp.int32, (ROWS, width), 0)

    def block(index, state):
        start = pl.multiple_of(index * ROWS, ROWS)
        pieces = []
        for offset in range(ROWS):
            t = start + offset
            factor = jnp.exp2(decay_ref[0, pl.ds(t, 1), :] * rate)
            state = factor * state + drive_ref[0, pl.ds(t, 1), :] * wide(b_ref[0, t], width)
            pieces.append(state * wide(c_ref[0, t], width))
        out_ref[0, pl.ds(start, ROWS), :] = fold_states(pieces, position)
        return state

    lax.fori_loop(0, length // ROWS, block, jnp.zeros_like(rate))

def scan_backward(
    decay_ref, drive_ref, b_ref, c_ref, rate_ref, dout_ref,
    ddrive_ref, ddecay_ref, drate_ref, db_ref, dc_ref, state_ref, factor_ref,
):
    length, width = decay_ref.shape[1:]
    rate = rate_ref[...]
    position = lax.broadcasted_iota(jnp.int32, (ROWS, width), 0)

    @pl.when(pl.program_id(1) == 0)
    def _():
        db_ref[...] = jnp.zeros_like(db_ref)
        dc_ref[...] = jnp.zeros_like(dc_ref)

    state_ref[0] = jnp.zeros_like(rate)

    def replay(index, state):
        start = pl.multiple_of(index * ROWS, ROWS)
        for offset in range(ROWS):
            t = start + offset
            factor = jnp.exp2(decay_ref[0, pl.ds(t, 1), :] * rate)
            state = factor * state + drive_ref[0, pl.ds(t, 1), :] * wide(b_ref[0, t], width)
            factor_ref[t] = factor
            state_ref[t + 1] = state
        return state

    lax.fori_loop(0, length // ROWS, replay, jnp.zeros_like(rate))

    def block(index, carried):
        later, drate = carried
        start = pl.multiple_of(length - ROWS - index * ROWS, ROWS)
        drive_pieces = [None] * ROWS
        decay_pieces = [None] * ROWS
        for offset in reversed(range(ROWS)):
            t = start + offset
            dout = dout_ref[0, pl.ds(t, 1), :]
            dstate = later + dout * wide(c_ref[0, t], width)
            dc_ref[0, t] += narrow(dout * state_ref[t + 1])
            db_ref[0, t] += narrow(dstate * drive_ref[0, pl.ds(t, 1), :])
            drive_pieces[offset] = dstate * wide(b_ref[0, t], width)
            later = dstate * factor_ref[t]
            power = later * state_ref[t]
            decay_pieces[offset] = power * rate
            drate = drate + power * decay_ref[0, pl.ds(t, 1), :]
        ddrive_ref[0, pl.ds(start, ROWS), :] = fold_states(drive_pieces, position)
        ddecay_ref[0, pl.ds(start, ROWS), :] = fold_states(decay_pieces, position)
        return later, drate

    zero = jnp.zeros_like(rate)
    drate_ref[0] = lax.fori_loop(0, length // ROWS, block, (zero, zero))[1]

def tile_width(width):
    for tiles in (3, 2, 1):
        if width % (tiles * LANES) == 0:
            return tiles * LANES
    return width

def scan_specs(length, states, width):
    tokens = pl.BlockSpec((1, length, width), lambda s, c: (s, 0, c))
    maps = pl.BlockSpec((1, length, states, LANES), lambda s, c: (s, 0, 0, 0))
    rates = pl.BlockSpec((states, width), lambda s, c: (0, c))
    return tokens, maps, rates

def run_forward(decay, drive, b_wide, c_wide, rate):
    count, length, channels = decay.shape
    states = rate.shape[0]
    width = tile_width(channels)
    tokens, maps, rates = scan_specs(length, states, width)
    return pl.pallas_call(
        scan_forward,
        grid=(count, channels // width),
        in_specs=[tokens, tokens, maps, maps, rates],
        out_specs=tokens,
        out_shape=jax.ShapeDtypeStruct(decay.shape, jnp.float32),
        cost_estimate=pl.CostEstimate(
            flops=8 * decay.size * states, transcendentals=decay.size * states,
            bytes_accessed=4 * (3 * decay.size + 2 * b_wide.size)),
        name="scan_forward",
    )(decay, drive, b_wide, c_wide, rate)

def run_backward(decay, drive, b_wide, c_wide, rate, dout):
    count, length, channels = decay.shape
    states = rate.shape[0]
    width = tile_width(channels)
    tokens, maps, rates = scan_specs(length, states, width)
    full = jax.ShapeDtypeStruct(decay.shape, jnp.float32)
    return pl.pallas_call(
        scan_backward,
        grid=(count, channels // width),
        in_specs=[tokens, tokens, maps, maps, rates, tokens],
        out_specs=[tokens, tokens, pl.BlockSpec((1, states, width), lambda s, c: (s, 0, c)), maps, maps],
        out_shape=[full, full, jax.ShapeDtypeStruct((count, states, channels), jnp.float32),
            jax.ShapeDtypeStruct(b_wide.shape, jnp.float32), jax.ShapeDtypeStruct(b_wide.shape, jnp.float32)],
        scratch_shapes=[pltpu.VMEM((length + 1, states, width), jnp.float32), pltpu.VMEM((length, states, width), jnp.float32)],
        cost_estimate=pl.CostEstimate(
            flops=30 * decay.size * states, transcendentals=decay.size * states,
            bytes_accessed=4 * (5 * decay.size + 4 * b_wide.size)),
        compiler_params=pltpu.CompilerParams(vmem_limit_bytes=32 << 20),
        name="scan_backward",
    )(decay, drive, b_wide, c_wide, rate, dout)

HIGHEST = lax.Precision.HIGHEST
EPSILON = 1e-05
LOG2E = 1.4426950408889634
FAR = 1e30
LOW = jnp.bfloat16
BOTH = ("dp", "expert")


def dot(left, right, contract):
    return lax.dot_general(left, right, (contract, ((), ())), preferred_element_type=jnp.float32)


def rms_scale(values, gain_row):
    return (
        values * lax.rsqrt(jnp.mean(values * values, axis=-1, keepdims=True) + EPSILON) * gain_row
    )


def gelu_tanh(values):
    return jax.nn.gelu(values, approximate=True)


def norm_route(residual, gain_two, router_full, chosen_rows):
    normed_two = rms_scale(residual, gain_two)
    logits = jnp.dot(normed_two, router_full, precision=HIGHEST, preferred_element_type=jnp.float32)
    probabilities = jax.nn.softmax(logits, axis=-1)
    return (normed_two, jnp.sum(probabilities * chosen_rows, axis=1))


def later_rows(values, offset):
    if offset == 0:
        return values
    return jnp.pad(values, ((0, 0), (offset, 0), (0, 0)))[:, : values.shape[1]]


def earlier_rows(values, offset):
    if offset == 0:
        return values
    return jnp.pad(values, ((0, 0), (0, offset), (0, 0)))[:, offset:]


def same_document(segments, offset):
    if offset == 0:
        return jnp.ones(segments.shape, jnp.float32)
    padded = jnp.pad(segments, ((0, 0), (offset, 0)), constant_values=-1)
    return (padded[:, : segments.shape[1]] == segments).astype(jnp.float32)


def conv_sum(inner, taps, bias_row, masks):
    count = taps.shape[0]
    total = bias_row
    for offset in range(count):
        total = total + taps[count - 1 - offset] * later_rows(inner, offset) * masks[offset]
    return total


def dispatch_matrix(route_rows, expert_count, capacity, padded_capacity):
    length = route_rows.shape[1]
    chosen = (
        route_rows[:, :, None] == jnp.arange(expert_count, dtype=jnp.int32)[None, None]
    ).astype(jnp.float32)
    before = jnp.tril(jnp.ones((length, length), jnp.float32), -1)
    earlier = jnp.einsum("tu,sue->ste", before, chosen, preferred_element_type=jnp.float32)
    slot = jnp.sum(earlier * chosen, axis=2).astype(jnp.int32)
    places = jnp.arange(padded_capacity, dtype=jnp.int32)
    taken = ((slot[:, :, None] == places) & (places < capacity)).astype(jnp.float32)
    return (chosen[:, :, :, None] * taken[:, :, None, :]).reshape(
        route_rows.shape[0], length, expert_count * padded_capacity
    )


def own_part(weight, axis_name):
    rows = weight.shape[0] // lax.axis_size(axis_name)
    return lax.dynamic_slice_in_dim(weight, lax.axis_index(axis_name) * rows, rows, axis=0)


def on_device(
    layer_input,
    segments,
    routes,
    cotangent,
    norm1_gain,
    in_weight,
    conv_weight,
    conv_bias,
    xproj_weight,
    dtproj_weight,
    dt_bias,
    a_log,
    skip_gain,
    out_weight,
    norm2_gain,
    router_weight,
    up_weight,
    down_weight,
):
    seq_len, model_width = layer_input.shape[2:]
    sequences = layer_input.shape[0] * layer_input.shape[1]
    tokens = sequences * seq_len
    expert_devices = lax.axis_size("expert")
    dp_devices = lax.axis_size("dp")
    local_experts = up_weight.shape[0]
    assert local_experts == 1
    expert_count = expert_devices
    capacity = seq_len * 5 // (4 * expert_count)
    padded_capacity = -(-capacity // 16) * 16
    slots = sequences * padded_capacity
    taps = conv_weight.shape[0]
    rank = dtproj_weight.shape[0]
    states = a_log.shape[0]
    pair = [(i, i ^ 1) for i in range(dp_devices)]
    ring = [(i, (i + 2) % dp_devices) for i in range(dp_devices)]
    steps = dp_devices // 2

    with jax.named_scope("fetch_in"):
        in_full = lax.all_gather(own_part(in_weight, "expert"), BOTH, axis=0, tiled=True)
    with jax.named_scope("fetch_small"):
        small = jnp.concatenate(
            [
                xproj_weight,
                dtproj_weight.T,
                a_log.T,
                conv_weight.T,
                conv_bias[:, None],
                dt_bias[:, None],
                skip_gain[:, None],
            ],
            axis=1,
        )
        small_full = lax.all_gather(small, BOTH, axis=0, tiled=True)
    with jax.named_scope("fetch_out"):
        out_full = lax.all_gather(own_part(out_weight, "expert"), BOTH, axis=0, tiled=True)
    with jax.named_scope("fetch_expert"):
        ups = [up_weight[0]]
        downs = [down_weight[0]]
        for _ in range(steps - 1):
            ups.append(lax.ppermute(ups[-1], "dp", ring))
            downs.append(lax.ppermute(downs[-1], "dp", ring))

    xproj_width = rank + 2 * states
    xproj_full = small_full[:, :xproj_width]
    across = small_full[:, xproj_width:].T
    dtproj_full = across[:rank]
    across = across[rank:].astype(jnp.float32)
    log_rates = across[:states]
    conv_full = across[states : states + taps]
    convb_full = across[states + taps]
    dtb_full = across[states + taps + 1]
    skip_full = across[states + taps + 2]
    inner_width = out_full.shape[0]
    gain_one = norm1_gain.astype(jnp.float32)
    gain_two = norm2_gain.astype(jnp.float32)
    router_full = router_weight.astype(jnp.float32)

    def split(values):
        return values.reshape(sequences, seq_len, values.shape[-1])

    def flat(values):
        return values.reshape(tokens, values.shape[-1])

    rows_in = layer_input.reshape(tokens, model_width).astype(jnp.float32)
    cot_rows = cotangent.reshape(tokens, model_width).astype(jnp.float32)
    segment_rows = segments.reshape(sequences, seq_len)
    route_rows = routes.reshape(sequences, seq_len)
    masks = [same_document(segment_rows, offset)[:, :, None] for offset in range(taps)]
    normed_one, norm_pull = jax.vjp(rms_scale, rows_in, gain_one)
    normed_low = normed_one.astype(LOW)
    joined = dot(normed_low, in_full, ((1,), (1,)))
    inner = split(joined[:, :inner_width])
    gate_in = split(joined[:, inner_width:])
    conv_out, silu_pull = jax.vjp(jax.nn.silu, conv_sum(inner, conv_full, convb_full, masks))
    conv_low = flat(conv_out).astype(LOW)
    projected = dot(conv_low, xproj_full, ((1,), (0,)))
    dt_low = projected[:, :rank].astype(LOW)
    b_wide = jnp.broadcast_to(
        split(projected[:, rank : rank + states])[..., None], (sequences, seq_len, states, LANES)
    )
    c_wide = jnp.broadcast_to(
        split(projected[:, rank + states :])[..., None], (sequences, seq_len, states, LANES)
    )
    dt_sum = split(dot(dt_low, dtproj_full, ((1,), (0,)))) + dtb_full
    delta = jax.nn.softplus(dt_sum)
    decay = jnp.where(masks[1] > 0, delta, FAR)
    drive = delta * conv_out
    rate = -jnp.exp(log_rates)
    rate_two = rate * LOG2E
    scanned = run_forward(decay, drive, b_wide, c_wide, rate_two)
    mixed = scanned + skip_full * conv_out
    gate_silu, gate_pull = jax.vjp(jax.nn.silu, gate_in)
    mixed_low = flat(mixed * gate_silu).astype(LOW)
    residual = rows_in + dot(mixed_low, out_full, ((1,), (0,)))

    chosen_rows = (
        route_rows.reshape(tokens, 1) == jnp.arange(expert_count, dtype=jnp.int32)[None]
    ).astype(jnp.float32)

    def route_piece(resid_value, gain_value, router_value):
        return norm_route(resid_value, gain_value, router_value, chosen_rows)

    (normed_two, gate_row), route_pull = jax.vjp(route_piece, residual, gain_two, router_full)
    placed = dispatch_matrix(route_rows, expert_count, capacity, padded_capacity).astype(LOW)
    sending = jnp.concatenate(
        [normed_two.astype(LOW), (cot_rows * gate_row[:, None]).astype(LOW)], axis=1
    )
    packed = jnp.einsum(
        "stk,std->skd", placed, split(sending), preferred_element_type=jnp.float32
    ).astype(LOW)
    packed = packed.reshape(sequences, expert_count, padded_capacity, 2 * model_width)
    packed = packed.transpose(1, 0, 2, 3).reshape(expert_count, slots, 2 * model_width)
    received = lax.all_to_all(packed, "expert", split_axis=0, concat_axis=0, tiled=True)
    received = received.reshape(expert_count * slots, 2 * model_width)
    own_count = received.shape[0]
    with jax.named_scope("pair_rows"):
        partner = lax.ppermute(received, "dp", pair)
    rows_all = jnp.concatenate([received, partner], axis=0)
    slot_rows = rows_all[:, :model_width]
    d_returned = rows_all[:, model_width:]

    returned = 0.0
    d_slots = 0.0
    up_terms = []
    down_terms = []
    for up, down in zip(ups, downs):
        hidden = dot(slot_rows, up, ((1,), (1,)))
        active, gelu_pull = jax.vjp(gelu_tanh, hidden)
        active_low = active.astype(LOW)
        returned = returned + dot(active_low, down, ((1,), (0,)))
        d_active = dot(d_returned, down, ((1,), (1,)))
        d_hidden_low = gelu_pull(d_active)[0].astype(LOW)
        d_slots = d_slots + dot(d_hidden_low, up, ((1,), (0,)))
        down_terms.append(dot(active_low, d_returned, ((0,), (0,))))
        up_terms.append(dot(d_hidden_low, slot_rows, ((0,), (0,))))
    results = jnp.concatenate([returned, d_slots], axis=1)
    with jax.named_scope("pair_results"):
        from_partner = lax.ppermute(results[own_count:].astype(LOW), "dp", pair)
    results = (results[:own_count] + from_partner.astype(jnp.float32)).astype(LOW)
    arrived = lax.all_to_all(
        results.reshape(expert_count, slots, 2 * model_width),
        "expert",
        split_axis=0,
        concat_axis=0,
        tiled=True,
    )
    arrived = arrived.reshape(expert_count, sequences, padded_capacity, 2 * model_width)
    arrived = arrived.transpose(1, 0, 2, 3).reshape(
        sequences, expert_count * padded_capacity, 2 * model_width
    )
    gathered_both = flat(
        jnp.einsum("stk,skd->std", placed, arrived, preferred_element_type=jnp.float32)
    )
    gathered = gathered_both[:, :model_width]
    d_sent = gathered_both[:, model_width:]
    layer_output = (residual + gate_row[:, None] * gathered).astype(LOW)

    with jax.named_scope("reduce_expert"):

        def ring_sum(terms):
            travelling = terms[1 % steps]
            for step in range(2, steps + 1):
                moved = lax.ppermute(travelling.astype(LOW), "dp", ring)
                travelling = terms[step % steps] + moved.astype(jnp.float32)
            return travelling

        up_grad = ring_sum(up_terms)
        down_grad = ring_sum(down_terms)

    d_gate = jnp.sum(cot_rows * gathered, axis=1)
    d_resid_norm, d_gain_two, d_router = route_pull((d_sent, d_gate))
    d_residual = cot_rows + d_resid_norm
    d_branch_low = d_residual.astype(LOW)

    out_term = dot(mixed_low, d_branch_low, ((0,), (0,))).astype(LOW)
    with jax.named_scope("reduce_out"):
        out_part = lax.psum_scatter(out_term, BOTH, scatter_dimension=0, tiled=True)
    d_mixed = split(dot(d_branch_low, out_full, ((1,), (1,))))
    d_gate_in = gate_pull(d_mixed * mixed)[0]
    d_scanned = d_mixed * gate_silu
    d_drive, d_decay, d_rate, d_b, d_c = run_backward(
        decay, drive, b_wide, c_wide, rate_two, d_scanned
    )
    d_skip = jnp.sum(d_scanned * conv_out, axis=(0, 1))
    d_alog = jnp.sum(d_rate, axis=0) * rate
    d_delta = d_decay * (1.0 / LOG2E) + d_drive * conv_out
    d_dt = d_delta * jax.nn.sigmoid(dt_sum)
    d_dtb = jnp.sum(d_dt, axis=(0, 1))
    d_dt_low = flat(d_dt).astype(LOW)
    dtproj_term = dot(d_dt_low, dt_low, ((0,), (0,)))
    d_dt_rows = dot(d_dt_low, dtproj_full, ((1,), (1,)))
    d_proj_low = jnp.concatenate(
        [
            d_dt_rows,
            jnp.sum(d_b, axis=3).reshape(tokens, states),
            jnp.sum(d_c, axis=3).reshape(tokens, states),
        ],
        axis=1,
    ).astype(LOW)
    xproj_term = dot(conv_low, d_proj_low, ((0,), (0,)))
    d_conv = (
        d_drive * delta
        + d_scanned * skip_full
        + split(dot(d_proj_low, xproj_full, ((1,), (1,))))
    )
    d_sum = silu_pull(d_conv)[0]
    d_convb = jnp.sum(d_sum, axis=(0, 1))
    d_inner = jnp.zeros_like(d_sum)
    tap_rows = [None] * taps
    for offset in range(taps):
        masked = d_sum * masks[offset]
        tap_rows[taps - 1 - offset] = jnp.sum(masked * later_rows(inner, offset), axis=(0, 1))
        d_inner = d_inner + conv_full[taps - 1 - offset] * earlier_rows(masked, offset)
    d_joined_low = jnp.concatenate([flat(d_inner), flat(d_gate_in)], axis=1).astype(LOW)
    in_term = dot(d_joined_low, normed_low, ((0,), (0,))).astype(LOW)
    with jax.named_scope("reduce_in"):
        in_part = lax.psum_scatter(in_term, BOTH, scatter_dimension=0, tiled=True)
    d_normed = dot(d_joined_low, in_full, ((1,), (0,)))
    d_rows_norm, d_gain_one = norm_pull(d_normed)
    input_grad = d_residual + d_rows_norm

    with jax.named_scope("reduce_small"):
        small_term = jnp.concatenate(
            [xproj_term, dtproj_term, d_alog.T]
            + [row[:, None] for row in tap_rows]
            + [d_convb[:, None], d_dtb[:, None], d_skip[:, None]],
            axis=1,
        ).astype(LOW)
        devices = dp_devices * expert_devices
        pieces = lax.all_to_all(
            small_term.reshape(devices, inner_width // devices, -1),
            BOTH,
            split_axis=0,
            concat_axis=0,
            tiled=True,
        )
        small_grad = jnp.sum(pieces.astype(jnp.float32), axis=0)
    xproj_grad = small_grad[:, :xproj_width]
    small_across = small_grad[:, xproj_width:].T
    dtproj_grad = small_across[:rank]
    alog_grad = small_across[rank : rank + states]
    conv_grad = small_across[rank + states : rank + states + taps]
    convb_grad, dtb_grad, skip_grad = small_across[rank + states + taps :]
    with jax.named_scope("reduce_gains"):
        gains = lax.psum(
            jnp.concatenate([d_gain_one[None], d_gain_two[None], d_router.T], axis=0), BOTH
        )
    with jax.named_scope("share_rows"):
        out_grad = lax.all_gather(out_part, "expert", axis=0, tiled=True).astype(jnp.float32)
        in_grad = lax.all_gather(in_part, "expert", axis=0, tiled=True).astype(jnp.float32)

    return (
        layer_output.reshape(layer_input.shape),
        input_grad.reshape(layer_input.shape),
        gains[0],
        in_grad,
        conv_grad,
        convb_grad,
        xproj_grad,
        dtproj_grad,
        dtb_grad,
        alog_grad,
        skip_grad,
        out_grad,
        gains[1],
        gains[2:].T,
        up_grad[None],
        down_grad[None],
    )


def solution(mesh):
    placed = (
        P(None, ("dp", "expert"), None, None),
        P(None, ("dp", "expert"), None),
        P(None, ("dp", "expert"), None, None),
        P(None, ("dp", "expert"), None, None),
        P(),
        P("dp", None),
        P(None, ("dp", "expert")),
        P(("dp", "expert")),
        P(("dp", "expert"), None),
        P(None, ("dp", "expert")),
        P(("dp", "expert")),
        P(None, ("dp", "expert")),
        P(("dp", "expert")),
        P("dp", None),
        P(),
        P(),
        P("expert", "dp", None),
        P("expert", "dp", None),
    )
    return jax.shard_map(
        on_device,
        mesh=mesh,
        in_specs=placed,
        out_specs=(
            P(None, ("dp", "expert"), None, None),
            P(None, ("dp", "expert"), None, None),
            P(),
            P("dp", None),
            P(None, ("dp", "expert")),
            P(("dp", "expert")),
            P(("dp", "expert"), None),
            P(None, ("dp", "expert")),
            P(("dp", "expert")),
            P(None, ("dp", "expert")),
            P(("dp", "expert")),
            P("dp", None),
            P(),
            P(),
            P("expert", "dp", None),
            P("expert", "dp", None),
        ),
        check_vma=False,
    )
```

```python
import jax
import jax.numpy as jnp
from jax import lax
from jax.experimental import pallas as pl
from jax.experimental.pallas import tpu as pltpu
from jax.sharding import PartitionSpec as P

LANES = 128
VMEM_GRANT = 60 << 20
ROWS = 8

def wide(tile, width):
    return jnp.concatenate([tile] * (width // LANES), axis=1)

def narrow(values):
    total = values[:, :LANES]
    for start in range(LANES, values.shape[1], LANES):
        total = total + values[:, start : start + LANES]
    return total

def fold_states(pieces, position):
    folded = []
    for piece in pieces:
        total = piece[:ROWS]
        for start in range(ROWS, piece.shape[0], ROWS):
            total = total + piece[start : start + ROWS]
        folded.append(total)
    low = (position & 4) == 0
    folded = [
        jnp.where(low, a, b) + pltpu.roll(jnp.where(low, b, a), 4, 0)
        for a, b in zip(folded[:4], folded[4:])
    ]
    for step in (2, 1):
        low = (position & step) == 0
        half = len(folded) // 2
        folded = [
            jnp.where(low, a + pltpu.roll(a, ROWS - step, 0), b + pltpu.roll(b, step, 0))
            for a, b in zip(folded[:half], folded[half:])
        ]
    return folded[0]

def scan_forward(decay_ref, drive_ref, b_ref, c_ref, rate_ref, out_ref):
    length, width = decay_ref.shape[1:]
    rate = rate_ref[...]
    position = lax.broadcasted_iota(jnp.int32, (ROWS, width), 0)

    def block(index, state):
        start = pl.multiple_of(index * ROWS, ROWS)
        pieces = []
        for offset in range(ROWS):
            t = start + offset
            factor = jnp.exp2(decay_ref[0, pl.ds(t, 1), :] * rate)
            state = factor * state + drive_ref[0, pl.ds(t, 1), :] * wide(b_ref[0, t], width)
            pieces.append(state * wide(c_ref[0, t], width))
        out_ref[0, pl.ds(start, ROWS), :] = fold_states(pieces, position)
        return state

    lax.fori_loop(0, length // ROWS, block, jnp.zeros_like(rate))

def scan_backward(
    decay_ref, drive_ref, b_ref, c_ref, rate_ref, dout_ref,
    ddrive_ref, ddecay_ref, drate_ref, db_sum_ref, dc_sum_ref,
    db_ref, dc_ref, state_ref, factor_ref,
):
    length, width = decay_ref.shape[1:]
    rate = rate_ref[...]
    position = lax.broadcasted_iota(jnp.int32, (ROWS, width), 0)

    @pl.when(pl.program_id(1) == 0)
    def _():
        db_ref[...] = jnp.zeros_like(db_ref)
        dc_ref[...] = jnp.zeros_like(dc_ref)

    state_ref[0] = jnp.zeros_like(rate)

    def replay(index, state):
        start = pl.multiple_of(index * ROWS, ROWS)
        for offset in range(ROWS):
            t = start + offset
            factor = jnp.exp2(decay_ref[0, pl.ds(t, 1), :] * rate)
            state = factor * state + drive_ref[0, pl.ds(t, 1), :] * wide(b_ref[0, t], width)
            factor_ref[t] = factor
            state_ref[t + 1] = state
        return state

    lax.fori_loop(0, length // ROWS, replay, jnp.zeros_like(rate))

    def block(index, carried):
        later, drate = carried
        start = pl.multiple_of(length - ROWS - index * ROWS, ROWS)
        drive_pieces = [None] * ROWS
        decay_pieces = [None] * ROWS
        for offset in reversed(range(ROWS)):
            t = start + offset
            dout = dout_ref[0, pl.ds(t, 1), :]
            dstate = later + dout * wide(c_ref[0, t], width)
            dc_ref[t] += narrow(dout * state_ref[t + 1])
            db_ref[t] += narrow(dstate * drive_ref[0, pl.ds(t, 1), :])
            drive_pieces[offset] = dstate * wide(b_ref[0, t], width)
            later = dstate * factor_ref[t]
            power = later * state_ref[t]
            decay_pieces[offset] = power * rate
            drate = drate + power * decay_ref[0, pl.ds(t, 1), :]
        ddrive_ref[0, pl.ds(start, ROWS), :] = fold_states(drive_pieces, position)
        ddecay_ref[0, pl.ds(start, ROWS), :] = fold_states(decay_pieces, position)
        return later, drate

    zero = jnp.zeros_like(rate)
    drate_ref[0] = lax.fori_loop(0, length // ROWS, block, (zero, zero))[1]

    @pl.when(pl.program_id(1) == pl.num_programs(1) - 1)
    def _():
        ones = jnp.ones((ROWS, LANES), jnp.float32)
        for total_ref, sum_ref in ((db_ref, db_sum_ref), (dc_ref, dc_sum_ref)):
            sum_ref[0] = lax.dot_general(
                ones,
                total_ref[...].reshape(-1, LANES),
                (((1,), (1,)), ((), ())),
                precision=lax.Precision.HIGHEST,
                preferred_element_type=jnp.float32,
            )

def tile_width(width):
    for tiles in (3, 2, 1):
        if width % (tiles * LANES) == 0:
            return tiles * LANES
    return width

def scan_specs(length, states, width):
    tokens = pl.BlockSpec((1, length, width), lambda s, c: (s, 0, c))
    maps = pl.BlockSpec((1, length, states, LANES), lambda s, c: (s, 0, 0, 0))
    rates = pl.BlockSpec((states, width), lambda s, c: (0, c))
    return tokens, maps, rates

def run_forward(decay, drive, b_wide, c_wide, rate):
    count, length, channels = decay.shape
    states = rate.shape[0]
    width = tile_width(channels)
    tokens, maps, rates = scan_specs(length, states, width)
    return pl.pallas_call(
        scan_forward,
        grid=(count, channels // width),
        in_specs=[tokens, tokens, maps, maps, rates],
        out_specs=tokens,
        out_shape=jax.ShapeDtypeStruct(decay.shape, jnp.float32),
        cost_estimate=pl.CostEstimate(
            flops=decay.size, transcendentals=0,
            bytes_accessed=4 * (3 * decay.size + 2 * b_wide.size)),
        compiler_params=pltpu.CompilerParams(vmem_limit_bytes=VMEM_GRANT),
        name="scan_forward",
    )(decay, drive, b_wide, c_wide, rate)

def run_backward(decay, drive, b_wide, c_wide, rate, dout):
    count, length, channels = decay.shape
    states = rate.shape[0]
    width = tile_width(channels)
    tokens, maps, rates = scan_specs(length, states, width)
    full = jax.ShapeDtypeStruct(decay.shape, jnp.float32)
    summed = jax.ShapeDtypeStruct((count, ROWS, length * states), jnp.float32)
    sums = pl.BlockSpec((1, ROWS, length * states), lambda s, c: (s, 0, 0))
    return pl.pallas_call(
        scan_backward,
        grid=(count, channels // width),
        in_specs=[tokens, tokens, maps, maps, rates, tokens],
        out_specs=[tokens, tokens, pl.BlockSpec((1, states, width), lambda s, c: (s, 0, c)), sums, sums],
        out_shape=[full, full, jax.ShapeDtypeStruct((count, states, channels), jnp.float32),
            summed, summed],
        scratch_shapes=[pltpu.VMEM((length, states, LANES), jnp.float32), pltpu.VMEM((length, states, LANES), jnp.float32),
            pltpu.VMEM((length + 1, states, width), jnp.float32), pltpu.VMEM((length, states, width), jnp.float32)],
        cost_estimate=pl.CostEstimate(
            flops=decay.size, transcendentals=0,
            bytes_accessed=4 * (5 * decay.size + 4 * b_wide.size)),
        compiler_params=pltpu.CompilerParams(vmem_limit_bytes=VMEM_GRANT),
        name="scan_backward",
    )(decay, drive, b_wide, c_wide, rate, dout)


def product(left, right, contract):
    return lax.dot_general(left, right, (contract, ((), ())), preferred_element_type=jnp.float32)


def gate_backward(
    d_branch_ref, normed_ref, out_ref, mixed_low_ref, mixed_ref, gate_ref,
    term_ref, d_gate_ref, d_scanned_ref,
):
    model = d_branch_ref.shape[1]
    d_branch = d_branch_ref[...]
    d_mixed = product(d_branch, out_ref[...], ((1,), (1,)))
    gate = gate_ref[...]
    chance = jax.nn.sigmoid(gate)
    d_gate = d_mixed * mixed_ref[...] * (chance * (1.0 + gate * (1.0 - chance)))
    d_gate = d_gate.astype(jnp.bfloat16)
    d_gate_ref[...] = d_gate
    d_scanned_ref[...] = d_mixed * gate * chance
    term_ref[:, :model] = product(mixed_low_ref[...], d_branch, ((0,), (0,))).astype(jnp.bfloat16)
    term_ref[:, model:] = product(d_gate, normed_ref[...], ((0,), (0,))).astype(jnp.bfloat16)


def run_gate_backward(d_branch, normed, out_rows, mixed_low, mixed, gate):
    count, model = d_branch.shape
    channels = mixed.shape[1]
    width = tile_width(channels)
    whole = pl.BlockSpec((count, model), lambda c: (0, 0))
    rows = pl.BlockSpec((width, model), lambda c: (c, 0))
    tokens = pl.BlockSpec((count, width), lambda c: (0, c))
    return pl.pallas_call(
        gate_backward,
        grid=(channels // width,),
        in_specs=[whole, whole, rows, tokens, tokens, tokens],
        out_specs=[pl.BlockSpec((width, 2 * model), lambda c: (c, 0)), tokens, tokens],
        out_shape=[
            jax.ShapeDtypeStruct((channels, 2 * model), jnp.bfloat16),
            jax.ShapeDtypeStruct((count, channels), jnp.bfloat16),
            jax.ShapeDtypeStruct((count, channels), jnp.float32),
        ],
        cost_estimate=pl.CostEstimate(flops=count, transcendentals=0, bytes_accessed=count),
        compiler_params=pltpu.CompilerParams(vmem_limit_bytes=VMEM_GRANT),
        name="gate_backward",
    )(d_branch, normed, out_rows, mixed_low, mixed, gate)


def conv_backward(
    d_drive_ref, delta_ref, d_scanned_ref, inner_ref, d_gate_ref, d_proj_ref, normed_ref,
    masks_ref, conv_ref, xproj_ref, in_ref, d_dt_ref, dt_ref, rows_ref,
    term_ref, d_normed_ref, small_ref,
):
    taps = masks_ref.shape[1]
    model = normed_ref.shape[1]
    count = inner_ref.shape[0]
    d_conv = (
        d_drive_ref[...] * delta_ref[...]
        + d_scanned_ref[...] * conv_ref[taps + 1 : taps + 2]
        + product(d_proj_ref[...], xproj_ref[...], ((1,), (1,)))
    )
    inner = inner_ref[...]
    shifted = [inner] + [pltpu.roll(inner, offset, 0) for offset in range(1, taps)]
    masked = [shifted[offset] * masks_ref[:, offset : offset + 1] for offset in range(taps)]
    total = conv_ref[taps : taps + 1]
    for offset in range(taps):
        total = total + conv_ref[taps - 1 - offset : taps - offset] * masked[offset]
    chance = jax.nn.sigmoid(total)
    d_sum = d_conv * (chance * (1.0 + total * (1.0 - chance)))
    d_inner = jnp.zeros_like(inner)
    rows = []
    for offset in range(taps):
        rows.append(jnp.sum(d_sum * masked[offset], axis=0, keepdims=True))
        back = d_sum * masks_ref[:, offset : offset + 1]
        if offset:
            back = pltpu.roll(back, count - offset, 0)
        d_inner = d_inner + conv_ref[taps - 1 - offset : taps - offset] * back
    rows = rows[::-1] + [jnp.sum(d_sum, axis=0, keepdims=True)]
    rows = jnp.concatenate(
        rows + [jnp.zeros_like(rows[0])] * (ROWS - len(rows)) + [rows_ref[...]], axis=0
    ).astype(jnp.bfloat16)
    extent = rows.shape[0]
    same = lax.broadcasted_iota(jnp.int32, (extent, extent), 0) == lax.broadcasted_iota(
        jnp.int32, (extent, extent), 1
    )
    columns = product(rows, same.astype(jnp.bfloat16), ((0,), (0,)))
    conv_low = (total * chance).astype(jnp.bfloat16)
    edge = d_proj_ref.shape[1]
    middle = edge + dt_ref.shape[1]
    small_ref[:, :edge] = product(conv_low, d_proj_ref[...], ((0,), (0,))).astype(jnp.bfloat16)
    small_ref[:, edge:middle] = product(d_dt_ref[...], dt_ref[...], ((0,), (0,))).astype(
        jnp.bfloat16
    )
    small_ref[:, middle:] = columns.astype(jnp.bfloat16)
    d_inner = d_inner.astype(jnp.bfloat16)
    term_ref[...] = product(d_inner, normed_ref[...], ((0,), (0,))).astype(jnp.bfloat16)
    d_normed = product(d_inner, in_ref[:, :model], ((1,), (0,))) + product(
        d_gate_ref[...], in_ref[:, model:], ((1,), (0,))
    )

    @pl.when(pl.program_id(0) == 0)
    def _():
        d_normed_ref[...] = d_normed

    @pl.when(pl.program_id(0) > 0)
    def _():
        d_normed_ref[...] += d_normed


def run_conv_backward(
    d_drive,
    delta,
    d_scanned,
    inner,
    d_gate,
    d_proj,
    normed,
    masks,
    conv_rows,
    xproj,
    in_rows,
    d_dt,
    dt,
    more_rows,
):
    count, channels = inner.shape
    model = normed.shape[1]
    width = tile_width(channels)
    tokens = pl.BlockSpec((count, width), lambda c: (0, c))
    small_width = d_proj.shape[1] + dt.shape[1] + ROWS + more_rows.shape[0]

    def whole(values):
        return pl.BlockSpec(values.shape, lambda c: (0, 0))

    def rows(values):
        return pl.BlockSpec((width, values.shape[1]), lambda c: (c, 0))

    return pl.pallas_call(
        conv_backward,
        grid=(channels // width,),
        in_specs=[
            tokens,
            tokens,
            tokens,
            tokens,
            tokens,
            whole(d_proj),
            whole(normed),
            whole(masks),
            pl.BlockSpec((ROWS, width), lambda c: (0, c)),
            rows(xproj),
            rows(in_rows),
            tokens,
            whole(dt),
            pl.BlockSpec((more_rows.shape[0], width), lambda c: (0, c)),
        ],
        out_specs=[
            pl.BlockSpec((width, model), lambda c: (c, 0)),
            pl.BlockSpec((count, model), lambda c: (0, 0)),
            pl.BlockSpec((width, small_width), lambda c: (c, 0)),
        ],
        out_shape=[
            jax.ShapeDtypeStruct((channels, model), jnp.bfloat16),
            jax.ShapeDtypeStruct((count, model), jnp.float32),
            jax.ShapeDtypeStruct((channels, small_width), jnp.bfloat16),
        ],
        cost_estimate=pl.CostEstimate(flops=count, transcendentals=0, bytes_accessed=count),
        compiler_params=pltpu.CompilerParams(vmem_limit_bytes=VMEM_GRANT),
        name="conv_backward",
    )(
        d_drive,
        delta,
        d_scanned,
        inner,
        d_gate,
        d_proj,
        normed,
        masks,
        conv_rows,
        xproj,
        in_rows,
        d_dt,
        dt,
        more_rows,
    )


HIGHEST = lax.Precision.HIGHEST
EPSILON = 1e-05
LOG2E = 1.4426950408889634
FAR = 1e30
LOW = jnp.bfloat16
BOTH = ("dp", "expert")


def dot(left, right, contract):
    return lax.dot_general(left, right, (contract, ((), ())), preferred_element_type=jnp.float32)


def rms_scale(values, gain_row):
    return (
        values * lax.rsqrt(jnp.mean(values * values, axis=-1, keepdims=True) + EPSILON) * gain_row
    )


def gelu_tanh(values):
    return jax.nn.gelu(values, approximate=True)


def norm_route(residual, gain_two, router_full, chosen_rows):
    normed_two = rms_scale(residual, gain_two)
    logits = jnp.dot(normed_two, router_full, precision=HIGHEST, preferred_element_type=jnp.float32)
    probabilities = jax.nn.softmax(logits, axis=-1)
    return (normed_two, jnp.sum(probabilities * chosen_rows, axis=1))


def later_rows(values, offset):
    if offset == 0:
        return values
    return jnp.pad(values, ((0, 0), (offset, 0), (0, 0)))[:, : values.shape[1]]


def same_document(segments, offset):
    if offset == 0:
        return jnp.ones(segments.shape, jnp.float32)
    padded = jnp.pad(segments, ((0, 0), (offset, 0)), constant_values=-1)
    return (padded[:, : segments.shape[1]] == segments).astype(jnp.float32)


def conv_sum(inner, taps, bias_row, masks):
    count = taps.shape[0]
    total = bias_row
    for offset in range(count):
        total = total + taps[count - 1 - offset] * later_rows(inner, offset) * masks[offset]
    return total


def dispatch_matrices(order_rows, expert_count, capacity, padded_capacity):
    length = order_rows.shape[1]
    chosen = (
        order_rows[:, :, None] == jnp.arange(expert_count, dtype=jnp.int32)[None, None]
    ).astype(jnp.float32)
    before = jnp.tril(jnp.ones((length, length), jnp.float32), -1)
    earlier = jnp.einsum("tu,sue->ste", before, chosen, preferred_element_type=jnp.float32)
    slot = jnp.sum(earlier * chosen, axis=2).astype(jnp.int32)
    places = jnp.arange(padded_capacity, dtype=jnp.int32)
    taken = ((slot[:, :, None] == places) & (places < capacity)).astype(jnp.float32)
    return [(chosen[:, :, k, None] * taken).astype(LOW) for k in range(expert_count)]


def hop(values, step):
    axis_name, distance = step
    size = lax.axis_size(axis_name)
    return lax.ppermute(values, axis_name, [(i, i ^ distance) for i in range(size)])


class Ring:
    def __init__(self, axis_name, stride, size):
        self.axis_name = axis_name
        self.stride = stride
        self.size = size
        self.place = lax.axis_index(axis_name) // stride % size

    def hop(self, values, distance=1):
        pairs = []
        for i in range(lax.axis_size(self.axis_name)):
            place = i // self.stride % self.size
            pairs.append((i, i + ((place + distance) % self.size - place) * self.stride))
        return lax.ppermute(values, self.axis_name, pairs)


def mesh_rings():
    dp_size, expert_size = lax.axis_size("dp"), lax.axis_size("expert")
    return [
        Ring("dp", 2, dp_size // 2),
        Ring("dp", 1, 2),
        Ring("expert", 2, expert_size // 2),
        Ring("expert", 1, 2),
    ]


def cubes():
    expert_size = lax.axis_size("expert")
    wide = 2 * expert_size
    return [
        [place * wide + i for i in range(wide)] for place in range(lax.axis_size("dp") // 2)
    ]


def far_gather(block):
    ring = mesh_rings()[0]
    blocks = [block[None]]
    for _ in range(ring.size - 1):
        blocks.append((yield ring.hop(blocks[-1])))
    line = jnp.concatenate(blocks[::-1] + blocks[:0:-1], axis=0)
    return lax.dynamic_slice_in_dim(line, ring.size - 1 - ring.place, ring.size, axis=0)


def cube_gather(block):
    return lax.all_gather(block, BOTH, axis=0, tiled=True, axis_index_groups=cubes())


def cube_scatter(total):
    return lax.psum_scatter(
        total, BOTH, scatter_dimension=0, tiled=True, axis_index_groups=cubes()
    )


def block_of(values, place, axis):
    return lax.dynamic_index_in_dim(values, place, axis, keepdims=True)


def far_and_pair(block):
    pair = mesh_rings()[1]
    blocks = yield from far_gather(block)
    blocks = blocks.reshape((-1, 2) + block.shape)
    moved = yield pair.hop(block_of(blocks, 1 - pair.place, 1))
    kept = block_of(blocks, pair.place, 1)
    return jnp.where(
        pair.place == 0,
        jnp.concatenate([kept, moved], axis=1),
        jnp.concatenate([moved, kept], axis=1),
    )


def far_and_pair_sum(blocks):
    pair = mesh_rings()[1]
    moved = yield pair.hop(block_of(blocks, 1 - pair.place, 1))
    kept = block_of(blocks, pair.place, 1)
    values = jnp.where(
        pair.place == 0,
        jnp.concatenate([kept, moved], axis=1),
        jnp.concatenate([moved, kept], axis=1),
    )
    values = values.reshape((-1,) + blocks.shape[2:])
    return (yield from far_sum(values))


def cube_stages_gather(block):
    for ring in mesh_rings()[:0:-1]:
        blocks = [block[None]]
        for _ in range(ring.size - 1):
            blocks.append((yield ring.hop(blocks[-1])))
        line = jnp.concatenate(blocks[::-1] + blocks[:0:-1], axis=0)
        block = lax.dynamic_slice_in_dim(line, ring.size - 1 - ring.place, ring.size, axis=0)
        block = block.reshape((-1,) + block.shape[2:])
    return block


def small_gather(block):
    cube = yield from cube_stages_gather(block)
    places = yield from far_gather(cube)
    width = block.shape[1]
    places = places.reshape(-1, 2, 2, lax.axis_size("expert"), block.shape[0], width)
    return places.transpose(1, 3, 0, 2, 4, 5).reshape(-1, width)


def add_low(kept, moved):
    return (kept.astype(jnp.float32) + moved.astype(jnp.float32)).astype(LOW)


def far_sum(blocks):
    ring = mesh_rings()[0]
    moved = yield tuple(
        ring.hop(block_of(blocks, (ring.place + distance) % ring.size, 0)[0], distance)
        for distance in range(1, ring.size)
    )
    total = block_of(blocks, ring.place, 0)[0].astype(jnp.float32)
    for part in moved:
        total = total + part.astype(jnp.float32)
    return total.astype(LOW)


def ring_sum(blocks):
    ring = mesh_rings()[0]
    count = len(blocks)
    travelling = blocks[1 % count]
    for step in range(2, count + 1):
        moved = yield ring.hop(travelling.astype(LOW))
        travelling = blocks[step % count].astype(jnp.float32) + moved.astype(jnp.float32)
    return travelling


def butterfly(values):
    for axis_name in ("expert", "dp"):
        distance = 1
        while distance < lax.axis_size(axis_name):
            values = values + (yield hop(values, (axis_name, distance)))
            distance *= 2
    return values


def shared_rows(values):
    rings = mesh_rings()
    gathered = values
    for ring in rings[2:]:
        blocks = [gathered[None]]
        for _ in range(ring.size - 1):
            blocks.append((yield ring.hop(blocks[-1])))
        line = jnp.concatenate(blocks[::-1] + blocks[:0:-1], axis=0)
        gathered = lax.dynamic_slice_in_dim(line, ring.size - 1 - ring.place, ring.size, axis=0)
    parts, rows, width = values.shape
    return gathered.transpose(2, 1, 0, 3, 4).reshape(parts, -1, width)


class Streams:
    def __init__(self):
        self.under_way = {}
        self.done = {}
        self.started = set()
        self.blocks = []

    def _take(self, name, stages, value):
        try:
            self.under_way[name] = (stages, stages.send(value))
        except StopIteration as end:
            self.under_way.pop(name, None)
            self.done[name] = end.value

    def start(self, name, stages):
        self.started.add(name)
        self._take(name, stages, None)

    def advance(self, names, *anchors):
        names = [name for name in names if name in self.under_way]
        values = [self.under_way[name][1] for name in names]
        values, anchors = lax.optimization_barrier((values, anchors))
        for name, value in zip(names, values):
            self._take(name, self.under_way[name][0], value)
        return anchors[0] if len(anchors) == 1 else anchors

    def finish(self, names):
        while any(name in self.under_way for name in names):
            self.advance(names)


def part_rows(weight, start, rows):
    return lax.dynamic_slice_in_dim(weight, start, rows, axis=0)


def on_device(
    layer_input,
    segments,
    routes,
    cotangent,
    norm1_gain,
    in_weight,
    conv_weight,
    conv_bias,
    xproj_weight,
    dtproj_weight,
    dt_bias,
    a_log,
    skip_gain,
    out_weight,
    norm2_gain,
    router_weight,
    up_weight,
    down_weight,
):
    seq_len, model_width = layer_input.shape[2:]
    sequences = layer_input.shape[0] * layer_input.shape[1]
    tokens = sequences * seq_len
    expert_devices = lax.axis_size("expert")
    dp_devices = lax.axis_size("dp")
    devices = dp_devices * expert_devices
    assert up_weight.shape[0] == 1
    expert_count = expert_devices
    capacity = seq_len * 5 // (4 * expert_count)
    padded_capacity = -(-capacity // 16) * 16
    slots = sequences * padded_capacity
    taps = conv_weight.shape[0]
    rank = dtproj_weight.shape[0]
    states = a_log.shape[0]
    channels = skip_gain.shape[0]
    inner_width = channels * devices
    steps = dp_devices // 2
    expert_index = lax.axis_index("expert")
    small = jnp.concatenate(
        [
            xproj_weight,
            dtproj_weight.T,
            a_log.T,
            conv_weight.T,
            conv_bias[:, None],
            dt_bias[:, None],
            skip_gain[:, None],
        ],
        axis=1,
    )
    streams = Streams()

    def ring_blocks(block):
        ring = mesh_rings()[0]
        blocks = streams.blocks
        blocks.append(block)
        for _ in range(steps - 1):
            blocks.append((yield ring.hop(blocks[-1])))
        return blocks

    in_block = lax.dynamic_index_in_dim(
        in_weight.reshape(2, expert_devices, channels, model_width), expert_index, 1, keepdims=False
    ).reshape(2 * channels, model_width)
    streams.start("in", far_gather(in_block))
    streams.start("small", small_gather(small))
    for _ in range(steps - 1):
        streams.advance(("in", "small"))
    in_blocks = streams.done["in"].reshape(2, -1, model_width)
    with jax.named_scope("fetch_in"):
        in_cube = cube_gather(jnp.concatenate([in_blocks[0], in_blocks[1]], axis=1))
    out_block = part_rows(out_weight, expert_index * channels, channels)
    out_block = lax.optimization_barrier((out_block, in_blocks))[0]
    streams.start("out", far_and_pair(out_block))
    for _ in range(steps - 2):
        streams.advance(("out", "small"))
    expert_block = jnp.concatenate([up_weight[0], down_weight[0]], axis=0)
    expert_block = streams.advance(("out", "small"), expert_block)
    streams.start("expert", ring_blocks(expert_block))
    streams.finish(("out", "small"))
    with jax.named_scope("fetch_out"):
        out_full = cube_gather(streams.done["out"].reshape(-1, model_width))
    small_full = streams.done["small"]
    xproj_width = rank + 2 * states
    xproj_full = small_full[:, :xproj_width]
    across = small_full[:, xproj_width:].T
    dtproj_full = across[:rank]
    across = across[rank:].astype(jnp.float32)
    log_rates = across[:states]
    conv_full = across[states : states + taps]
    convb_full = across[states + taps]
    dtb_full = across[states + taps + 1]
    skip_full = across[states + taps + 2]
    conv_rows = jnp.concatenate(
        [
            conv_full,
            convb_full[None],
            skip_full[None],
            jnp.zeros((ROWS - taps - 2, inner_width), jnp.float32),
        ],
        axis=0,
    )
    segment_rows = segments.reshape(sequences, seq_len)
    masks = [same_document(segment_rows, offset)[:, :, None] for offset in range(taps)]
    mask_columns = jnp.concatenate([mask.reshape(tokens, 1) for mask in masks], axis=1)
    rate = -jnp.exp(log_rates)
    rate_two = rate * LOG2E
    route_rows = routes.reshape(sequences, seq_len)
    placed = dispatch_matrices(
        route_rows ^ expert_index.astype(jnp.int32), expert_count, capacity, padded_capacity
    )
    in_cube, conv_rows, mask_columns, xproj_full, dtproj_full, rate_two, placed, dtb_full = (
        streams.advance(
            ("expert",),
            in_cube,
            conv_rows,
            mask_columns,
            xproj_full,
            dtproj_full,
            rate_two,
            placed,
            dtb_full,
        )
    )
    inner_full = in_cube[:, :model_width]
    gate_full = in_cube[:, model_width:]
    gain_one = norm1_gain.astype(jnp.float32)
    gain_two = norm2_gain.astype(jnp.float32)
    router_full = router_weight.astype(jnp.float32)

    def split(values):
        return values.reshape(sequences, seq_len, values.shape[-1])

    def flat(values):
        return values.reshape(tokens, values.shape[-1])

    rows_in = layer_input.reshape(tokens, model_width).astype(jnp.float32)
    cot_rows = cotangent.reshape(tokens, model_width).astype(jnp.float32)
    normed_one, norm_pull = jax.vjp(rms_scale, rows_in, gain_one)
    normed_low = normed_one.astype(LOW)
    inner = split(dot(normed_low, inner_full, ((1,), (1,))))
    gate_in = split(dot(normed_low, gate_full, ((1,), (1,))))
    conv_out = jax.nn.silu(conv_sum(inner, conv_full, convb_full, masks))
    conv_low = flat(conv_out).astype(LOW)
    projected = dot(conv_low, xproj_full, ((1,), (0,)))
    dt_low = projected[:, :rank].astype(LOW)
    b_wide = jnp.broadcast_to(
        split(projected[:, rank : rank + states])[..., None], (sequences, seq_len, states, LANES)
    )
    c_wide = jnp.broadcast_to(
        split(projected[:, rank + states :])[..., None], (sequences, seq_len, states, LANES)
    )
    dt_sum = split(dot(dt_low, dtproj_full, ((1,), (0,)))) + dtb_full
    delta = jax.nn.softplus(dt_sum)
    decay = jnp.where(masks[1] > 0, delta, FAR)
    drive = delta * conv_out
    scanned = run_forward(decay, drive, b_wide, c_wide, rate_two)
    scanned = streams.advance(("expert",), scanned)
    mixed = scanned + skip_full * conv_out
    gate_silu = jax.nn.silu(gate_in)
    mixed_low = flat(mixed * gate_silu).astype(LOW)
    residual = rows_in + dot(mixed_low, out_full, ((1,), (0,)))

    chosen_rows = (
        route_rows.reshape(tokens, 1) == jnp.arange(expert_count, dtype=jnp.int32)[None]
    ).astype(jnp.float32)

    def route_piece(resid_value, gain_value, router_value):
        return norm_route(resid_value, gain_value, router_value, chosen_rows)

    (normed_two, gate_row), route_pull = jax.vjp(route_piece, residual, gain_two, router_full)
    sending = split(
        jnp.concatenate(
            [normed_two.astype(LOW), (cot_rows * gate_row[:, None]).astype(LOW)], axis=1
        )
    )

    def partners(cross, k):
        place = lambda d, e: d * expert_devices + e
        return [
            (place(d, e), place(d ^ cross, e ^ k))
            for d in range(dp_devices)
            for e in range(expert_devices)
        ]

    def exchange(piece, cross, k):
        if not cross and not k:
            return piece
        return lax.ppermute(piece, BOTH, partners(cross, k))

    pieces = [
        jnp.einsum("stk,std->skd", matrix, sending, preferred_element_type=jnp.float32).astype(LOW)
        for matrix in placed
    ]
    with jax.named_scope("send_rows"):
        received = [
            [exchange(pieces[k], cross, k).reshape(slots, -1) for k in range(expert_count)]
            for cross in (0, 1)
        ]

    units = up_weight.shape[1]
    up_terms = [0.0] * steps
    down_terms = [0.0] * steps
    kept = []
    sums = [[0.0, 0.0], [0.0, 0.0]]

    def expert_block(cross, k, rows, block):
        up, down = block[:units], block[units:]
        slot_rows, d_returned = rows[:, :model_width], rows[:, model_width:]
        hidden = dot(slot_rows, up, ((1,), (1,)))
        active, gelu_pull = jax.vjp(gelu_tanh, hidden)
        active_low = active.astype(LOW)
        d_active = dot(d_returned, down, ((1,), (1,)))
        d_hidden_low = gelu_pull(d_active)[0].astype(LOW)
        sums[cross][0] = sums[cross][0] + dot(active_low, down, ((1,), (0,)))
        sums[cross][1] = sums[cross][1] + dot(d_hidden_low, up, ((1,), (0,)))
        kept.append((k, active_low, d_hidden_low, slot_rows, d_returned))

    while len(streams.blocks) < steps - 1:
        streams.advance(("expert",))
    groups = [jnp.concatenate(received[0], axis=0), None]
    early = list(enumerate(streams.blocks[: steps - 1]))
    for k, block in early:
        expert_block(0, k, groups[0], block)
    sums[0], cross_pieces = lax.optimization_barrier((sums[0], received[1]))
    groups[1] = jnp.concatenate(cross_pieces, axis=0)
    for k, block in early:
        expert_block(1, k, groups[1], block)
    sums = list(streams.advance(("expert",), *sums))
    last = steps - 1
    for cross in (1, 0):
        expert_block(cross, last, groups[cross], streams.done["expert"][last])
    results = [
        jnp.concatenate([returned.astype(LOW), d_slots.astype(LOW)], axis=1).reshape(
            expert_count, sequences, padded_capacity, 2 * model_width
        )
        for returned, d_slots in sums
    ]
    with jax.named_scope("send_results"):
        arrived = [
            [exchange(results[cross][k], cross, k) for k in range(expert_count)]
            for cross in (0, 1)
        ]
    for k, active_low, d_hidden_low, slot_rows, d_returned in kept:
        down_terms[k] = down_terms[k] + dot(active_low, d_returned, ((0,), (0,)))
        up_terms[k] = up_terms[k] + dot(d_hidden_low, slot_rows, ((0,), (0,)))
    terms = [
        jnp.concatenate([up.astype(LOW), down.astype(LOW)], axis=0)
        for up, down in zip(up_terms, down_terms)
    ]
    terms, arrived = lax.optimization_barrier((terms, arrived))
    streams.start("expert_grad", ring_sum(terms))
    gathered_both = 0.0
    for k in range(expert_count):
        total = (arrived[0][k].astype(jnp.float32) + arrived[1][k].astype(jnp.float32)).astype(LOW)
        gathered_both = gathered_both + jnp.einsum(
            "stk,skd->std", placed[k], total, preferred_element_type=jnp.float32
        )
    gathered_both = flat(gathered_both)
    gathered = gathered_both[:, :model_width]
    d_sent = gathered_both[:, model_width:]
    layer_output = (residual + gate_row[:, None] * gathered).astype(LOW)


    d_gate = jnp.sum(cot_rows * gathered, axis=1)
    d_resid_norm, d_gain_two, d_router = route_pull((d_sent, d_gate))
    d_residual = cot_rows + d_resid_norm
    d_branch_low = d_residual.astype(LOW)

    out_gate_term, d_gate_low, d_scanned = run_gate_backward(
        d_branch_low, normed_low, out_full, mixed_low, flat(mixed), flat(gate_in)
    )
    with jax.named_scope("reduce_out_gate"):
        out_gate_blocks = cube_scatter(out_gate_term)
    d_scanned = split(d_scanned)
    d_drive, d_decay, d_rate, d_b, d_c = run_backward(
        decay, drive, b_wide, c_wide, rate_two, d_scanned
    )
    d_drive = streams.advance(("expert_grad",), d_drive)
    d_skip = jnp.sum(d_scanned * conv_out, axis=(0, 1))
    d_alog = jnp.sum(d_rate, axis=0) * rate
    d_delta = d_decay * (1.0 / LOG2E) + d_drive * conv_out
    d_dt = d_delta * jax.nn.sigmoid(dt_sum)
    d_dtb = jnp.sum(d_dt, axis=(0, 1))
    d_dt_low = flat(d_dt).astype(LOW)
    d_dt_rows = dot(d_dt_low, dtproj_full, ((1,), (1,)))
    d_proj_low = jnp.concatenate(
        [
            d_dt_rows,
            d_b[:, 0].reshape(tokens, states),
            d_c[:, 0].reshape(tokens, states),
        ],
        axis=1,
    ).astype(LOW)
    more_rows = jnp.concatenate([d_alog, d_dtb[None], d_skip[None]], axis=0)
    more_rows = jnp.pad(more_rows, ((0, -more_rows.shape[0] % ROWS), (0, 0)))
    inner_term, d_normed, small_term = run_conv_backward(
        flat(d_drive),
        flat(delta),
        flat(d_scanned),
        flat(inner),
        d_gate_low,
        d_proj_low,
        normed_low,
        mask_columns,
        conv_rows,
        xproj_full,
        in_cube,
        d_dt_low,
        dt_low,
        more_rows,
    )
    inner_term, d_normed, small_term = streams.advance(
        ("expert_grad",), inner_term, d_normed, small_term
    )
    with jax.named_scope("reduce_inner"):
        inner_blocks = cube_scatter(inner_term)
    with jax.named_scope("reduce_small"):
        small_width = small_term.shape[1]
        pieces = small_term.reshape(2, expert_devices, steps // 2, 2, channels, small_width)
        pieces = lax.all_to_all(
            pieces.transpose(2, 0, 3, 1, 4, 5).reshape(devices, channels, small_width),
            BOTH,
            split_axis=0,
            concat_axis=0,
            tiled=True,
        )
    out_blocks = out_gate_blocks[:, :model_width]
    gate_blocks = out_gate_blocks[:, model_width:]
    streams.start(
        "out_grad", far_and_pair_sum(out_blocks.reshape(-1, 2, channels, model_width))
    )
    d_rows_norm, d_gain_one = norm_pull(d_normed)
    input_grad = d_residual + d_rows_norm

    gains = jnp.concatenate([d_gain_one[None], d_gain_two[None], d_router.T], axis=0)
    streams.start("gains", butterfly(gains))
    streams.advance(("out_grad", "gains"))
    streams.advance(("gains", "expert_grad"))
    streams.finish(("out_grad",))
    streams.start("out_rows", shared_rows(streams.done["out_grad"][None]))
    streams.finish(("gains", "out_rows", "expert_grad"))
    in_places = jnp.concatenate([inner_blocks, gate_blocks], axis=0)
    streams.start("in_grad", far_sum(in_places.reshape(steps, 2, channels, model_width)))
    pieces = streams.advance(("in_grad",), pieces)
    streams.start("in_rows", shared_rows(streams.done["in_grad"]))
    streams.finish(("in_rows",))
    in_grad = streams.done["in_rows"].reshape(in_weight.shape).astype(jnp.float32)
    out_grad = streams.done["out_rows"][0].astype(jnp.float32)
    expert_grad = streams.done["expert_grad"].astype(jnp.float32)
    up_grad, down_grad = expert_grad[:units], expert_grad[units:]
    gains = streams.done["gains"]
    small_grad = jnp.sum(pieces.astype(jnp.float32), axis=0)
    xproj_grad = small_grad[:, :xproj_width]
    row_grads = small_grad[:, xproj_width:].T
    dtproj_grad = row_grads[:rank]
    row_grads = row_grads[rank:]
    conv_grad = row_grads[:taps]
    convb_grad = row_grads[taps]
    alog_grad = row_grads[ROWS : ROWS + states]
    dtb_grad, skip_grad = row_grads[ROWS + states], row_grads[ROWS + states + 1]

    return (
        layer_output.reshape(layer_input.shape),
        input_grad.reshape(layer_input.shape),
        gains[0],
        in_grad,
        conv_grad,
        convb_grad,
        xproj_grad,
        dtproj_grad,
        dtb_grad,
        alog_grad,
        skip_grad,
        out_grad,
        gains[1],
        gains[2:].T,
        up_grad[None],
        down_grad[None],
    )


def solution(mesh):
    placed = (
        P(None, ("dp", "expert"), None, None),
        P(None, ("dp", "expert"), None),
        P(None, ("dp", "expert"), None, None),
        P(None, ("dp", "expert"), None, None),
        P(),
        P("dp", None),
        P(None, ("dp", "expert")),
        P(("dp", "expert")),
        P(("dp", "expert"), None),
        P(None, ("dp", "expert")),
        P(("dp", "expert")),
        P(None, ("dp", "expert")),
        P(("dp", "expert")),
        P("dp", None),
        P(),
        P(),
        P("expert", "dp", None),
        P("expert", "dp", None),
    )
    return jax.shard_map(
        on_device,
        mesh=mesh,
        in_specs=placed,
        out_specs=(
            P(None, ("dp", "expert"), None, None),
            P(None, ("dp", "expert"), None, None),
            P(),
            P("dp", None),
            P(None, ("dp", "expert")),
            P(("dp", "expert")),
            P(("dp", "expert"), None),
            P(None, ("dp", "expert")),
            P(("dp", "expert")),
            P(None, ("dp", "expert")),
            P(("dp", "expert")),
            P("dp", None),
            P(),
            P(),
            P("expert", "dp", None),
            P("expert", "dp", None),
        ),
        check_vma=False,
    )
```

```python
import functools

import jax
import jax.numpy as jnp
from jax import lax
from jax.experimental import pallas as pl
from jax.experimental.pallas import tpu as pltpu
from jax.sharding import PartitionSpec as P

LANES = 128
VMEM_GRANT = 40 << 20
ROWS = 8

def wide(tile, width):
    return jnp.concatenate([tile] * (width // LANES), axis=1)

def narrow(values):
    total = values[:, :LANES]
    for start in range(LANES, values.shape[1], LANES):
        total = total + values[:, start : start + LANES]
    return total

def fold_states(pieces, position):
    folded = []
    for piece in pieces:
        total = piece[:ROWS]
        for start in range(ROWS, piece.shape[0], ROWS):
            total = total + piece[start : start + ROWS]
        folded.append(total)
    low = (position & 4) == 0
    folded = [
        jnp.where(low, a, b) + pltpu.roll(jnp.where(low, b, a), 4, 0)
        for a, b in zip(folded[:4], folded[4:])
    ]
    for step in (2, 1):
        low = (position & step) == 0
        half = len(folded) // 2
        folded = [
            jnp.where(low, a + pltpu.roll(a, ROWS - step, 0), b + pltpu.roll(b, step, 0))
            for a, b in zip(folded[:half], folded[half:])
        ]
    return folded[0]

def scan_forward(decay_ref, drive_ref, b_ref, c_ref, rate_ref, out_ref):
    length, width = decay_ref.shape[1:]
    rate = rate_ref[...]
    position = lax.broadcasted_iota(jnp.int32, (ROWS, width), 0)

    def block(index, state):
        start = pl.multiple_of(index * ROWS, ROWS)
        pieces = []
        for offset in range(ROWS):
            t = start + offset
            factor = jnp.exp2(decay_ref[0, pl.ds(t, 1), :] * rate)
            state = factor * state + drive_ref[0, pl.ds(t, 1), :] * wide(b_ref[0, t], width)
            pieces.append(state * wide(c_ref[0, t], width))
        out_ref[0, pl.ds(start, ROWS), :] = fold_states(pieces, position)
        return state

    lax.fori_loop(0, length // ROWS, block, jnp.zeros_like(rate))

def scan_backward(
    decay_ref, drive_ref, b_ref, c_ref, rate_ref, dout_ref,
    ddrive_ref, ddecay_ref, drate_ref, db_sum_ref, dc_sum_ref,
    db_ref, dc_ref, state_ref, factor_ref,
):
    length, width = decay_ref.shape[1:]
    rate = rate_ref[...]
    position = lax.broadcasted_iota(jnp.int32, (ROWS, width), 0)

    @pl.when(pl.program_id(1) == 0)
    def _():
        db_ref[...] = jnp.zeros_like(db_ref)
        dc_ref[...] = jnp.zeros_like(dc_ref)

    state_ref[0] = jnp.zeros_like(rate)

    def replay(index, state):
        start = pl.multiple_of(index * ROWS, ROWS)
        for offset in range(ROWS):
            t = start + offset
            factor = jnp.exp2(decay_ref[0, pl.ds(t, 1), :] * rate)
            state = factor * state + drive_ref[0, pl.ds(t, 1), :] * wide(b_ref[0, t], width)
            factor_ref[t] = factor
            state_ref[t + 1] = state
        return state

    lax.fori_loop(0, length // ROWS, replay, jnp.zeros_like(rate))

    def block(index, carried):
        later, drate = carried
        start = pl.multiple_of(length - ROWS - index * ROWS, ROWS)
        drive_pieces = [None] * ROWS
        decay_pieces = [None] * ROWS
        for offset in reversed(range(ROWS)):
            t = start + offset
            dout = dout_ref[0, pl.ds(t, 1), :]
            dstate = later + dout * wide(c_ref[0, t], width)
            dc_ref[t] += narrow(dout * state_ref[t + 1])
            db_ref[t] += narrow(dstate * drive_ref[0, pl.ds(t, 1), :])
            drive_pieces[offset] = dstate * wide(b_ref[0, t], width)
            later = dstate * factor_ref[t]
            power = later * state_ref[t]
            decay_pieces[offset] = power * rate
            drate = drate + power * decay_ref[0, pl.ds(t, 1), :]
        ddrive_ref[0, pl.ds(start, ROWS), :] = fold_states(drive_pieces, position)
        ddecay_ref[0, pl.ds(start, ROWS), :] = fold_states(decay_pieces, position)
        return later, drate

    zero = jnp.zeros_like(rate)
    drate_ref[0] = lax.fori_loop(0, length // ROWS, block, (zero, zero))[1]

    @pl.when(pl.program_id(1) == pl.num_programs(1) - 1)
    def _():
        ones = jnp.ones((ROWS, LANES), jnp.float32)
        for total_ref, sum_ref in ((db_ref, db_sum_ref), (dc_ref, dc_sum_ref)):
            sum_ref[0] = lax.dot_general(
                ones,
                total_ref[...].reshape(-1, LANES),
                (((1,), (1,)), ((), ())),
                precision=lax.Precision.HIGHEST,
                preferred_element_type=jnp.float32,
            )

def tile_width(width):
    for tiles in (3, 2, 1):
        if width % (tiles * LANES) == 0:
            return tiles * LANES
    return width

def scan_specs(length, states, width):
    tokens = pl.BlockSpec((1, length, width), lambda s, c: (s, 0, c))
    maps = pl.BlockSpec((1, length, states, LANES), lambda s, c: (s, 0, 0, 0))
    rates = pl.BlockSpec((states, width), lambda s, c: (0, c))
    return tokens, maps, rates

def run_forward(decay, drive, b_wide, c_wide, rate):
    count, length, channels = decay.shape
    states = rate.shape[0]
    width = tile_width(channels)
    tokens, maps, rates = scan_specs(length, states, width)
    return pl.pallas_call(
        scan_forward,
        grid=(count, channels // width),
        in_specs=[tokens, tokens, maps, maps, rates],
        out_specs=tokens,
        out_shape=jax.ShapeDtypeStruct(decay.shape, jnp.float32),
        cost_estimate=pl.CostEstimate(
            flops=decay.size, transcendentals=0,
            bytes_accessed=4 * (3 * decay.size + 2 * b_wide.size)),
        compiler_params=pltpu.CompilerParams(vmem_limit_bytes=VMEM_GRANT),
        name="scan_forward",
    )(decay, drive, b_wide, c_wide, rate)

def run_backward(decay, drive, b_wide, c_wide, rate, dout):
    count, length, channels = decay.shape
    states = rate.shape[0]
    width = tile_width(channels)
    tokens, maps, rates = scan_specs(length, states, width)
    full = jax.ShapeDtypeStruct(decay.shape, jnp.float32)
    summed = jax.ShapeDtypeStruct((count, ROWS, length * states), jnp.float32)
    sums = pl.BlockSpec((1, ROWS, length * states), lambda s, c: (s, 0, 0))
    return pl.pallas_call(
        scan_backward,
        grid=(count, channels // width),
        in_specs=[tokens, tokens, maps, maps, rates, tokens],
        out_specs=[tokens, tokens, pl.BlockSpec((1, states, width), lambda s, c: (s, 0, c)), sums, sums],
        out_shape=[full, full, jax.ShapeDtypeStruct((count, states, channels), jnp.float32),
            summed, summed],
        scratch_shapes=[pltpu.VMEM((length, states, LANES), jnp.float32), pltpu.VMEM((length, states, LANES), jnp.float32),
            pltpu.VMEM((length + 1, states, width), jnp.float32), pltpu.VMEM((length, states, width), jnp.float32)],
        cost_estimate=pl.CostEstimate(
            flops=decay.size, transcendentals=0,
            bytes_accessed=4 * (5 * decay.size + 4 * b_wide.size)),
        compiler_params=pltpu.CompilerParams(vmem_limit_bytes=VMEM_GRANT),
        name="scan_backward",
    )(decay, drive, b_wide, c_wide, rate, dout)


def product(left, right, contract):
    return lax.dot_general(left, right, (contract, ((), ())), preferred_element_type=jnp.float32)


def gate_backward(
    d_branch_ref, normed_ref, out_ref, mixed_low_ref, mixed_ref, gate_ref,
    term_ref, d_gate_ref, d_scanned_ref,
):
    model = d_branch_ref.shape[1]
    d_branch = d_branch_ref[...]
    d_mixed = product(d_branch, out_ref[...], ((1,), (1,)))
    gate = gate_ref[...]
    chance = jax.nn.sigmoid(gate)
    d_gate = d_mixed * mixed_ref[...] * (chance * (1.0 + gate * (1.0 - chance)))
    d_gate = d_gate.astype(jnp.bfloat16)
    d_gate_ref[...] = d_gate
    d_scanned_ref[...] = d_mixed * gate * chance
    term_ref[:, :model] = product(mixed_low_ref[...], d_branch, ((0,), (0,))).astype(jnp.bfloat16)
    term_ref[:, model:] = product(d_gate, normed_ref[...], ((0,), (0,))).astype(jnp.bfloat16)


def run_gate_backward(d_branch, normed, out_rows, mixed_low, mixed, gate):
    count, model = d_branch.shape
    channels = mixed.shape[1]
    width = tile_width(channels)
    whole = pl.BlockSpec((count, model), lambda c: (0, 0))
    rows = pl.BlockSpec((width, model), lambda c: (c, 0))
    tokens = pl.BlockSpec((count, width), lambda c: (0, c))
    return pl.pallas_call(
        gate_backward,
        grid=(channels // width,),
        in_specs=[whole, whole, rows, tokens, tokens, tokens],
        out_specs=[pl.BlockSpec((width, 2 * model), lambda c: (c, 0)), tokens, tokens],
        out_shape=[
            jax.ShapeDtypeStruct((channels, 2 * model), jnp.bfloat16),
            jax.ShapeDtypeStruct((count, channels), jnp.bfloat16),
            jax.ShapeDtypeStruct((count, channels), jnp.float32),
        ],
        cost_estimate=pl.CostEstimate(flops=count, transcendentals=0, bytes_accessed=count),
        compiler_params=pltpu.CompilerParams(vmem_limit_bytes=VMEM_GRANT),
        name="gate_backward",
    )(d_branch, normed, out_rows, mixed_low, mixed, gate)


def conv_backward(
    d_drive_ref, delta_ref, d_scanned_ref, inner_ref, d_gate_ref, d_proj_ref, normed_ref,
    masks_ref, conv_ref, xproj_ref, in_ref, d_dt_ref, dt_ref, rows_ref,
    term_ref, d_normed_ref,
):
    taps = masks_ref.shape[1]
    model = normed_ref.shape[1]
    count = inner_ref.shape[0]
    d_conv = (
        d_drive_ref[...] * delta_ref[...]
        + d_scanned_ref[...] * conv_ref[taps + 1 : taps + 2]
        + product(d_proj_ref[...], xproj_ref[...], ((1,), (1,)))
    )
    inner = inner_ref[...]
    shifted = [inner] + [pltpu.roll(inner, offset, 0) for offset in range(1, taps)]
    masked = [shifted[offset] * masks_ref[:, offset : offset + 1] for offset in range(taps)]
    total = conv_ref[taps : taps + 1]
    for offset in range(taps):
        total = total + conv_ref[taps - 1 - offset : taps - offset] * masked[offset]
    chance = jax.nn.sigmoid(total)
    d_sum = d_conv * (chance * (1.0 + total * (1.0 - chance)))
    d_inner = jnp.zeros_like(inner)
    rows = []
    for offset in range(taps):
        rows.append(jnp.sum(d_sum * masked[offset], axis=0, keepdims=True))
        back = d_sum * masks_ref[:, offset : offset + 1]
        if offset:
            back = pltpu.roll(back, count - offset, 0)
        d_inner = d_inner + conv_ref[taps - 1 - offset : taps - offset] * back
    rows = rows[::-1] + [jnp.sum(d_sum, axis=0, keepdims=True)]
    rows = jnp.concatenate(
        rows + [jnp.zeros_like(rows[0])] * (ROWS - len(rows)) + [rows_ref[...]], axis=0
    ).astype(jnp.bfloat16)
    extent = rows.shape[0]
    same = lax.broadcasted_iota(jnp.int32, (extent, extent), 0) == lax.broadcasted_iota(
        jnp.int32, (extent, extent), 1
    )
    columns = product(rows, same.astype(jnp.bfloat16), ((0,), (0,)))
    conv_low = (total * chance).astype(jnp.bfloat16)
    edge = model + d_proj_ref.shape[1]
    middle = edge + dt_ref.shape[1]
    term_ref[:, model:edge] = product(conv_low, d_proj_ref[...], ((0,), (0,))).astype(jnp.bfloat16)
    term_ref[:, edge:middle] = product(d_dt_ref[...], dt_ref[...], ((0,), (0,))).astype(
        jnp.bfloat16
    )
    term_ref[:, middle:] = columns.astype(jnp.bfloat16)
    d_inner = d_inner.astype(jnp.bfloat16)
    term_ref[:, :model] = product(d_inner, normed_ref[...], ((0,), (0,))).astype(jnp.bfloat16)
    d_normed = product(d_inner, in_ref[:, :model], ((1,), (0,))) + product(
        d_gate_ref[...], in_ref[:, model:], ((1,), (0,))
    )

    @pl.when(pl.program_id(0) == 0)
    def _():
        d_normed_ref[...] = d_normed

    @pl.when(pl.program_id(0) > 0)
    def _():
        d_normed_ref[...] += d_normed


def run_conv_backward(
    d_drive,
    delta,
    d_scanned,
    inner,
    d_gate,
    d_proj,
    normed,
    masks,
    conv_rows,
    xproj,
    in_rows,
    d_dt,
    dt,
    more_rows,
):
    count, channels = inner.shape
    model = normed.shape[1]
    width = tile_width(channels)
    tokens = pl.BlockSpec((count, width), lambda c: (0, c))
    small_width = d_proj.shape[1] + dt.shape[1] + ROWS + more_rows.shape[0]

    def whole(values):
        return pl.BlockSpec(values.shape, lambda c: (0, 0))

    def rows(values):
        return pl.BlockSpec((width, values.shape[1]), lambda c: (c, 0))

    return pl.pallas_call(
        conv_backward,
        grid=(channels // width,),
        in_specs=[
            tokens,
            tokens,
            tokens,
            tokens,
            tokens,
            whole(d_proj),
            whole(normed),
            whole(masks),
            pl.BlockSpec((ROWS, width), lambda c: (0, c)),
            rows(xproj),
            rows(in_rows),
            tokens,
            whole(dt),
            pl.BlockSpec((more_rows.shape[0], width), lambda c: (0, c)),
        ],
        out_specs=[
            pl.BlockSpec((width, model + small_width), lambda c: (c, 0)),
            pl.BlockSpec((count, model), lambda c: (0, 0)),
        ],
        out_shape=[
            jax.ShapeDtypeStruct((channels, model + small_width), jnp.bfloat16),
            jax.ShapeDtypeStruct((count, model), jnp.float32),
        ],
        cost_estimate=pl.CostEstimate(flops=count, transcendentals=0, bytes_accessed=count),
        compiler_params=pltpu.CompilerParams(vmem_limit_bytes=VMEM_GRANT),
        name="conv_backward",
    )(
        d_drive,
        delta,
        d_scanned,
        inner,
        d_gate,
        d_proj,
        normed,
        masks,
        conv_rows,
        xproj,
        in_rows,
        d_dt,
        dt,
        more_rows,
    )


GELU_SCALE = 0.7978845608028654
GELU_CUBE = 0.044715


def expert_pass(pieces, blocks, *refs):
    piece_refs, block_refs = refs[:pieces], refs[pieces : pieces + blocks]
    refs = refs[pieces + blocks :]
    result_refs, (rows_ref, active_ref, d_hidden_ref) = refs[:pieces], refs[pieces : pieces + 3]
    total_ref, held_ref, sems = refs[pieces + 3 :]
    copies = [
        pltpu.make_async_copy(block_refs[k], held_ref.at[k], sems.at[k]) for k in range(blocks)
    ]
    for copy in copies:
        copy.start()
    length = piece_refs[0].shape[0]
    for n in range(pieces):
        rows_ref[n * length : (n + 1) * length, :] = piece_refs[n][...]
    model = rows_ref.shape[1] // 2
    units = held_ref.shape[1] // 2
    slot_rows, d_returned = rows_ref[:, :model], rows_ref[:, model:]
    for k in range(blocks):
        copies[k].wait()
        up, down = held_ref[k, :units, :], held_ref[k, units:, :]
        hidden = product(slot_rows, up, ((1,), (1,)))
        square = hidden * hidden
        bend = jnp.tanh(GELU_SCALE * (hidden + GELU_CUBE * (square * hidden)))
        share = 0.5 * (1.0 + bend)
        active = (hidden * share).astype(jnp.bfloat16)
        slope = share + hidden * (0.5 * GELU_SCALE) * (1.0 - bend * bend) * (
            1.0 + 3.0 * GELU_CUBE * square
        )
        d_active = product(d_returned, down, ((1,), (1,)))
        d_hidden = (d_active * slope).astype(jnp.bfloat16)
        active_ref[:, k * units : (k + 1) * units] = active
        d_hidden_ref[:, k * units : (k + 1) * units] = d_hidden
        returned = product(active, down, ((1,), (0,)))
        d_slots = product(d_hidden, up, ((1,), (0,)))
        if k:
            returned = returned + total_ref[:, :model]
            d_slots = d_slots + total_ref[:, model:]
        if k < blocks - 1:
            total_ref[:, :model] = returned
            total_ref[:, model:] = d_slots
        else:
            for n in range(pieces):
                part = slice(n * length, (n + 1) * length)
                result_refs[n][:, :model] = returned[part].astype(jnp.bfloat16)
                result_refs[n][:, model:] = d_slots[part].astype(jnp.bfloat16)


def run_expert(pieces, blocks):
    length, width = pieces[0].shape
    rows = length * len(pieces)
    units = blocks[0].shape[0] // 2
    low = jnp.bfloat16
    vmem = pl.BlockSpec(memory_space=pltpu.VMEM)
    out = pl.pallas_call(
        functools.partial(expert_pass, len(pieces), len(blocks)),
        in_specs=[vmem] * len(pieces) + [pl.BlockSpec(memory_space=pl.ANY)] * len(blocks),
        out_specs=[vmem] * (len(pieces) + 3),
        out_shape=[jax.ShapeDtypeStruct((length, width), low)] * len(pieces)
        + [
            jax.ShapeDtypeStruct((rows, width), low),
            jax.ShapeDtypeStruct((rows, units * len(blocks)), low),
            jax.ShapeDtypeStruct((rows, units * len(blocks)), low),
        ],
        scratch_shapes=[
            pltpu.VMEM((rows, width), jnp.float32),
            pltpu.VMEM((len(blocks),) + blocks[0].shape, low),
            pltpu.SemaphoreType.DMA((len(blocks),)),
        ],
        cost_estimate=pl.CostEstimate(flops=rows, transcendentals=0, bytes_accessed=rows),
        compiler_params=pltpu.CompilerParams(vmem_limit_bytes=VMEM_GRANT),
        name="expert_pass",
    )(*pieces, *blocks)
    return out[: len(pieces)], out[len(pieces) :]


HIGHEST = lax.Precision.HIGHEST
EPSILON = 1e-05
LOG2E = 1.4426950408889634
FAR = 1e30
LOW = jnp.bfloat16
BOTH = ("dp", "expert")


def dot(left, right, contract):
    return lax.dot_general(left, right, (contract, ((), ())), preferred_element_type=jnp.float32)


def rms_scale(values, gain_row):
    return (
        values * lax.rsqrt(jnp.mean(values * values, axis=-1, keepdims=True) + EPSILON) * gain_row
    )


def gelu_tanh(values):
    return jax.nn.gelu(values, approximate=True)


def norm_route(residual, gain_two, router_full, chosen_rows):
    normed_two = rms_scale(residual, gain_two)
    logits = jnp.dot(normed_two, router_full, precision=HIGHEST, preferred_element_type=jnp.float32)
    probabilities = jax.nn.softmax(logits, axis=-1)
    return (normed_two, jnp.sum(probabilities * chosen_rows, axis=1))


def later_rows(values, offset):
    if offset == 0:
        return values
    return jnp.pad(values, ((0, 0), (offset, 0), (0, 0)))[:, : values.shape[1]]


def same_document(segments, offset):
    if offset == 0:
        return jnp.ones(segments.shape, jnp.float32)
    padded = jnp.pad(segments, ((0, 0), (offset, 0)), constant_values=-1)
    return (padded[:, : segments.shape[1]] == segments).astype(jnp.float32)


def conv_sum(inner, taps, bias_row, masks):
    count = taps.shape[0]
    total = bias_row
    for offset in range(count):
        total = total + taps[count - 1 - offset] * later_rows(inner, offset) * masks[offset]
    return total


def dispatch_matrices(order_rows, expert_count, capacity, padded_capacity):
    length = order_rows.shape[1]
    chosen = (
        order_rows[:, :, None] == jnp.arange(expert_count, dtype=jnp.int32)[None, None]
    ).astype(jnp.float32)
    before = jnp.tril(jnp.ones((length, length), jnp.float32), -1)
    earlier = jnp.einsum("tu,sue->ste", before, chosen, preferred_element_type=jnp.float32)
    slot = jnp.sum(earlier * chosen, axis=2).astype(jnp.int32)
    places = jnp.arange(padded_capacity, dtype=jnp.int32)
    taken = ((slot[:, :, None] == places) & (places < capacity)).astype(jnp.float32)
    return [(chosen[:, :, k, None] * taken).astype(LOW) for k in range(expert_count)]


def hop(values, step):
    axis_name, distance = step
    size = lax.axis_size(axis_name)
    return lax.ppermute(values, axis_name, [(i, i ^ distance) for i in range(size)])


class Ring:
    def __init__(self, axis_name, stride, size):
        self.axis_name = axis_name
        self.stride = stride
        self.size = size
        self.place = lax.axis_index(axis_name) // stride % size

    def hop(self, values, distance=1):
        pairs = []
        for i in range(lax.axis_size(self.axis_name)):
            place = i // self.stride % self.size
            pairs.append((i, i + ((place + distance) % self.size - place) * self.stride))
        return lax.ppermute(values, self.axis_name, pairs)


def mesh_rings():
    dp_size, expert_size = lax.axis_size("dp"), lax.axis_size("expert")
    return [
        Ring("dp", 2, dp_size // 2),
        Ring("dp", 1, 2),
        Ring("expert", 2, expert_size // 2),
        Ring("expert", 1, 2),
    ]


def cubes():
    expert_size = lax.axis_size("expert")
    wide = 2 * expert_size
    return [
        [place * wide + i for i in range(wide)] for place in range(lax.axis_size("dp") // 2)
    ]


def far_gather(block):
    ring = mesh_rings()[0]
    blocks = [block[None]]
    for _ in range(ring.size - 1):
        blocks.append((yield ring.hop(blocks[-1])))
    line = jnp.concatenate(blocks[::-1] + blocks[:0:-1], axis=0)
    return lax.dynamic_slice_in_dim(line, ring.size - 1 - ring.place, ring.size, axis=0)


def cube_gather(block):
    return lax.all_gather(block, BOTH, axis=0, tiled=True, axis_index_groups=cubes())


def cube_scatter(total):
    return lax.psum_scatter(
        total, BOTH, scatter_dimension=0, tiled=True, axis_index_groups=cubes()
    )


def block_of(values, place, axis):
    return lax.dynamic_index_in_dim(values, place, axis, keepdims=True)


def far_and_pair(block):
    pair = mesh_rings()[1]
    blocks = yield from far_gather(block)
    blocks = blocks.reshape((-1, 2) + block.shape)
    moved = yield pair.hop(block_of(blocks, 1 - pair.place, 1))
    kept = block_of(blocks, pair.place, 1)
    return jnp.where(
        pair.place == 0,
        jnp.concatenate([kept, moved], axis=1),
        jnp.concatenate([moved, kept], axis=1),
    )


def far_and_pair_sum(blocks):
    pair = mesh_rings()[1]
    moved = yield pair.hop(block_of(blocks, 1 - pair.place, 1))
    kept = block_of(blocks, pair.place, 1)
    values = jnp.where(
        pair.place == 0,
        jnp.concatenate([kept, moved], axis=1),
        jnp.concatenate([moved, kept], axis=1),
    )
    values = values.reshape((-1,) + blocks.shape[2:])
    return (yield from far_sum(values))


def cube_stages_gather(block):
    for ring in mesh_rings()[:0:-1]:
        blocks = [block[None]]
        for _ in range(ring.size - 1):
            blocks.append((yield ring.hop(blocks[-1])))
        line = jnp.concatenate(blocks[::-1] + blocks[:0:-1], axis=0)
        block = lax.dynamic_slice_in_dim(line, ring.size - 1 - ring.place, ring.size, axis=0)
        block = block.reshape((-1,) + block.shape[2:])
    return block


def small_gather(block):
    block = yield from far_and_pair(block)
    return (yield from cube_stages_gather(block.reshape(-1, block.shape[-1])))


def add_low(kept, moved):
    return (kept.astype(jnp.float32) + moved.astype(jnp.float32)).astype(LOW)


def far_sum(blocks, more=None):
    ring = mesh_rings()[0]

    def block(distance):
        place = (ring.place + distance) % ring.size
        if more is None:
            return block_of(blocks, place, 0)[0]
        middle = ring.size // 2
        return jnp.where(
            place < middle,
            block_of(blocks, place % middle, 0)[0],
            block_of(more, place % middle, 0)[0],
        )

    moved = yield tuple(ring.hop(block(distance), distance) for distance in range(1, ring.size))
    total = block(0).astype(jnp.float32)
    for part in moved:
        total = total + part.astype(jnp.float32)
    return total.astype(LOW)


def ring_sum(blocks):
    ring = mesh_rings()[0]
    count = len(blocks)
    travelling = blocks[1 % count]
    for step in range(2, count + 1):
        travelling = yield travelling.astype(LOW)
        moved = yield ring.hop(travelling)
        travelling = blocks[step % count].astype(jnp.float32) + moved.astype(jnp.float32)
    return travelling


def butterfly(values, axis_name, first, last):
    distance = first
    while distance < last:
        values = values + (yield hop(values, (axis_name, distance)))
        distance *= 2
    return values


def near_sum(values):
    values = yield from butterfly(values, "expert", 1, lax.axis_size("expert"))
    return (yield from butterfly(values, "dp", 1, 2))


def shared_rows(values):
    rings = mesh_rings()
    gathered = values
    for ring in rings[2:]:
        blocks = [gathered[None]]
        for _ in range(ring.size - 1):
            blocks.append((yield ring.hop(blocks[-1])))
        line = jnp.concatenate(blocks[::-1] + blocks[:0:-1], axis=0)
        gathered = lax.dynamic_slice_in_dim(line, ring.size - 1 - ring.place, ring.size, axis=0)
    parts, rows, width = values.shape
    return gathered.transpose(2, 1, 0, 3, 4).reshape(parts, -1, width)


class Streams:
    def __init__(self):
        self.under_way = {}
        self.done = {}
        self.started = set()
        self.blocks = []

    def _take(self, name, stages, value):
        try:
            self.under_way[name] = (stages, stages.send(value))
        except StopIteration as end:
            self.under_way.pop(name, None)
            self.done[name] = end.value

    def start(self, name, stages):
        self.started.add(name)
        self._take(name, stages, None)

    def advance(self, names, *anchors):
        names = [name for name in names if name in self.under_way]
        values = [self.under_way[name][1] for name in names]
        values, anchors = lax.optimization_barrier((values, anchors))
        for name, value in zip(names, values):
            self._take(name, self.under_way[name][0], value)
        return anchors[0] if len(anchors) == 1 else anchors

    def finish(self, names):
        while any(name in self.under_way for name in names):
            self.advance(names)


def part_rows(weight, start, rows):
    return lax.dynamic_slice_in_dim(weight, start, rows, axis=0)


def on_device(
    layer_input,
    segments,
    routes,
    cotangent,
    norm1_gain,
    in_weight,
    conv_weight,
    conv_bias,
    xproj_weight,
    dtproj_weight,
    dt_bias,
    a_log,
    skip_gain,
    out_weight,
    norm2_gain,
    router_weight,
    up_weight,
    down_weight,
):
    seq_len, model_width = layer_input.shape[2:]
    sequences = layer_input.shape[0] * layer_input.shape[1]
    tokens = sequences * seq_len
    expert_devices = lax.axis_size("expert")
    dp_devices = lax.axis_size("dp")
    devices = dp_devices * expert_devices
    assert up_weight.shape[0] == 1
    expert_count = expert_devices
    capacity = seq_len * 5 // (4 * expert_count)
    padded_capacity = -(-capacity // 16) * 16
    slots = sequences * padded_capacity
    taps = conv_weight.shape[0]
    rank = dtproj_weight.shape[0]
    states = a_log.shape[0]
    channels = skip_gain.shape[0]
    inner_width = channels * devices
    steps = dp_devices // 2
    expert_index = lax.axis_index("expert")
    small = jnp.concatenate(
        [
            xproj_weight,
            dtproj_weight.T,
            a_log.T,
            conv_weight.T,
            conv_bias[:, None],
            dt_bias[:, None],
            skip_gain[:, None],
        ],
        axis=1,
    )
    streams = Streams()

    def ring_blocks(block):
        ring = mesh_rings()[0]
        blocks = streams.blocks
        blocks.append(block)
        for _ in range(steps - 1):
            blocks.append((yield ring.hop(blocks[-1])))
        return blocks

    in_block = lax.dynamic_index_in_dim(
        in_weight.reshape(2, expert_devices, channels, model_width), expert_index, 1, keepdims=False
    ).reshape(2 * channels, model_width)
    streams.start("in", far_gather(in_block))
    streams.start("small", small_gather(small))
    for _ in range(steps - 1):
        streams.advance(("in", "small"))
    in_blocks = streams.done["in"].reshape(2, -1, model_width)
    with jax.named_scope("fetch_in"):
        in_cube = cube_gather(jnp.concatenate([in_blocks[0], in_blocks[1]], axis=1))
    expert_block = jnp.concatenate([up_weight[0], down_weight[0]], axis=0)
    expert_block = lax.optimization_barrier((expert_block, in_blocks))[0]
    streams.start("expert", ring_blocks(expert_block))
    for _ in range(3):
        streams.advance(("small",))
    out_block = part_rows(out_weight, expert_index * channels, channels)
    out_block = streams.advance(("small", "expert"), out_block)
    streams.start("out", far_and_pair(out_block))
    streams.finish(("out", "small"))
    with jax.named_scope("fetch_out"):
        out_full = cube_gather(streams.done["out"].reshape(-1, model_width))
    small_full = streams.done["small"]
    xproj_width = rank + 2 * states
    xproj_full = small_full[:, :xproj_width]
    across = small_full[:, xproj_width:].T
    dtproj_full = across[:rank]
    across = across[rank:].astype(jnp.float32)
    log_rates = across[:states]
    conv_full = across[states : states + taps]
    convb_full = across[states + taps]
    dtb_full = across[states + taps + 1]
    skip_full = across[states + taps + 2]
    conv_rows = jnp.concatenate(
        [
            conv_full,
            convb_full[None],
            skip_full[None],
            jnp.zeros((ROWS - taps - 2, inner_width), jnp.float32),
        ],
        axis=0,
    )
    segment_rows = segments.reshape(sequences, seq_len)
    masks = [same_document(segment_rows, offset)[:, :, None] for offset in range(taps)]
    mask_columns = jnp.concatenate([mask.reshape(tokens, 1) for mask in masks], axis=1)
    rate = -jnp.exp(log_rates)
    rate_two = rate * LOG2E
    route_rows = routes.reshape(sequences, seq_len)
    placed = dispatch_matrices(
        route_rows ^ expert_index.astype(jnp.int32), expert_count, capacity, padded_capacity
    )
    in_cube, conv_rows, mask_columns, xproj_full, dtproj_full, rate_two, placed, dtb_full = (
        lax.optimization_barrier(
            (in_cube, conv_rows, mask_columns, xproj_full, dtproj_full, rate_two, placed, dtb_full)
        )
    )
    inner_full = in_cube[:, :model_width]
    gate_full = in_cube[:, model_width:]
    gain_one = norm1_gain.astype(jnp.float32)
    gain_two = norm2_gain.astype(jnp.float32)
    router_full = router_weight.astype(jnp.float32)

    def split(values):
        return values.reshape(sequences, seq_len, values.shape[-1])

    def flat(values):
        return values.reshape(tokens, values.shape[-1])

    rows_in = layer_input.reshape(tokens, model_width).astype(jnp.float32)
    cot_rows = cotangent.reshape(tokens, model_width).astype(jnp.float32)
    normed_one, norm_pull = jax.vjp(rms_scale, rows_in, gain_one)
    normed_low = normed_one.astype(LOW)
    inner = split(dot(normed_low, inner_full, ((1,), (1,))))
    gate_in = split(dot(normed_low, gate_full, ((1,), (1,))))
    conv_out = jax.nn.silu(conv_sum(inner, conv_full, convb_full, masks))
    conv_low = flat(conv_out).astype(LOW)
    projected = dot(conv_low, xproj_full, ((1,), (0,)))
    dt_low = projected[:, :rank].astype(LOW)
    b_wide = jnp.broadcast_to(
        split(projected[:, rank : rank + states])[..., None], (sequences, seq_len, states, LANES)
    )
    c_wide = jnp.broadcast_to(
        split(projected[:, rank + states :])[..., None], (sequences, seq_len, states, LANES)
    )
    dt_sum = split(dot(dt_low, dtproj_full, ((1,), (0,)))) + dtb_full
    delta = jax.nn.softplus(dt_sum)
    decay = jnp.where(masks[1] > 0, delta, FAR)
    drive = delta * conv_out
    scanned = run_forward(decay, drive, b_wide, c_wide, rate_two)
    scanned = streams.advance(("expert",), scanned)
    mixed = scanned + skip_full * conv_out
    gate_silu = jax.nn.silu(gate_in)
    mixed_low = flat(mixed * gate_silu).astype(LOW)
    residual = rows_in + dot(mixed_low, out_full, ((1,), (0,)))

    chosen_rows = (
        route_rows.reshape(tokens, 1) == jnp.arange(expert_count, dtype=jnp.int32)[None]
    ).astype(jnp.float32)

    def route_piece(resid_value, gain_value, router_value):
        return norm_route(resid_value, gain_value, router_value, chosen_rows)

    (normed_two, gate_row), route_pull = jax.vjp(route_piece, residual, gain_two, router_full)
    sending = split(
        jnp.concatenate(
            [normed_two.astype(LOW), (cot_rows * gate_row[:, None]).astype(LOW)], axis=1
        )
    )

    def partners(cross, k):
        place = lambda d, e: d * expert_devices + e
        return [
            (place(d, e), place(d ^ cross, e ^ k))
            for d in range(dp_devices)
            for e in range(expert_devices)
        ]

    def exchange(piece, cross, k):
        if not cross and not k:
            return piece
        return lax.ppermute(piece, BOTH, partners(cross, k))

    pieces = [
        jnp.einsum("stk,std->skd", matrix, sending, preferred_element_type=jnp.float32).astype(LOW)
        for matrix in placed
    ]
    with jax.named_scope("send_rows"):
        received = [
            [exchange(pieces[k], cross, k).reshape(slots, -1) for k in range(expert_count)]
            for cross in (0, 1)
        ]

    units = up_weight.shape[1]
    while len(streams.blocks) < steps - 1:
        streams.advance(("expert",))
    received[0] = list(streams.advance(("expert",), *received[0]))
    blocks = streams.done["expert"]
    own_results, own_kept = run_expert(received[0], blocks)
    cross_results, cross_kept = run_expert(received[1], blocks)
    results = [
        [piece.reshape(sequences, padded_capacity, 2 * model_width) for piece in group]
        for group in (own_results, cross_results)
    ]
    kept = [own_kept, cross_kept]
    kept, results = lax.optimization_barrier((kept, results))
    with jax.named_scope("send_results"):
        arrived = [
            [exchange(results[cross][k], cross, k) for k in range(expert_count)]
            for cross in (0, 1)
        ]
    kept, arrived[0] = lax.optimization_barrier((kept, arrived[0]))
    up_terms = [0.0] * steps
    down_terms = [0.0] * steps
    for rows, active_rows, d_hidden_rows in kept:
        for k in range(steps):
            part = slice(k * units, (k + 1) * units)
            up_terms[k] = up_terms[k] + dot(
                d_hidden_rows[:, part], rows[:, :model_width], ((0,), (0,))
            )
            down_terms[k] = down_terms[k] + dot(
                active_rows[:, part], rows[:, model_width:], ((0,), (0,))
            )
    terms = [
        jnp.concatenate([up.astype(LOW), down.astype(LOW)], axis=0)
        for up, down in zip(up_terms, down_terms)
    ]
    terms, arrived[1] = lax.optimization_barrier((terms, arrived[1]))
    streams.start("expert_grad", ring_sum(terms))
    streams.advance(("expert_grad",))
    gathered_both = 0.0
    for k in range(expert_count):
        total = (arrived[0][k].astype(jnp.float32) + arrived[1][k].astype(jnp.float32)).astype(LOW)
        gathered_both = gathered_both + jnp.einsum(
            "stk,skd->std", placed[k], total, preferred_element_type=jnp.float32
        )
    gathered_both = flat(gathered_both)
    gathered = gathered_both[:, :model_width]
    d_sent = gathered_both[:, model_width:]
    layer_output = (residual + gate_row[:, None] * gathered).astype(LOW)


    d_gate = jnp.sum(cot_rows * gathered, axis=1)
    d_resid_norm, d_gain_two, d_router = route_pull((d_sent, d_gate))
    d_residual = cot_rows + d_resid_norm
    d_branch_low = d_residual.astype(LOW)

    out_gate_term, d_gate_low, d_scanned = run_gate_backward(
        d_branch_low, normed_low, out_full, mixed_low, flat(mixed), flat(gate_in)
    )
    with jax.named_scope("reduce_out_gate"):
        out_gate_blocks = cube_scatter(out_gate_term)
    d_scanned = split(d_scanned)
    d_drive, d_decay, d_rate, d_b, d_c = run_backward(
        decay, drive, b_wide, c_wide, rate_two, d_scanned
    )
    d_drive = streams.advance(("expert_grad",), d_drive)
    streams.advance(("expert_grad",))
    d_skip = jnp.sum(d_scanned * conv_out, axis=(0, 1))
    d_alog = jnp.sum(d_rate, axis=0) * rate
    d_delta = d_decay * (1.0 / LOG2E) + d_drive * conv_out
    d_dt = d_delta * jax.nn.sigmoid(dt_sum)
    d_dtb = jnp.sum(d_dt, axis=(0, 1))
    d_dt_low = flat(d_dt).astype(LOW)
    d_dt_rows = dot(d_dt_low, dtproj_full, ((1,), (1,)))
    d_proj_low = jnp.concatenate(
        [
            d_dt_rows,
            d_b[:, 0].reshape(tokens, states),
            d_c[:, 0].reshape(tokens, states),
        ],
        axis=1,
    ).astype(LOW)
    more_rows = jnp.concatenate([d_alog, d_dtb[None], d_skip[None]], axis=0)
    more_rows = jnp.pad(more_rows, ((0, -more_rows.shape[0] % ROWS), (0, 0)))
    inner_term, d_normed = run_conv_backward(
        flat(d_drive),
        flat(delta),
        flat(d_scanned),
        flat(inner),
        d_gate_low,
        d_proj_low,
        normed_low,
        mask_columns,
        conv_rows,
        xproj_full,
        in_cube,
        d_dt_low,
        dt_low,
        more_rows,
    )
    inner_term, d_normed, out_gate_blocks = streams.advance(
        ("expert_grad",), inner_term, d_normed, out_gate_blocks
    )
    with jax.named_scope("reduce_inner"):
        inner_blocks = cube_scatter(inner_term)
    out_blocks = out_gate_blocks[:, :model_width]
    gate_blocks = out_gate_blocks[:, model_width:]
    streams.start(
        "out_grad", far_and_pair_sum(out_blocks.reshape(-1, 2, channels, model_width))
    )
    d_rows_norm, d_gain_one = norm_pull(d_normed)
    input_grad = d_residual + d_rows_norm

    gains = jnp.concatenate([d_gain_one[None], d_gain_two[None], d_router.T], axis=0)
    streams.start("gains", near_sum(gains))
    streams.advance(("out_grad",))
    streams.finish(("out_grad",))
    out_part = streams.advance(("expert_grad",), streams.done["out_grad"])
    streams.finish(("gains",))
    gains = streams.done["gains"]
    inner_blocks = streams.advance(("expert_grad",), inner_blocks)
    half = (steps // 2, 2, channels, model_width)
    streams.start(
        "in_grad",
        far_sum(inner_blocks[:, :model_width].reshape(half), gate_blocks.reshape(half)),
    )
    small_blocks = inner_blocks[:, model_width:]
    streams.start(
        "small_grad",
        far_and_pair_sum(small_blocks.reshape(-1, 2, channels, small_blocks.shape[1])),
    )
    streams.advance(("small_grad",))
    streams.start("out_rows", shared_rows(out_part[None]))
    gains = streams.advance(("in_grad",), gains)
    streams.start("in_rows", shared_rows(streams.done["in_grad"]))
    streams.start("gains", butterfly(gains, "dp", 2, dp_devices))
    streams.advance(("in_rows", "out_rows", "gains"))
    streams.finish(("in_rows", "out_rows", "gains", "small_grad", "expert_grad"))
    gains = streams.done["gains"]
    in_grad = streams.done["in_rows"].reshape(in_weight.shape).astype(jnp.float32)
    out_grad = streams.done["out_rows"][0].astype(jnp.float32)
    expert_grad = streams.done["expert_grad"].astype(jnp.float32)
    up_grad, down_grad = expert_grad[:units], expert_grad[units:]
    small_grad = streams.done["small_grad"].astype(jnp.float32)
    xproj_grad = small_grad[:, :xproj_width]
    row_grads = small_grad[:, xproj_width:].T
    dtproj_grad = row_grads[:rank]
    row_grads = row_grads[rank:]
    conv_grad = row_grads[:taps]
    convb_grad = row_grads[taps]
    alog_grad = row_grads[ROWS : ROWS + states]
    dtb_grad, skip_grad = row_grads[ROWS + states], row_grads[ROWS + states + 1]

    return (
        layer_output.reshape(layer_input.shape),
        input_grad.reshape(layer_input.shape),
        gains[0],
        in_grad,
        conv_grad,
        convb_grad,
        xproj_grad,
        dtproj_grad,
        dtb_grad,
        alog_grad,
        skip_grad,
        out_grad,
        gains[1],
        gains[2:].T,
        up_grad[None],
        down_grad[None],
    )


def solution(mesh):
    placed = (
        P(None, ("dp", "expert"), None, None),
        P(None, ("dp", "expert"), None),
        P(None, ("dp", "expert"), None, None),
        P(None, ("dp", "expert"), None, None),
        P(),
        P("dp", None),
        P(None, ("dp", "expert")),
        P(("dp", "expert")),
        P(("dp", "expert"), None),
        P(None, ("dp", "expert")),
        P(("dp", "expert")),
        P(None, ("dp", "expert")),
        P(("dp", "expert")),
        P("dp", None),
        P(),
        P(),
        P("expert", "dp", None),
        P("expert", "dp", None),
    )
    return jax.shard_map(
        on_device,
        mesh=mesh,
        in_specs=placed,
        out_specs=(
            P(None, ("dp", "expert"), None, None),
            P(None, ("dp", "expert"), None, None),
            P(),
            P("dp", None),
            P(None, ("dp", "expert")),
            P(("dp", "expert")),
            P(("dp", "expert"), None),
            P(None, ("dp", "expert")),
            P(("dp", "expert")),
            P(None, ("dp", "expert")),
            P(("dp", "expert")),
            P("dp", None),
            P(),
            P(),
            P("expert", "dp", None),
            P("expert", "dp", None),
        ),
        check_vma=False,
    )
```

```python
import functools

import jax
import jax.numpy as jnp
from jax import lax
from jax.experimental import pallas as pl
from jax.experimental.pallas import tpu as pltpu
from jax.sharding import PartitionSpec as P

LANES = 128
VMEM_GRANT = 40 << 20
ROWS = 8

def wide(tile, width):
    return jnp.concatenate([tile] * (width // LANES), axis=1)

def narrow(values):
    total = values[:, :LANES]
    for start in range(LANES, values.shape[1], LANES):
        total = total + values[:, start : start + LANES]
    return total

def fold_states(pieces, position):
    folded = []
    for piece in pieces:
        total = piece[:ROWS]
        for start in range(ROWS, piece.shape[0], ROWS):
            total = total + piece[start : start + ROWS]
        folded.append(total)
    low = (position & 4) == 0
    folded = [
        jnp.where(low, a, b) + pltpu.roll(jnp.where(low, b, a), 4, 0)
        for a, b in zip(folded[:4], folded[4:])
    ]
    for step in (2, 1):
        low = (position & step) == 0
        half = len(folded) // 2
        folded = [
            jnp.where(low, a + pltpu.roll(a, ROWS - step, 0), b + pltpu.roll(b, step, 0))
            for a, b in zip(folded[:half], folded[half:])
        ]
    return folded[0]

def scan_forward(decay_ref, drive_ref, b_ref, c_ref, rate_ref, out_ref):
    length, width = decay_ref.shape[1:]
    rate = rate_ref[...]
    position = lax.broadcasted_iota(jnp.int32, (ROWS, width), 0)

    def block(index, state):
        start = pl.multiple_of(index * ROWS, ROWS)
        pieces = []
        for offset in range(ROWS):
            t = start + offset
            factor = jnp.exp2(decay_ref[0, pl.ds(t, 1), :] * rate)
            state = factor * state + drive_ref[0, pl.ds(t, 1), :] * wide(b_ref[0, t], width)
            pieces.append(state * wide(c_ref[0, t], width))
        out_ref[0, pl.ds(start, ROWS), :] = fold_states(pieces, position)
        return state

    lax.fori_loop(0, length // ROWS, block, jnp.zeros_like(rate))

def scan_backward(
    decay_ref, drive_ref, b_ref, c_ref, rate_ref, dout_ref, delta_ref, conv_out_ref, dt_sum_ref,
    skip_ref, dtproj_ref,
    d_conv_ref, d_dt_ref, d_low_ref, rows_ref, db_sum_ref, dc_sum_ref,
    db_ref, dc_ref, state_ref, factor_ref, ddrive_ref, ddecay_ref,
):
    length, width = decay_ref.shape[1:]
    rate = rate_ref[...]
    position = lax.broadcasted_iota(jnp.int32, (ROWS, width), 0)

    @pl.when(pl.program_id(1) == 0)
    def _():
        db_ref[...] = jnp.zeros_like(db_ref)
        dc_ref[...] = jnp.zeros_like(dc_ref)

    state_ref[0] = jnp.zeros_like(rate)

    def replay(index, state):
        start = pl.multiple_of(index * ROWS, ROWS)
        for offset in range(ROWS):
            t = start + offset
            factor = jnp.exp2(decay_ref[0, pl.ds(t, 1), :] * rate)
            state = factor * state + drive_ref[0, pl.ds(t, 1), :] * wide(b_ref[0, t], width)
            factor_ref[t] = factor
            state_ref[t + 1] = state
        return state

    lax.fori_loop(0, length // ROWS, replay, jnp.zeros_like(rate))

    def block(index, carried):
        later, drate = carried
        start = pl.multiple_of(length - ROWS - index * ROWS, ROWS)
        drive_pieces = [None] * ROWS
        decay_pieces = [None] * ROWS
        for offset in reversed(range(ROWS)):
            t = start + offset
            dout = dout_ref[0, pl.ds(t, 1), :]
            dstate = later + dout * wide(c_ref[0, t], width)
            dc_ref[t] += narrow(dout * state_ref[t + 1])
            db_ref[t] += narrow(dstate * drive_ref[0, pl.ds(t, 1), :])
            drive_pieces[offset] = dstate * wide(b_ref[0, t], width)
            later = dstate * factor_ref[t]
            power = later * state_ref[t]
            decay_pieces[offset] = power * rate
            drate = drate + power * decay_ref[0, pl.ds(t, 1), :]
        ddrive_ref[pl.ds(start, ROWS), :] = fold_states(drive_pieces, position)
        ddecay_ref[pl.ds(start, ROWS), :] = fold_states(decay_pieces, position)
        return later, drate

    zero = jnp.zeros_like(rate)
    drate = lax.fori_loop(0, length // ROWS, block, (zero, zero))[1]
    states = rate.shape[0]
    ddrive = ddrive_ref[...]
    dout = dout_ref[0]
    conv_out = conv_out_ref[0]
    d_conv_ref[0] = ddrive * delta_ref[0] + dout * skip_ref[...]
    d_delta = ddecay_ref[...] * (1.0 / LOG2E) + ddrive * conv_out
    d_dt = d_delta * jax.nn.sigmoid(dt_sum_ref[0])
    d_dt_low = d_dt.astype(jnp.bfloat16)
    d_dt_ref[0] = d_dt_low
    rows_ref[0, :states, :] = drate * rate * (1.0 / LOG2E)
    rows_ref[0, states:, :] = jnp.concatenate(
        [
            jnp.sum(d_dt, axis=0, keepdims=True),
            jnp.sum(dout * conv_out, axis=0, keepdims=True),
            jnp.zeros((rows_ref.shape[1] - states - 2, width), jnp.float32),
        ],
        axis=0,
    )
    d_low = product(d_dt_low, dtproj_ref[...], ((1,), (1,)))

    @pl.when(pl.program_id(1) == 0)
    def _():
        d_low_ref[0] = d_low

    @pl.when(pl.program_id(1) > 0)
    def _():
        d_low_ref[0] += d_low

    @pl.when(pl.program_id(1) == pl.num_programs(1) - 1)
    def _():
        ones = jnp.ones((ROWS, LANES), jnp.float32)
        for total_ref, sum_ref in ((db_ref, db_sum_ref), (dc_ref, dc_sum_ref)):
            sum_ref[0] = lax.dot_general(
                ones,
                total_ref[...].reshape(-1, LANES),
                (((1,), (1,)), ((), ())),
                precision=lax.Precision.HIGHEST,
                preferred_element_type=jnp.float32,
            )

def tile_width(width):
    for tiles in (3, 2, 1):
        if width % (tiles * LANES) == 0:
            return tiles * LANES
    return width

def scan_specs(length, states, width):
    tokens = pl.BlockSpec((1, length, width), lambda s, c: (s, 0, c))
    maps = pl.BlockSpec((1, length, states, LANES), lambda s, c: (s, 0, 0, 0))
    rates = pl.BlockSpec((states, width), lambda s, c: (0, c))
    return tokens, maps, rates

def run_forward(decay, drive, b_wide, c_wide, rate):
    count, length, channels = decay.shape
    states = rate.shape[0]
    width = tile_width(channels)
    tokens, maps, rates = scan_specs(length, states, width)
    return pl.pallas_call(
        scan_forward,
        grid=(count, channels // width),
        in_specs=[tokens, tokens, maps, maps, rates],
        out_specs=tokens,
        out_shape=jax.ShapeDtypeStruct(decay.shape, jnp.float32),
        cost_estimate=pl.CostEstimate(
            flops=decay.size, transcendentals=0,
            bytes_accessed=4 * (3 * decay.size + 2 * b_wide.size)),
        compiler_params=pltpu.CompilerParams(vmem_limit_bytes=VMEM_GRANT),
        name="scan_forward",
    )(decay, drive, b_wide, c_wide, rate)

def run_backward(
    decay, drive, b_wide, c_wide, rate, dout, delta, conv_out, dt_sum, skip, dtproj
):
    count, length, channels = decay.shape
    states = rate.shape[0]
    rank = dtproj.shape[0]
    width = tile_width(channels)
    extra = states + ROWS
    tokens, maps, rates = scan_specs(length, states, width)
    summed = jax.ShapeDtypeStruct((count, ROWS, length * states), jnp.float32)
    sums = pl.BlockSpec((1, ROWS, length * states), lambda s, c: (s, 0, 0))
    return pl.pallas_call(
        scan_backward,
        grid=(count, channels // width),
        in_specs=[tokens, tokens, maps, maps, rates, tokens, tokens, tokens, tokens]
        + [
            pl.BlockSpec((1, width), lambda s, c: (0, c)),
            pl.BlockSpec((rank, width), lambda s, c: (0, c)),
        ],
        out_specs=[
            tokens,
            tokens,
            pl.BlockSpec((1, length, rank), lambda s, c: (s, 0, 0)),
            pl.BlockSpec((1, extra, width), lambda s, c: (s, 0, c)),
            sums,
            sums,
        ],
        out_shape=[
            jax.ShapeDtypeStruct(decay.shape, jnp.float32),
            jax.ShapeDtypeStruct(decay.shape, jnp.bfloat16),
            jax.ShapeDtypeStruct((count, length, rank), jnp.float32),
            jax.ShapeDtypeStruct((count, extra, channels), jnp.float32),
            summed,
            summed,
        ],
        scratch_shapes=[
            pltpu.VMEM((length, states, LANES), jnp.float32),
            pltpu.VMEM((length, states, LANES), jnp.float32),
            pltpu.VMEM((length + 1, states, width), jnp.float32),
            pltpu.VMEM((length, states, width), jnp.float32),
            pltpu.VMEM((length, width), jnp.float32),
            pltpu.VMEM((length, width), jnp.float32),
        ],
        cost_estimate=pl.CostEstimate(
            flops=decay.size, transcendentals=0, bytes_accessed=decay.size
        ),
        compiler_params=pltpu.CompilerParams(vmem_limit_bytes=60 << 20),
        name="scan_backward",
    )(decay, drive, b_wide, c_wide, rate, dout, delta, conv_out, dt_sum, skip, dtproj)


def product(left, right, contract):
    return lax.dot_general(left, right, (contract, ((), ())), preferred_element_type=jnp.float32)


def conv_forward(
    normed_ref, in_ref, masks_ref, conv_ref, xproj_ref, inner_ref, gate_ref, conv_out_ref, maps_ref
):
    taps = masks_ref.shape[1]
    model = normed_ref.shape[1]
    inner = product(normed_ref[...], in_ref[:, :model], ((1,), (1,)))
    inner_ref[...] = inner
    gate_ref[...] = product(normed_ref[...], in_ref[:, model:], ((1,), (1,)))
    total = conv_ref[taps : taps + 1] + conv_ref[taps - 1 : taps] * inner
    for offset in range(1, taps):
        total = total + conv_ref[taps - 1 - offset : taps - offset] * (
            pltpu.roll(inner, offset, 0) * masks_ref[:, offset : offset + 1]
        )
    conv_out = total * jax.nn.sigmoid(total)
    conv_out_ref[...] = conv_out
    maps = product(conv_out.astype(jnp.bfloat16), xproj_ref[...], ((1,), (0,)))

    @pl.when(pl.program_id(0) == 0)
    def _():
        maps_ref[...] = maps

    @pl.when(pl.program_id(0) > 0)
    def _():
        maps_ref[...] += maps


def run_conv_forward(normed, in_rows, masks, conv_rows, xproj):
    count, model = normed.shape
    channels = in_rows.shape[0]
    width = tile_width(channels)
    tokens = pl.BlockSpec((count, width), lambda c: (0, c))
    full = jax.ShapeDtypeStruct((count, channels), jnp.float32)

    def whole(values):
        return pl.BlockSpec(values.shape, lambda c: (0, 0))

    def rows(values):
        return pl.BlockSpec((width, values.shape[1]), lambda c: (c, 0))

    return pl.pallas_call(
        conv_forward,
        grid=(channels // width,),
        in_specs=[
            whole(normed),
            rows(in_rows),
            whole(masks),
            pl.BlockSpec((ROWS, width), lambda c: (0, c)),
            rows(xproj),
        ],
        out_specs=[
            tokens,
            tokens,
            tokens,
            pl.BlockSpec((count, xproj.shape[1]), lambda c: (0, 0)),
        ],
        out_shape=[full, full, full, jax.ShapeDtypeStruct((count, xproj.shape[1]), jnp.float32)],
        cost_estimate=pl.CostEstimate(flops=count, transcendentals=0, bytes_accessed=count),
        compiler_params=pltpu.CompilerParams(vmem_limit_bytes=VMEM_GRANT),
        name="conv_forward",
    )(normed, in_rows, masks, conv_rows, xproj)


def gate_backward(
    d_branch_ref, normed_ref, out_ref, mixed_low_ref, mixed_ref, gate_ref,
    term_ref, d_gate_ref, d_scanned_ref,
):
    model = d_branch_ref.shape[1]
    d_branch = d_branch_ref[...]
    d_mixed = product(d_branch, out_ref[...], ((1,), (1,)))
    gate = gate_ref[...]
    chance = jax.nn.sigmoid(gate)
    d_gate = d_mixed * mixed_ref[...] * (chance * (1.0 + gate * (1.0 - chance)))
    d_gate = d_gate.astype(jnp.bfloat16)
    d_gate_ref[...] = d_gate
    d_scanned_ref[...] = d_mixed * gate * chance
    term_ref[:, :model] = product(mixed_low_ref[...], d_branch, ((0,), (0,))).astype(jnp.bfloat16)
    term_ref[:, model:] = product(d_gate, normed_ref[...], ((0,), (0,))).astype(jnp.bfloat16)


def run_gate_backward(d_branch, normed, out_rows, mixed_low, mixed, gate):
    count, model = d_branch.shape
    channels = mixed.shape[1]
    width = tile_width(channels)
    whole = pl.BlockSpec((count, model), lambda c: (0, 0))
    rows = pl.BlockSpec((width, model), lambda c: (c, 0))
    tokens = pl.BlockSpec((count, width), lambda c: (0, c))
    return pl.pallas_call(
        gate_backward,
        grid=(channels // width,),
        in_specs=[whole, whole, rows, tokens, tokens, tokens],
        out_specs=[pl.BlockSpec((width, 2 * model), lambda c: (c, 0)), tokens, tokens],
        out_shape=[
            jax.ShapeDtypeStruct((channels, 2 * model), jnp.bfloat16),
            jax.ShapeDtypeStruct((count, channels), jnp.bfloat16),
            jax.ShapeDtypeStruct((count, channels), jnp.float32),
        ],
        cost_estimate=pl.CostEstimate(flops=count, transcendentals=0, bytes_accessed=count),
        compiler_params=pltpu.CompilerParams(vmem_limit_bytes=VMEM_GRANT),
        name="gate_backward",
    )(d_branch, normed, out_rows, mixed_low, mixed, gate)


def conv_backward(
    d_scan_ref, inner_ref, d_gate_ref, d_proj_ref, normed_ref,
    masks_ref, conv_ref, xproj_ref, in_ref, d_dt_ref, dt_ref, rows_ref,
    term_ref, d_normed_ref,
):
    taps = masks_ref.shape[1]
    model = normed_ref.shape[1]
    count = inner_ref.shape[0]
    d_conv = d_scan_ref[...] + product(d_proj_ref[...], xproj_ref[...], ((1,), (1,)))
    inner = inner_ref[...]
    shifted = [inner] + [pltpu.roll(inner, offset, 0) for offset in range(1, taps)]
    masked = [shifted[offset] * masks_ref[:, offset : offset + 1] for offset in range(taps)]
    total = conv_ref[taps : taps + 1]
    for offset in range(taps):
        total = total + conv_ref[taps - 1 - offset : taps - offset] * masked[offset]
    chance = jax.nn.sigmoid(total)
    d_sum = d_conv * (chance * (1.0 + total * (1.0 - chance)))
    d_inner = jnp.zeros_like(inner)
    rows = []
    for offset in range(taps):
        rows.append(jnp.sum(d_sum * masked[offset], axis=0, keepdims=True))
        back = d_sum * masks_ref[:, offset : offset + 1]
        if offset:
            back = pltpu.roll(back, count - offset, 0)
        d_inner = d_inner + conv_ref[taps - 1 - offset : taps - offset] * back
    rows = rows[::-1] + [jnp.sum(d_sum, axis=0, keepdims=True)]
    rows = jnp.concatenate(
        rows + [jnp.zeros_like(rows[0])] * (ROWS - len(rows)) + [rows_ref[...]], axis=0
    ).astype(jnp.bfloat16)
    extent = rows.shape[0]
    same = lax.broadcasted_iota(jnp.int32, (extent, extent), 0) == lax.broadcasted_iota(
        jnp.int32, (extent, extent), 1
    )
    columns = product(rows, same.astype(jnp.bfloat16), ((0,), (0,)))
    conv_low = (total * chance).astype(jnp.bfloat16)
    edge = model + d_proj_ref.shape[1]
    middle = edge + dt_ref.shape[1]
    term_ref[:, model:edge] = product(conv_low, d_proj_ref[...], ((0,), (0,))).astype(jnp.bfloat16)
    term_ref[:, edge:middle] = product(d_dt_ref[...], dt_ref[...], ((0,), (0,))).astype(
        jnp.bfloat16
    )
    term_ref[:, middle:] = columns.astype(jnp.bfloat16)
    d_inner = d_inner.astype(jnp.bfloat16)
    term_ref[:, :model] = product(d_inner, normed_ref[...], ((0,), (0,))).astype(jnp.bfloat16)
    d_normed = product(d_inner, in_ref[:, :model], ((1,), (0,))) + product(
        d_gate_ref[...], in_ref[:, model:], ((1,), (0,))
    )

    @pl.when(pl.program_id(0) == 0)
    def _():
        d_normed_ref[...] = d_normed

    @pl.when(pl.program_id(0) > 0)
    def _():
        d_normed_ref[...] += d_normed


def run_conv_backward(
    d_scan,
    inner,
    d_gate,
    d_proj,
    normed,
    masks,
    conv_rows,
    xproj,
    in_rows,
    d_dt,
    dt,
    more_rows,
):
    count, channels = inner.shape
    model = normed.shape[1]
    width = tile_width(channels)
    tokens = pl.BlockSpec((count, width), lambda c: (0, c))
    small_width = d_proj.shape[1] + dt.shape[1] + ROWS + more_rows.shape[0]

    def whole(values):
        return pl.BlockSpec(values.shape, lambda c: (0, 0))

    def rows(values):
        return pl.BlockSpec((width, values.shape[1]), lambda c: (c, 0))

    return pl.pallas_call(
        conv_backward,
        grid=(channels // width,),
        in_specs=[
            tokens,
            tokens,
            tokens,
            whole(d_proj),
            whole(normed),
            whole(masks),
            pl.BlockSpec((ROWS, width), lambda c: (0, c)),
            rows(xproj),
            rows(in_rows),
            tokens,
            whole(dt),
            pl.BlockSpec((more_rows.shape[0], width), lambda c: (0, c)),
        ],
        out_specs=[
            pl.BlockSpec((width, model + small_width), lambda c: (c, 0)),
            pl.BlockSpec((count, model), lambda c: (0, 0)),
        ],
        out_shape=[
            jax.ShapeDtypeStruct((channels, model + small_width), jnp.bfloat16),
            jax.ShapeDtypeStruct((count, model), jnp.float32),
        ],
        cost_estimate=pl.CostEstimate(flops=count, transcendentals=0, bytes_accessed=count),
        compiler_params=pltpu.CompilerParams(vmem_limit_bytes=VMEM_GRANT),
        name="conv_backward",
    )(
        d_scan,
        inner,
        d_gate,
        d_proj,
        normed,
        masks,
        conv_rows,
        xproj,
        in_rows,
        d_dt,
        dt,
        more_rows,
    )


GELU_SCALE = 0.7978845608028654
GELU_CUBE = 0.044715


def expert_units(slot_rows, d_returned, up, down):
    hidden = product(slot_rows, up, ((1,), (1,)))
    square = hidden * hidden
    bend = jnp.tanh(GELU_SCALE * (hidden + GELU_CUBE * (square * hidden)))
    share = 0.5 * (1.0 + bend)
    active = (hidden * share).astype(jnp.bfloat16)
    slope = share + hidden * (0.5 * GELU_SCALE) * (1.0 - bend * bend) * (
        1.0 + 3.0 * GELU_CUBE * square
    )
    d_active = product(d_returned, down, ((1,), (1,)))
    d_hidden = (d_active * slope).astype(jnp.bfloat16)
    returned = product(active, down, ((1,), (0,)))
    d_slots = product(d_hidden, up, ((1,), (0,)))
    return active, d_hidden, returned, d_slots


def expert_first(pieces, blocks, *refs):
    piece_refs, block_refs = refs[:pieces], refs[pieces : pieces + blocks]
    rows_ref, active_ref, d_hidden_ref, total_ref, held_ref, sems = refs[pieces + blocks :]
    copies = [
        pltpu.make_async_copy(block_refs[k], held_ref.at[k], sems.at[k]) for k in range(blocks)
    ]
    for copy in copies:
        copy.start()
    length = piece_refs[0].shape[0]
    for n in range(pieces):
        rows_ref[n * length : (n + 1) * length, :] = piece_refs[n][...]
    model = rows_ref.shape[1] // 2
    units = held_ref.shape[1] // 2
    slot_rows, d_returned = rows_ref[:, :model], rows_ref[:, model:]
    for k in range(blocks):
        copies[k].wait()
        active, d_hidden, returned, d_slots = expert_units(
            slot_rows, d_returned, held_ref[k, :units, :], held_ref[k, units:, :]
        )
        active_ref[:, k * units : (k + 1) * units] = active
        d_hidden_ref[:, k * units : (k + 1) * units] = d_hidden
        if k:
            returned = returned + total_ref[:, :model]
            d_slots = d_slots + total_ref[:, model:]
        total_ref[:, :model] = returned
        total_ref[:, model:] = d_slots


def run_expert_first(pieces, blocks):
    length, width = pieces[0].shape
    rows = length * len(pieces)
    units = blocks[0].shape[0] // 2
    low = jnp.bfloat16
    vmem = pl.BlockSpec(memory_space=pltpu.VMEM)
    return pl.pallas_call(
        functools.partial(expert_first, len(pieces), len(blocks)),
        in_specs=[vmem] * len(pieces) + [pl.BlockSpec(memory_space=pl.ANY)] * len(blocks),
        out_specs=[vmem] * 4,
        out_shape=[
            jax.ShapeDtypeStruct((rows, width), low),
            jax.ShapeDtypeStruct((rows, units * len(blocks)), low),
            jax.ShapeDtypeStruct((rows, units * len(blocks)), low),
            jax.ShapeDtypeStruct((rows, width), jnp.float32),
        ],
        scratch_shapes=[
            pltpu.VMEM((len(blocks),) + blocks[0].shape, low),
            pltpu.SemaphoreType.DMA((len(blocks),)),
        ],
        cost_estimate=pl.CostEstimate(flops=rows, transcendentals=0, bytes_accessed=rows),
        compiler_params=pltpu.CompilerParams(vmem_limit_bytes=VMEM_GRANT),
        name="expert_first",
    )(*pieces, *blocks)


def expert_last(pieces, rows_refs, total_refs, block_ref, result_refs, active_ref, d_hidden_ref):
    model = rows_refs[0].shape[1] // 2
    units = block_ref.shape[0] // 2
    extent = rows_refs[0].shape[0]
    length = extent // pieces
    for n in range(2):
        active, d_hidden, returned, d_slots = expert_units(
            rows_refs[n][:, :model],
            rows_refs[n][:, model:],
            block_ref[:units, :],
            block_ref[units:, :],
        )
        active_ref[n * extent : (n + 1) * extent, :] = active
        d_hidden_ref[n * extent : (n + 1) * extent, :] = d_hidden
        returned = (returned + total_refs[n][:, :model]).astype(jnp.bfloat16)
        d_slots = (d_slots + total_refs[n][:, model:]).astype(jnp.bfloat16)
        for m in range(pieces):
            part = slice(m * length, (m + 1) * length)
            result_refs[n * pieces + m][:, :model] = returned[part]
            result_refs[n * pieces + m][:, model:] = d_slots[part]


def run_expert_last(pieces, rows, totals, block):
    extent, width = rows[0].shape
    units = block.shape[0] // 2
    low = jnp.bfloat16
    vmem = pl.BlockSpec(memory_space=pltpu.VMEM)

    def kernel(*refs):
        expert_last(pieces, refs[:2], refs[2:4], refs[4], refs[5:-2], refs[-2], refs[-1])

    out = pl.pallas_call(
        kernel,
        in_specs=[vmem] * 5,
        out_specs=[vmem] * (2 * pieces + 2),
        out_shape=[jax.ShapeDtypeStruct((extent // pieces, width), low)] * (2 * pieces)
        + [jax.ShapeDtypeStruct((2 * extent, units), low)] * 2,
        cost_estimate=pl.CostEstimate(flops=extent, transcendentals=0, bytes_accessed=extent),
        compiler_params=pltpu.CompilerParams(vmem_limit_bytes=VMEM_GRANT),
        name="expert_last",
    )(*rows, *totals, block)
    return [out[:pieces], out[pieces:-2]], out[-2], out[-1]


HIGHEST = lax.Precision.HIGHEST
EPSILON = 1e-05
LOG2E = 1.4426950408889634
FAR = 1e30
LOW = jnp.bfloat16
BOTH = ("dp", "expert")


def dot(left, right, contract):
    return lax.dot_general(left, right, (contract, ((), ())), preferred_element_type=jnp.float32)


def rms_scale(values, gain_row):
    return (
        values * lax.rsqrt(jnp.mean(values * values, axis=-1, keepdims=True) + EPSILON) * gain_row
    )


def norm_route(residual, gain_two, router_full, chosen_rows):
    normed_two = rms_scale(residual, gain_two)
    logits = jnp.dot(normed_two, router_full, precision=HIGHEST, preferred_element_type=jnp.float32)
    probabilities = jax.nn.softmax(logits, axis=-1)
    return (normed_two, jnp.sum(probabilities * chosen_rows, axis=1))


def same_document(segments, offset):
    if offset == 0:
        return jnp.ones(segments.shape, jnp.float32)
    padded = jnp.pad(segments, ((0, 0), (offset, 0)), constant_values=-1)
    return (padded[:, : segments.shape[1]] == segments).astype(jnp.float32)


def dispatch_matrices(order_rows, expert_count, capacity, padded_capacity):
    length = order_rows.shape[1]
    chosen = (
        order_rows[:, :, None] == jnp.arange(expert_count, dtype=jnp.int32)[None, None]
    ).astype(jnp.float32)
    before = jnp.tril(jnp.ones((length, length), jnp.float32), -1)
    earlier = jnp.einsum("tu,sue->ste", before, chosen, preferred_element_type=jnp.float32)
    slot = jnp.sum(earlier * chosen, axis=2).astype(jnp.int32)
    places = jnp.arange(padded_capacity, dtype=jnp.int32)
    taken = ((slot[:, :, None] == places) & (places < capacity)).astype(jnp.float32)
    return [(chosen[:, :, k, None] * taken).astype(LOW) for k in range(expert_count)]


def hop(values, step):
    axis_name, distance = step
    size = lax.axis_size(axis_name)
    return lax.ppermute(values, axis_name, [(i, i ^ distance) for i in range(size)])


class Ring:
    def __init__(self, axis_name, stride, size):
        self.axis_name = axis_name
        self.stride = stride
        self.size = size
        self.place = lax.axis_index(axis_name) // stride % size

    def hop(self, values, distance=1):
        pairs = []
        for i in range(lax.axis_size(self.axis_name)):
            place = i // self.stride % self.size
            pairs.append((i, i + ((place + distance) % self.size - place) * self.stride))
        return lax.ppermute(values, self.axis_name, pairs)


def mesh_rings():
    dp_size, expert_size = lax.axis_size("dp"), lax.axis_size("expert")
    return [
        Ring("dp", 2, dp_size // 2),
        Ring("dp", 1, 2),
        Ring("expert", 2, expert_size // 2),
        Ring("expert", 1, 2),
    ]


def cubes():
    expert_size = lax.axis_size("expert")
    wide = 2 * expert_size
    return [
        [place * wide + i for i in range(wide)] for place in range(lax.axis_size("dp") // 2)
    ]


def far_gather(block):
    ring = mesh_rings()[0]
    blocks = [block[None]]
    for _ in range(ring.size - 1):
        blocks.append((yield ring.hop(blocks[-1])))
    line = jnp.concatenate(blocks[::-1] + blocks[:0:-1], axis=0)
    return lax.dynamic_slice_in_dim(line, ring.size - 1 - ring.place, ring.size, axis=0)


def cube_gather(block):
    return lax.all_gather(block, BOTH, axis=0, tiled=True, axis_index_groups=cubes())


def cube_scatter(total):
    return lax.psum_scatter(
        total, BOTH, scatter_dimension=0, tiled=True, axis_index_groups=cubes()
    )


def block_of(values, place, axis):
    return lax.dynamic_index_in_dim(values, place, axis, keepdims=True)


def far_and_pair(block):
    pair = mesh_rings()[1]
    blocks = yield from far_gather(block)
    blocks = blocks.reshape((-1, 2) + block.shape)
    moved = yield pair.hop(block_of(blocks, 1 - pair.place, 1))
    kept = block_of(blocks, pair.place, 1)
    return jnp.where(
        pair.place == 0,
        jnp.concatenate([kept, moved], axis=1),
        jnp.concatenate([moved, kept], axis=1),
    )


def far_and_pair_sum(blocks):
    pair = mesh_rings()[1]
    moved = yield pair.hop(block_of(blocks, 1 - pair.place, 1))
    kept = block_of(blocks, pair.place, 1)
    values = jnp.where(
        pair.place == 0,
        jnp.concatenate([kept, moved], axis=1),
        jnp.concatenate([moved, kept], axis=1),
    )
    values = values.reshape((-1,) + blocks.shape[2:])
    return (yield from far_sum(values))


def cube_stages_gather(block):
    for ring in mesh_rings()[:0:-1]:
        blocks = [block[None]]
        for _ in range(ring.size - 1):
            blocks.append((yield ring.hop(blocks[-1])))
        line = jnp.concatenate(blocks[::-1] + blocks[:0:-1], axis=0)
        block = lax.dynamic_slice_in_dim(line, ring.size - 1 - ring.place, ring.size, axis=0)
        block = block.reshape((-1,) + block.shape[2:])
    return block


def small_gather(block):
    block = yield from far_and_pair(block)
    return (yield from cube_stages_gather(block.reshape(-1, block.shape[-1])))


def add_low(kept, moved):
    return (kept.astype(jnp.float32) + moved.astype(jnp.float32)).astype(LOW)


def far_sum(blocks, more=None):
    ring = mesh_rings()[0]

    def block(distance):
        place = (ring.place + distance) % ring.size
        if more is None:
            return block_of(blocks, place, 0)[0]
        middle = ring.size // 2
        return jnp.where(
            place < middle,
            block_of(blocks, place % middle, 0)[0],
            block_of(more, place % middle, 0)[0],
        )

    moved = yield tuple(ring.hop(block(distance), distance) for distance in range(1, ring.size))
    total = block(0).astype(jnp.float32)
    for part in moved:
        total = total + part.astype(jnp.float32)
    return total.astype(LOW)


def ring_sum(blocks):
    ring = mesh_rings()[0]
    count = len(blocks)
    travelling = blocks[1 % count]
    for step in range(2, count + 1):
        travelling = yield travelling.astype(LOW)
        moved = yield ring.hop(travelling)
        travelling = blocks[step % count].astype(jnp.float32) + moved.astype(jnp.float32)
    return travelling


def butterfly(values, axis_name, first, last):
    distance = first
    while distance < last:
        values = values + (yield hop(values, (axis_name, distance)))
        distance *= 2
    return values


def near_sum(values):
    values = yield from butterfly(values, "expert", 1, lax.axis_size("expert"))
    return (yield from butterfly(values, "dp", 1, 2))


def shared_rows(values):
    rings = mesh_rings()
    gathered = values
    for ring in rings[2:]:
        blocks = [gathered[None]]
        for _ in range(ring.size - 1):
            blocks.append((yield ring.hop(blocks[-1])))
        line = jnp.concatenate(blocks[::-1] + blocks[:0:-1], axis=0)
        gathered = lax.dynamic_slice_in_dim(line, ring.size - 1 - ring.place, ring.size, axis=0)
    parts, rows, width = values.shape
    return gathered.transpose(2, 1, 0, 3, 4).reshape(parts, -1, width)


class Streams:
    def __init__(self):
        self.under_way = {}
        self.done = {}
        self.started = set()
        self.blocks = []

    def _take(self, name, stages, value):
        try:
            self.under_way[name] = (stages, stages.send(value))
        except StopIteration as end:
            self.under_way.pop(name, None)
            self.done[name] = end.value

    def start(self, name, stages):
        self.started.add(name)
        self._take(name, stages, None)

    def advance(self, names, *anchors):
        names = [name for name in names if name in self.under_way]
        values = [self.under_way[name][1] for name in names]
        values, anchors = lax.optimization_barrier((values, anchors))
        for name, value in zip(names, values):
            self._take(name, self.under_way[name][0], value)
        return anchors[0] if len(anchors) == 1 else anchors

    def finish(self, names):
        while any(name in self.under_way for name in names):
            self.advance(names)


def part_rows(weight, start, rows):
    return lax.dynamic_slice_in_dim(weight, start, rows, axis=0)


def on_device(
    layer_input,
    segments,
    routes,
    cotangent,
    norm1_gain,
    in_weight,
    conv_weight,
    conv_bias,
    xproj_weight,
    dtproj_weight,
    dt_bias,
    a_log,
    skip_gain,
    out_weight,
    norm2_gain,
    router_weight,
    up_weight,
    down_weight,
):
    seq_len, model_width = layer_input.shape[2:]
    sequences = layer_input.shape[0] * layer_input.shape[1]
    tokens = sequences * seq_len
    expert_devices = lax.axis_size("expert")
    dp_devices = lax.axis_size("dp")
    devices = dp_devices * expert_devices
    assert up_weight.shape[0] == 1
    expert_count = expert_devices
    capacity = seq_len * 5 // (4 * expert_count)
    padded_capacity = -(-capacity // 16) * 16
    slots = sequences * padded_capacity
    taps = conv_weight.shape[0]
    rank = dtproj_weight.shape[0]
    states = a_log.shape[0]
    channels = skip_gain.shape[0]
    inner_width = channels * devices
    steps = dp_devices // 2
    expert_index = lax.axis_index("expert")
    small = jnp.concatenate(
        [
            xproj_weight,
            dtproj_weight.T,
            a_log.T,
            conv_weight.T,
            conv_bias[:, None],
            dt_bias[:, None],
            skip_gain[:, None],
        ],
        axis=1,
    )
    streams = Streams()

    def ring_blocks(block):
        ring = mesh_rings()[0]
        blocks = streams.blocks
        blocks.append(block)
        for _ in range(steps - 1):
            blocks.append((yield ring.hop(blocks[-1])))
        return blocks

    in_block = lax.dynamic_index_in_dim(
        in_weight.reshape(2, expert_devices, channels, model_width), expert_index, 1, keepdims=False
    ).reshape(2 * channels, model_width)
    streams.start("in", far_gather(in_block))
    streams.start("small", small_gather(small))
    for _ in range(steps - 1):
        streams.advance(("in", "small"))
    in_blocks = streams.done["in"].reshape(2, -1, model_width)
    with jax.named_scope("fetch_in"):
        in_cube = cube_gather(jnp.concatenate([in_blocks[0], in_blocks[1]], axis=1))
    expert_block = jnp.concatenate([up_weight[0], down_weight[0]], axis=0)
    expert_block = lax.optimization_barrier((expert_block, in_blocks))[0]
    streams.start("expert", ring_blocks(expert_block))
    for _ in range(3):
        streams.advance(("small",))
    out_block = part_rows(out_weight, expert_index * channels, channels)
    out_block = streams.advance(("small", "expert"), out_block)
    streams.start("out", far_and_pair(out_block))
    streams.finish(("small",))
    small_full = streams.done["small"]
    xproj_width = rank + 2 * states
    xproj_full = small_full[:, :xproj_width]
    across = small_full[:, xproj_width:].T
    dtproj_full = across[:rank]
    across = across[rank:].astype(jnp.float32)
    log_rates = across[:states]
    conv_full = across[states : states + taps]
    convb_full = across[states + taps]
    dtb_full = across[states + taps + 1]
    skip_full = across[states + taps + 2]
    conv_rows = jnp.concatenate(
        [
            conv_full,
            convb_full[None],
            skip_full[None],
            jnp.zeros((ROWS - taps - 2, inner_width), jnp.float32),
        ],
        axis=0,
    )
    segment_rows = segments.reshape(sequences, seq_len)
    masks = [same_document(segment_rows, offset)[:, :, None] for offset in range(taps)]
    mask_columns = jnp.concatenate([mask.reshape(tokens, 1) for mask in masks], axis=1)
    rate = -jnp.exp(log_rates)
    rate_two = rate * LOG2E
    route_rows = routes.reshape(sequences, seq_len)
    placed = dispatch_matrices(
        route_rows ^ expert_index.astype(jnp.int32), expert_count, capacity, padded_capacity
    )
    conv_rows, mask_columns, xproj_full, dtproj_full, rate_two, placed, dtb_full = streams.advance(
        ("out",), conv_rows, mask_columns, xproj_full, dtproj_full, rate_two, placed, dtb_full
    )
    streams.finish(("out",))
    with jax.named_scope("fetch_out"):
        out_full = cube_gather(streams.done["out"].reshape(-1, model_width))
    gain_one = norm1_gain.astype(jnp.float32)
    gain_two = norm2_gain.astype(jnp.float32)
    router_full = router_weight.astype(jnp.float32)

    def split(values):
        return values.reshape(sequences, seq_len, values.shape[-1])

    def flat(values):
        return values.reshape(tokens, values.shape[-1])

    rows_in = layer_input.reshape(tokens, model_width).astype(jnp.float32)
    cot_rows = cotangent.reshape(tokens, model_width).astype(jnp.float32)
    normed_one, norm_pull = jax.vjp(rms_scale, rows_in, gain_one)
    normed_low = normed_one.astype(LOW)
    inner, gate_in, conv_out, projected = run_conv_forward(
        normed_low, in_cube, mask_columns, conv_rows, xproj_full
    )
    gate_in, conv_out = split(gate_in), split(conv_out)
    dt_low = projected[:, :rank].astype(LOW)
    b_wide = jnp.broadcast_to(
        split(projected[:, rank : rank + states])[..., None], (sequences, seq_len, states, LANES)
    )
    c_wide = jnp.broadcast_to(
        split(projected[:, rank + states :])[..., None], (sequences, seq_len, states, LANES)
    )
    dt_sum = split(dot(dt_low, dtproj_full, ((1,), (0,)))) + dtb_full
    delta = jax.nn.softplus(dt_sum)
    decay = jnp.where(masks[1] > 0, delta, FAR)
    drive = delta * conv_out
    scanned = run_forward(decay, drive, b_wide, c_wide, rate_two)
    scanned = streams.advance(("expert",), scanned)
    mixed = scanned + skip_full * conv_out
    gate_silu = jax.nn.silu(gate_in)
    mixed_low = flat(mixed * gate_silu).astype(LOW)
    residual = rows_in + dot(mixed_low, out_full, ((1,), (0,)))

    chosen_rows = (
        route_rows.reshape(tokens, 1) == jnp.arange(expert_count, dtype=jnp.int32)[None]
    ).astype(jnp.float32)

    def route_piece(resid_value, gain_value, router_value):
        return norm_route(resid_value, gain_value, router_value, chosen_rows)

    (normed_two, gate_row), route_pull = jax.vjp(route_piece, residual, gain_two, router_full)
    sending = split(
        jnp.concatenate(
            [normed_two.astype(LOW), (cot_rows * gate_row[:, None]).astype(LOW)], axis=1
        )
    )

    def partners(cross, k):
        place = lambda d, e: d * expert_devices + e
        return [
            (place(d, e), place(d ^ cross, e ^ k))
            for d in range(dp_devices)
            for e in range(expert_devices)
        ]

    def exchange(piece, cross, k):
        if not cross and not k:
            return piece
        return lax.ppermute(piece, BOTH, partners(cross, k))

    pieces = [
        jnp.einsum("stk,std->skd", matrix, sending, preferred_element_type=jnp.float32).astype(LOW)
        for matrix in placed
    ]
    with jax.named_scope("send_rows"):
        received = [
            [exchange(pieces[k], cross, k).reshape(slots, -1) for k in range(expert_count)]
            for cross in (0, 1)
        ]

    units = up_weight.shape[1]
    while len(streams.blocks) < steps - 1:
        streams.advance(("expert",))
    early = streams.blocks[: steps - 1]
    own_rows, own_active, own_d_hidden, own_total = run_expert_first(received[0], early)
    cross_rows, cross_active, cross_d_hidden, cross_total = run_expert_first(received[1], early)
    own_total, cross_total = streams.advance(("expert",), own_total, cross_total)
    results, last_active, last_d_hidden = run_expert_last(
        expert_count,
        [own_rows, cross_rows],
        [own_total, cross_total],
        streams.done["expert"][steps - 1],
    )
    results = [
        [piece.reshape(sequences, padded_capacity, 2 * model_width) for piece in group]
        for group in results
    ]
    extent = own_rows.shape[0]
    kept = [
        (own_rows, own_active, own_d_hidden, last_active[:extent], last_d_hidden[:extent]),
        (cross_rows, cross_active, cross_d_hidden, last_active[extent:], last_d_hidden[extent:]),
    ]
    kept, results = lax.optimization_barrier((kept, results))
    with jax.named_scope("send_results"):
        arrived = [
            [exchange(results[cross][k], cross, k) for k in range(expert_count)]
            for cross in (0, 1)
        ]
    kept, arrived[0] = lax.optimization_barrier((kept, arrived[0]))
    up_terms = [0.0] * steps
    down_terms = [0.0] * steps
    for rows, active_rows, d_hidden_rows, last_active, last_d_hidden in kept:
        for k in range(steps):
            part = slice(k * units, (k + 1) * units)
            active_k = active_rows[:, part] if k < steps - 1 else last_active
            d_hidden_k = d_hidden_rows[:, part] if k < steps - 1 else last_d_hidden
            up_terms[k] = up_terms[k] + dot(d_hidden_k, rows[:, :model_width], ((0,), (0,)))
            down_terms[k] = down_terms[k] + dot(active_k, rows[:, model_width:], ((0,), (0,)))
    terms = [
        jnp.concatenate([up.astype(LOW), down.astype(LOW)], axis=0)
        for up, down in zip(up_terms, down_terms)
    ]
    terms, arrived[1] = lax.optimization_barrier((terms, arrived[1]))
    streams.start("expert_grad", ring_sum(terms))
    streams.advance(("expert_grad",))
    gathered_both = 0.0
    for k in range(expert_count):
        total = (arrived[0][k].astype(jnp.float32) + arrived[1][k].astype(jnp.float32)).astype(LOW)
        gathered_both = gathered_both + jnp.einsum(
            "stk,skd->std", placed[k], total, preferred_element_type=jnp.float32
        )
    gathered_both = flat(gathered_both)
    gathered = gathered_both[:, :model_width]
    d_sent = gathered_both[:, model_width:]
    layer_output = (residual + gate_row[:, None] * gathered).astype(LOW)


    d_gate = jnp.sum(cot_rows * gathered, axis=1)
    d_resid_norm, d_gain_two, d_router = route_pull((d_sent, d_gate))
    d_residual = cot_rows + d_resid_norm
    d_branch_low = d_residual.astype(LOW)

    out_gate_term, d_gate_low, d_scanned = run_gate_backward(
        d_branch_low, normed_low, out_full, mixed_low, flat(mixed), flat(gate_in)
    )
    with jax.named_scope("reduce_out_gate"):
        out_gate_blocks = cube_scatter(out_gate_term)
    d_scanned = split(d_scanned)
    d_scan, d_dt_low, d_dt_rows, more_rows, d_b, d_c = run_backward(
        decay,
        drive,
        b_wide,
        c_wide,
        rate_two,
        d_scanned,
        delta,
        conv_out,
        dt_sum,
        skip_full[None],
        dtproj_full,
    )
    d_scan = streams.advance(("expert_grad",), d_scan)
    streams.advance(("expert_grad",))
    d_dt_low = flat(d_dt_low)
    d_proj_low = jnp.concatenate(
        [
            flat(d_dt_rows),
            d_b[:, 0].reshape(tokens, states),
            d_c[:, 0].reshape(tokens, states),
        ],
        axis=1,
    ).astype(LOW)
    more_rows = jnp.sum(more_rows, axis=0)
    inner_term, d_normed = run_conv_backward(
        flat(d_scan),
        inner,
        d_gate_low,
        d_proj_low,
        normed_low,
        mask_columns,
        conv_rows,
        xproj_full,
        in_cube,
        d_dt_low,
        dt_low,
        more_rows,
    )
    inner_term, d_normed, out_gate_blocks = streams.advance(
        ("expert_grad",), inner_term, d_normed, out_gate_blocks
    )
    with jax.named_scope("reduce_inner"):
        inner_blocks = cube_scatter(inner_term)
    out_blocks = out_gate_blocks[:, :model_width]
    gate_blocks = out_gate_blocks[:, model_width:]
    streams.start(
        "out_grad", far_and_pair_sum(out_blocks.reshape(-1, 2, channels, model_width))
    )
    d_rows_norm, d_gain_one = norm_pull(d_normed)
    input_grad = d_residual + d_rows_norm

    gains = jnp.concatenate([d_gain_one[None], d_gain_two[None], d_router.T], axis=0)
    streams.start("gains", near_sum(gains))
    streams.advance(("out_grad",))
    streams.finish(("out_grad",))
    out_part = streams.advance(("expert_grad",), streams.done["out_grad"])
    streams.finish(("gains",))
    gains = streams.done["gains"]
    inner_blocks = streams.advance(("expert_grad",), inner_blocks)
    half = (steps // 2, 2, channels, model_width)
    streams.start(
        "in_grad",
        far_sum(inner_blocks[:, :model_width].reshape(half), gate_blocks.reshape(half)),
    )
    small_blocks = inner_blocks[:, model_width:]
    streams.start(
        "small_grad",
        far_and_pair_sum(small_blocks.reshape(-1, 2, channels, small_blocks.shape[1])),
    )
    streams.advance(("small_grad",))
    streams.start("out_rows", shared_rows(out_part[None]))
    gains = streams.advance(("in_grad",), gains)
    streams.start("in_rows", shared_rows(streams.done["in_grad"]))
    streams.start("gains", butterfly(gains, "dp", 2, dp_devices))
    streams.advance(("in_rows", "out_rows", "gains"))
    streams.finish(("in_rows", "out_rows", "gains", "small_grad", "expert_grad"))
    gains = streams.done["gains"]
    in_grad = streams.done["in_rows"].reshape(in_weight.shape).astype(jnp.float32)
    out_grad = streams.done["out_rows"][0].astype(jnp.float32)
    expert_grad = streams.done["expert_grad"].astype(jnp.float32)
    up_grad, down_grad = expert_grad[:units], expert_grad[units:]
    small_grad = streams.done["small_grad"].astype(jnp.float32)
    xproj_grad = small_grad[:, :xproj_width]
    row_grads = small_grad[:, xproj_width:].T
    dtproj_grad = row_grads[:rank]
    row_grads = row_grads[rank:]
    conv_grad = row_grads[:taps]
    convb_grad = row_grads[taps]
    alog_grad = row_grads[ROWS : ROWS + states]
    dtb_grad, skip_grad = row_grads[ROWS + states], row_grads[ROWS + states + 1]

    return (
        layer_output.reshape(layer_input.shape),
        input_grad.reshape(layer_input.shape),
        gains[0],
        in_grad,
        conv_grad,
        convb_grad,
        xproj_grad,
        dtproj_grad,
        dtb_grad,
        alog_grad,
        skip_grad,
        out_grad,
        gains[1],
        gains[2:].T,
        up_grad[None],
        down_grad[None],
    )


def solution(mesh):
    placed = (
        P(None, ("dp", "expert"), None, None),
        P(None, ("dp", "expert"), None),
        P(None, ("dp", "expert"), None, None),
        P(None, ("dp", "expert"), None, None),
        P(),
        P("dp", None),
        P(None, ("dp", "expert")),
        P(("dp", "expert")),
        P(("dp", "expert"), None),
        P(None, ("dp", "expert")),
        P(("dp", "expert")),
        P(None, ("dp", "expert")),
        P(("dp", "expert")),
        P("dp", None),
        P(),
        P(),
        P("expert", "dp", None),
        P("expert", "dp", None),
    )
    return jax.shard_map(
        on_device,
        mesh=mesh,
        in_specs=placed,
        out_specs=(
            P(None, ("dp", "expert"), None, None),
            P(None, ("dp", "expert"), None, None),
            P(),
            P("dp", None),
            P(None, ("dp", "expert")),
            P(("dp", "expert")),
            P(("dp", "expert"), None),
            P(None, ("dp", "expert")),
            P(("dp", "expert")),
            P(None, ("dp", "expert")),
            P(("dp", "expert")),
            P("dp", None),
            P(),
            P(),
            P("expert", "dp", None),
            P("expert", "dp", None),
        ),
        check_vma=False,
    )
```

```python
import functools

import jax
import jax.numpy as jnp
from jax import lax
from jax.experimental import pallas as pl
from jax.experimental.pallas import tpu as pltpu
from jax.sharding import PartitionSpec as P

LANES = 128
VMEM_GRANT = 32 << 20
ROWS = 8

def wide(tile, width):
    return jnp.concatenate([tile] * (width // LANES), axis=1)

def narrow(values):
    total = values[:, :LANES]
    for start in range(LANES, values.shape[1], LANES):
        total = total + values[:, start : start + LANES]
    return total

def fold_states(pieces, position):
    folded = []
    for piece in pieces:
        total = piece[:ROWS]
        for start in range(ROWS, piece.shape[0], ROWS):
            total = total + piece[start : start + ROWS]
        folded.append(total)
    low = (position & 4) == 0
    folded = [
        jnp.where(low, a, b) + pltpu.roll(jnp.where(low, b, a), 4, 0)
        for a, b in zip(folded[:4], folded[4:])
    ]
    for step in (2, 1):
        low = (position & step) == 0
        half = len(folded) // 2
        folded = [
            jnp.where(low, a + pltpu.roll(a, ROWS - step, 0), b + pltpu.roll(b, step, 0))
            for a, b in zip(folded[:half], folded[half:])
        ]
    return folded[0]

def scan_forward(decay_ref, drive_ref, b_ref, c_ref, rate_ref, out_ref):
    length, width = decay_ref.shape[1:]
    rate = rate_ref[...]
    position = lax.broadcasted_iota(jnp.int32, (ROWS, width), 0)

    def block(index, state):
        start = pl.multiple_of(index * ROWS, ROWS)
        pieces = []
        for offset in range(ROWS):
            t = start + offset
            factor = jnp.exp2(decay_ref[0, pl.ds(t, 1), :] * rate)
            state = factor * state + drive_ref[0, pl.ds(t, 1), :] * wide(b_ref[0, t], width)
            pieces.append(state * wide(c_ref[0, t], width))
        out_ref[0, pl.ds(start, ROWS), :] = fold_states(pieces, position)
        return state

    lax.fori_loop(0, length // ROWS, block, jnp.zeros_like(rate))

def scan_backward(
    decay_ref, drive_ref, b_ref, c_ref, rate_ref, dout_ref, delta_ref, conv_out_ref, dt_sum_ref,
    skip_ref, dtproj_ref,
    d_conv_ref, d_dt_ref, d_low_ref, rows_ref, db_sum_ref, dc_sum_ref,
    db_ref, dc_ref, state_ref, factor_ref, ddrive_ref, ddecay_ref,
):
    length, width = decay_ref.shape[1:]
    rate = rate_ref[...]
    position = lax.broadcasted_iota(jnp.int32, (ROWS, width), 0)

    @pl.when(pl.program_id(1) == 0)
    def _():
        db_ref[...] = jnp.zeros_like(db_ref)
        dc_ref[...] = jnp.zeros_like(dc_ref)

    state_ref[0] = jnp.zeros_like(rate)

    def replay(index, state):
        start = pl.multiple_of(index * ROWS, ROWS)
        for offset in range(ROWS):
            t = start + offset
            factor = jnp.exp2(decay_ref[0, pl.ds(t, 1), :] * rate)
            state = factor * state + drive_ref[0, pl.ds(t, 1), :] * wide(b_ref[0, t], width)
            factor_ref[t] = factor
            state_ref[t + 1] = state
        return state

    lax.fori_loop(0, length // ROWS, replay, jnp.zeros_like(rate))

    def block(index, carried):
        later, drate = carried
        start = pl.multiple_of(length - ROWS - index * ROWS, ROWS)
        drive_pieces = [None] * ROWS
        decay_pieces = [None] * ROWS
        for offset in reversed(range(ROWS)):
            t = start + offset
            dout = dout_ref[0, pl.ds(t, 1), :]
            dstate = later + dout * wide(c_ref[0, t], width)
            dc_ref[t] += narrow(dout * state_ref[t + 1])
            db_ref[t] += narrow(dstate * drive_ref[0, pl.ds(t, 1), :])
            drive_pieces[offset] = dstate * wide(b_ref[0, t], width)
            later = dstate * factor_ref[t]
            power = later * state_ref[t]
            decay_pieces[offset] = power * rate
            drate = drate + power * decay_ref[0, pl.ds(t, 1), :]
        ddrive_ref[pl.ds(start, ROWS), :] = fold_states(drive_pieces, position)
        ddecay_ref[pl.ds(start, ROWS), :] = fold_states(decay_pieces, position)
        return later, drate

    zero = jnp.zeros_like(rate)
    drate = lax.fori_loop(0, length // ROWS, block, (zero, zero))[1]
    states = rate.shape[0]
    ddrive = ddrive_ref[...]
    dout = dout_ref[0]
    conv_out = conv_out_ref[0]
    d_conv_ref[0] = ddrive * delta_ref[0] + dout * skip_ref[...]
    d_delta = ddecay_ref[...] * (1.0 / LOG2E) + ddrive * conv_out
    d_dt = d_delta * jax.nn.sigmoid(dt_sum_ref[0])
    d_dt_low = d_dt.astype(jnp.bfloat16)
    d_dt_ref[0] = d_dt_low
    rows_ref[0, :states, :] = drate * rate * (1.0 / LOG2E)
    rows_ref[0, states:, :] = jnp.concatenate(
        [
            jnp.sum(d_dt, axis=0, keepdims=True),
            jnp.sum(dout * conv_out, axis=0, keepdims=True),
            jnp.zeros((rows_ref.shape[1] - states - 2, width), jnp.float32),
        ],
        axis=0,
    )
    d_low = product(d_dt_low, dtproj_ref[...], ((1,), (1,)))

    @pl.when(pl.program_id(1) == 0)
    def _():
        d_low_ref[0] = d_low

    @pl.when(pl.program_id(1) > 0)
    def _():
        d_low_ref[0] += d_low

    @pl.when(pl.program_id(1) == pl.num_programs(1) - 1)
    def _():
        ones = jnp.ones((ROWS, LANES), jnp.float32)
        for total_ref, sum_ref in ((db_ref, db_sum_ref), (dc_ref, dc_sum_ref)):
            sum_ref[0] = lax.dot_general(
                ones,
                total_ref[...].reshape(-1, LANES),
                (((1,), (1,)), ((), ())),
                precision=lax.Precision.HIGHEST,
                preferred_element_type=jnp.float32,
            )

def tile_width(width):
    for tiles in (3, 2, 1):
        if width % (tiles * LANES) == 0:
            return tiles * LANES
    return width

def scan_specs(length, states, width):
    tokens = pl.BlockSpec((1, length, width), lambda s, c: (s, 0, c))
    maps = pl.BlockSpec((1, length, states, LANES), lambda s, c: (s, 0, 0, 0))
    rates = pl.BlockSpec((states, width), lambda s, c: (0, c))
    return tokens, maps, rates

def run_forward(decay, drive, b_wide, c_wide, rate):
    count, length, channels = decay.shape
    states = rate.shape[0]
    width = tile_width(channels)
    tokens, maps, rates = scan_specs(length, states, width)
    return pl.pallas_call(
        scan_forward,
        grid=(count, channels // width),
        in_specs=[tokens, tokens, maps, maps, rates],
        out_specs=tokens,
        out_shape=jax.ShapeDtypeStruct(decay.shape, jnp.float32),
        cost_estimate=pl.CostEstimate(
            flops=decay.size, transcendentals=0,
            bytes_accessed=4 * (3 * decay.size + 2 * b_wide.size)),
        compiler_params=pltpu.CompilerParams(vmem_limit_bytes=VMEM_GRANT),
        name="scan_forward",
    )(decay, drive, b_wide, c_wide, rate)

def run_backward(
    decay, drive, b_wide, c_wide, rate, dout, delta, conv_out, dt_sum, skip, dtproj
):
    count, length, channels = decay.shape
    states = rate.shape[0]
    rank = dtproj.shape[0]
    width = tile_width(channels)
    extra = states + ROWS
    tokens, maps, rates = scan_specs(length, states, width)
    summed = jax.ShapeDtypeStruct((count, ROWS, length * states), jnp.float32)
    sums = pl.BlockSpec((1, ROWS, length * states), lambda s, c: (s, 0, 0))
    return pl.pallas_call(
        scan_backward,
        grid=(count, channels // width),
        in_specs=[tokens, tokens, maps, maps, rates, tokens, tokens, tokens, tokens]
        + [
            pl.BlockSpec((1, width), lambda s, c: (0, c)),
            pl.BlockSpec((rank, width), lambda s, c: (0, c)),
        ],
        out_specs=[
            tokens,
            tokens,
            pl.BlockSpec((1, length, rank), lambda s, c: (s, 0, 0)),
            pl.BlockSpec((1, extra, width), lambda s, c: (s, 0, c)),
            sums,
            sums,
        ],
        out_shape=[
            jax.ShapeDtypeStruct(decay.shape, jnp.float32),
            jax.ShapeDtypeStruct(decay.shape, jnp.bfloat16),
            jax.ShapeDtypeStruct((count, length, rank), jnp.float32),
            jax.ShapeDtypeStruct((count, extra, channels), jnp.float32),
            summed,
            summed,
        ],
        scratch_shapes=[
            pltpu.VMEM((length, states, LANES), jnp.float32),
            pltpu.VMEM((length, states, LANES), jnp.float32),
            pltpu.VMEM((length + 1, states, width), jnp.float32),
            pltpu.VMEM((length, states, width), jnp.float32),
            pltpu.VMEM((length, width), jnp.float32),
            pltpu.VMEM((length, width), jnp.float32),
        ],
        cost_estimate=pl.CostEstimate(
            flops=decay.size, transcendentals=0, bytes_accessed=decay.size
        ),
        compiler_params=pltpu.CompilerParams(vmem_limit_bytes=60 << 20),
        name="scan_backward",
    )(decay, drive, b_wide, c_wide, rate, dout, delta, conv_out, dt_sum, skip, dtproj)


def product(left, right, contract):
    return lax.dot_general(left, right, (contract, ((), ())), preferred_element_type=jnp.float32)


def conv_forward(
    normed_ref, in_ref, masks_ref, conv_ref, xproj_ref, inner_ref, gate_ref, conv_out_ref, maps_ref
):
    taps = masks_ref.shape[1]
    model = normed_ref.shape[1]
    inner = product(normed_ref[...], in_ref[:, :model], ((1,), (1,)))
    inner_ref[...] = inner
    gate_ref[...] = product(normed_ref[...], in_ref[:, model:], ((1,), (1,)))
    total = conv_ref[taps : taps + 1] + conv_ref[taps - 1 : taps] * inner
    for offset in range(1, taps):
        total = total + conv_ref[taps - 1 - offset : taps - offset] * (
            pltpu.roll(inner, offset, 0) * masks_ref[:, offset : offset + 1]
        )
    conv_out = total * jax.nn.sigmoid(total)
    conv_out_ref[...] = conv_out
    maps = product(conv_out.astype(jnp.bfloat16), xproj_ref[...], ((1,), (0,)))

    @pl.when(pl.program_id(0) == 0)
    def _():
        maps_ref[...] = maps

    @pl.when(pl.program_id(0) > 0)
    def _():
        maps_ref[...] += maps


def run_conv_forward(normed, in_rows, masks, conv_rows, xproj):
    count, model = normed.shape
    channels = in_rows.shape[0]
    width = tile_width(channels)
    tokens = pl.BlockSpec((count, width), lambda c: (0, c))
    full = jax.ShapeDtypeStruct((count, channels), jnp.float32)

    def whole(values):
        return pl.BlockSpec(values.shape, lambda c: (0, 0))

    def rows(values):
        return pl.BlockSpec((width, values.shape[1]), lambda c: (c, 0))

    return pl.pallas_call(
        conv_forward,
        grid=(channels // width,),
        in_specs=[
            whole(normed),
            rows(in_rows),
            whole(masks),
            pl.BlockSpec((ROWS, width), lambda c: (0, c)),
            rows(xproj),
        ],
        out_specs=[
            tokens,
            tokens,
            tokens,
            pl.BlockSpec((count, xproj.shape[1]), lambda c: (0, 0)),
        ],
        out_shape=[full, full, full, jax.ShapeDtypeStruct((count, xproj.shape[1]), jnp.float32)],
        cost_estimate=pl.CostEstimate(flops=count, transcendentals=0, bytes_accessed=count),
        compiler_params=pltpu.CompilerParams(vmem_limit_bytes=VMEM_GRANT),
        name="conv_forward",
    )(normed, in_rows, masks, conv_rows, xproj)


def gate_backward(
    d_branch_ref, normed_ref, out_ref, mixed_low_ref, mixed_ref, gate_ref,
    term_ref, d_gate_ref, d_scanned_ref,
):
    model = d_branch_ref.shape[1]
    d_branch = d_branch_ref[...]
    d_mixed = product(d_branch, out_ref[...], ((1,), (1,)))
    gate = gate_ref[...]
    chance = jax.nn.sigmoid(gate)
    d_gate = d_mixed * mixed_ref[...] * (chance * (1.0 + gate * (1.0 - chance)))
    d_gate = d_gate.astype(jnp.bfloat16)
    d_gate_ref[...] = d_gate
    d_scanned_ref[...] = d_mixed * gate * chance
    term_ref[:, :model] = product(mixed_low_ref[...], d_branch, ((0,), (0,))).astype(jnp.bfloat16)
    term_ref[:, model:] = product(d_gate, normed_ref[...], ((0,), (0,))).astype(jnp.bfloat16)


def run_gate_backward(d_branch, normed, out_rows, mixed_low, mixed, gate):
    count, model = d_branch.shape
    channels = mixed.shape[1]
    width = tile_width(channels)
    whole = pl.BlockSpec((count, model), lambda c: (0, 0))
    rows = pl.BlockSpec((width, model), lambda c: (c, 0))
    tokens = pl.BlockSpec((count, width), lambda c: (0, c))
    return pl.pallas_call(
        gate_backward,
        grid=(channels // width,),
        in_specs=[whole, whole, rows, tokens, tokens, tokens],
        out_specs=[pl.BlockSpec((width, 2 * model), lambda c: (c, 0)), tokens, tokens],
        out_shape=[
            jax.ShapeDtypeStruct((channels, 2 * model), jnp.bfloat16),
            jax.ShapeDtypeStruct((count, channels), jnp.bfloat16),
            jax.ShapeDtypeStruct((count, channels), jnp.float32),
        ],
        cost_estimate=pl.CostEstimate(flops=count, transcendentals=0, bytes_accessed=count),
        compiler_params=pltpu.CompilerParams(vmem_limit_bytes=VMEM_GRANT),
        name="gate_backward",
    )(d_branch, normed, out_rows, mixed_low, mixed, gate)


def conv_backward(
    d_scan_ref, inner_ref, d_gate_ref, d_proj_ref, normed_ref,
    masks_ref, conv_ref, xproj_ref, in_ref, d_dt_ref, dt_ref, rows_ref,
    term_ref, d_normed_ref,
):
    taps = masks_ref.shape[1]
    model = normed_ref.shape[1]
    count = inner_ref.shape[0]
    d_conv = d_scan_ref[...] + product(d_proj_ref[...], xproj_ref[...], ((1,), (1,)))
    inner = inner_ref[...]
    shifted = [inner] + [pltpu.roll(inner, offset, 0) for offset in range(1, taps)]
    masked = [shifted[offset] * masks_ref[:, offset : offset + 1] for offset in range(taps)]
    total = conv_ref[taps : taps + 1]
    for offset in range(taps):
        total = total + conv_ref[taps - 1 - offset : taps - offset] * masked[offset]
    chance = jax.nn.sigmoid(total)
    d_sum = d_conv * (chance * (1.0 + total * (1.0 - chance)))
    d_inner = jnp.zeros_like(inner)
    rows = []
    for offset in range(taps):
        rows.append(jnp.sum(d_sum * masked[offset], axis=0, keepdims=True))
        back = d_sum * masks_ref[:, offset : offset + 1]
        if offset:
            back = pltpu.roll(back, count - offset, 0)
        d_inner = d_inner + conv_ref[taps - 1 - offset : taps - offset] * back
    rows = rows[::-1] + [jnp.sum(d_sum, axis=0, keepdims=True)]
    rows = jnp.concatenate(
        rows + [jnp.zeros_like(rows[0])] * (ROWS - len(rows)) + [rows_ref[...]], axis=0
    ).astype(jnp.bfloat16)
    extent = rows.shape[0]
    same = lax.broadcasted_iota(jnp.int32, (extent, extent), 0) == lax.broadcasted_iota(
        jnp.int32, (extent, extent), 1
    )
    columns = product(rows, same.astype(jnp.bfloat16), ((0,), (0,)))
    conv_low = (total * chance).astype(jnp.bfloat16)
    edge = model + d_proj_ref.shape[1]
    middle = edge + dt_ref.shape[1]
    term_ref[:, model:edge] = product(conv_low, d_proj_ref[...], ((0,), (0,))).astype(jnp.bfloat16)
    term_ref[:, edge:middle] = product(d_dt_ref[...], dt_ref[...], ((0,), (0,))).astype(
        jnp.bfloat16
    )
    term_ref[:, middle:] = columns.astype(jnp.bfloat16)
    d_inner = d_inner.astype(jnp.bfloat16)
    term_ref[:, :model] = product(d_inner, normed_ref[...], ((0,), (0,))).astype(jnp.bfloat16)
    d_normed = product(d_inner, in_ref[:, :model], ((1,), (0,))) + product(
        d_gate_ref[...], in_ref[:, model:], ((1,), (0,))
    )

    @pl.when(pl.program_id(0) == 0)
    def _():
        d_normed_ref[...] = d_normed

    @pl.when(pl.program_id(0) > 0)
    def _():
        d_normed_ref[...] += d_normed


def run_conv_backward(
    d_scan,
    inner,
    d_gate,
    d_proj,
    normed,
    masks,
    conv_rows,
    xproj,
    in_rows,
    d_dt,
    dt,
    more_rows,
):
    count, channels = inner.shape
    model = normed.shape[1]
    width = tile_width(channels)
    tokens = pl.BlockSpec((count, width), lambda c: (0, c))
    small_width = d_proj.shape[1] + dt.shape[1] + ROWS + more_rows.shape[0]

    def whole(values):
        return pl.BlockSpec(values.shape, lambda c: (0, 0))

    def rows(values):
        return pl.BlockSpec((width, values.shape[1]), lambda c: (c, 0))

    return pl.pallas_call(
        conv_backward,
        grid=(channels // width,),
        in_specs=[
            tokens,
            tokens,
            tokens,
            whole(d_proj),
            whole(normed),
            whole(masks),
            pl.BlockSpec((ROWS, width), lambda c: (0, c)),
            rows(xproj),
            rows(in_rows),
            tokens,
            whole(dt),
            pl.BlockSpec((more_rows.shape[0], width), lambda c: (0, c)),
        ],
        out_specs=[
            pl.BlockSpec((width, model + small_width), lambda c: (c, 0)),
            pl.BlockSpec((count, model), lambda c: (0, 0)),
        ],
        out_shape=[
            jax.ShapeDtypeStruct((channels, model + small_width), jnp.bfloat16),
            jax.ShapeDtypeStruct((count, model), jnp.float32),
        ],
        cost_estimate=pl.CostEstimate(flops=count, transcendentals=0, bytes_accessed=count),
        compiler_params=pltpu.CompilerParams(vmem_limit_bytes=VMEM_GRANT),
        name="conv_backward",
    )(
        d_scan,
        inner,
        d_gate,
        d_proj,
        normed,
        masks,
        conv_rows,
        xproj,
        in_rows,
        d_dt,
        dt,
        more_rows,
    )


GELU_SCALE = 0.7978845608028654
GELU_CUBE = 0.044715


def expert_units(slot_rows, d_returned, up, down):
    hidden = product(slot_rows, up, ((1,), (1,)))
    square = hidden * hidden
    bend = jnp.tanh(GELU_SCALE * (hidden + GELU_CUBE * (square * hidden)))
    share = 0.5 * (1.0 + bend)
    active = (hidden * share).astype(jnp.bfloat16)
    slope = share + hidden * (0.5 * GELU_SCALE) * (1.0 - bend * bend) * (
        1.0 + 3.0 * GELU_CUBE * square
    )
    d_active = product(d_returned, down, ((1,), (1,)))
    d_hidden = (d_active * slope).astype(jnp.bfloat16)
    returned = product(active, down, ((1,), (0,)))
    d_slots = product(d_hidden, up, ((1,), (0,)))
    return active, d_hidden, returned, d_slots


def expert_first(pieces, blocks, *refs):
    piece_refs, block_refs = refs[:pieces], refs[pieces : pieces + blocks]
    rows_ref, active_ref, d_hidden_ref, total_ref, held_ref, sems = refs[pieces + blocks :]
    copies = [
        pltpu.make_async_copy(block_refs[k], held_ref.at[k], sems.at[k]) for k in range(blocks)
    ]
    for copy in copies:
        copy.start()
    length = piece_refs[0].shape[0]
    for n in range(pieces):
        rows_ref[n * length : (n + 1) * length, :] = piece_refs[n][...]
    model = rows_ref.shape[1] // 2
    units = held_ref.shape[1] // 2
    slot_rows, d_returned = rows_ref[:, :model], rows_ref[:, model:]
    for k in range(blocks):
        copies[k].wait()
        active, d_hidden, returned, d_slots = expert_units(
            slot_rows, d_returned, held_ref[k, :units, :], held_ref[k, units:, :]
        )
        active_ref[:, k * units : (k + 1) * units] = active
        d_hidden_ref[:, k * units : (k + 1) * units] = d_hidden
        if k:
            returned = returned + total_ref[:, :model]
            d_slots = d_slots + total_ref[:, model:]
        total_ref[:, :model] = returned
        total_ref[:, model:] = d_slots


def run_expert_first(pieces, blocks):
    length, width = pieces[0].shape
    rows = length * len(pieces)
    units = blocks[0].shape[0] // 2
    low = jnp.bfloat16
    vmem = pl.BlockSpec(memory_space=pltpu.VMEM)
    return pl.pallas_call(
        functools.partial(expert_first, len(pieces), len(blocks)),
        in_specs=[vmem] * len(pieces) + [pl.BlockSpec(memory_space=pl.ANY)] * len(blocks),
        out_specs=[vmem] * 4,
        out_shape=[
            jax.ShapeDtypeStruct((rows, width), low),
            jax.ShapeDtypeStruct((rows, units * len(blocks)), low),
            jax.ShapeDtypeStruct((rows, units * len(blocks)), low),
            jax.ShapeDtypeStruct((rows, width), jnp.float32),
        ],
        scratch_shapes=[
            pltpu.VMEM((len(blocks),) + blocks[0].shape, low),
            pltpu.SemaphoreType.DMA((len(blocks),)),
        ],
        cost_estimate=pl.CostEstimate(flops=rows, transcendentals=0, bytes_accessed=rows),
        compiler_params=pltpu.CompilerParams(vmem_limit_bytes=VMEM_GRANT),
        name="expert_first",
    )(*pieces, *blocks)


def expert_last(pieces, rows_refs, total_refs, block_ref, result_refs, active_ref, d_hidden_ref):
    model = rows_refs[0].shape[1] // 2
    units = block_ref.shape[0] // 2
    extent = rows_refs[0].shape[0]
    length = extent // pieces
    for n in range(2):
        active, d_hidden, returned, d_slots = expert_units(
            rows_refs[n][:, :model],
            rows_refs[n][:, model:],
            block_ref[:units, :],
            block_ref[units:, :],
        )
        active_ref[n * extent : (n + 1) * extent, :] = active
        d_hidden_ref[n * extent : (n + 1) * extent, :] = d_hidden
        returned = (returned + total_refs[n][:, :model]).astype(jnp.bfloat16)
        d_slots = (d_slots + total_refs[n][:, model:]).astype(jnp.bfloat16)
        for m in range(pieces):
            part = slice(m * length, (m + 1) * length)
            result_refs[n * pieces + m][:, :model] = returned[part]
            result_refs[n * pieces + m][:, model:] = d_slots[part]


def run_expert_last(pieces, rows, totals, block):
    extent, width = rows[0].shape
    units = block.shape[0] // 2
    low = jnp.bfloat16
    vmem = pl.BlockSpec(memory_space=pltpu.VMEM)

    def kernel(*refs):
        expert_last(pieces, refs[:2], refs[2:4], refs[4], refs[5:-2], refs[-2], refs[-1])

    out = pl.pallas_call(
        kernel,
        in_specs=[vmem] * 5,
        out_specs=[vmem] * (2 * pieces + 2),
        out_shape=[jax.ShapeDtypeStruct((extent // pieces, width), low)] * (2 * pieces)
        + [jax.ShapeDtypeStruct((2 * extent, units), low)] * 2,
        cost_estimate=pl.CostEstimate(flops=extent, transcendentals=0, bytes_accessed=extent),
        compiler_params=pltpu.CompilerParams(vmem_limit_bytes=VMEM_GRANT),
        name="expert_last",
    )(*rows, *totals, block)
    return [out[:pieces], out[pieces:-2]], out[-2], out[-1]


HIGHEST = lax.Precision.HIGHEST
EPSILON = 1e-05
LOG2E = 1.4426950408889634
FAR = 1e30
LOW = jnp.bfloat16
BOTH = ("dp", "expert")


def dot(left, right, contract):
    return lax.dot_general(left, right, (contract, ((), ())), preferred_element_type=jnp.float32)


def rms_scale(values, gain_row):
    return (
        values * lax.rsqrt(jnp.mean(values * values, axis=-1, keepdims=True) + EPSILON) * gain_row
    )


def norm_route(residual, gain_two, router_full, chosen_rows):
    normed_two = rms_scale(residual, gain_two)
    logits = jnp.dot(normed_two, router_full, precision=HIGHEST, preferred_element_type=jnp.float32)
    probabilities = jax.nn.softmax(logits, axis=-1)
    return (normed_two, jnp.sum(probabilities * chosen_rows, axis=1))


def same_document(segments, offset):
    if offset == 0:
        return jnp.ones(segments.shape, jnp.float32)
    padded = jnp.pad(segments, ((0, 0), (offset, 0)), constant_values=-1)
    return (padded[:, : segments.shape[1]] == segments).astype(jnp.float32)


def dispatch_matrices(order_rows, expert_count, capacity, padded_capacity):
    length = order_rows.shape[1]
    chosen = (
        order_rows[:, :, None] == jnp.arange(expert_count, dtype=jnp.int32)[None, None]
    ).astype(jnp.float32)
    before = jnp.tril(jnp.ones((length, length), jnp.float32), -1)
    earlier = jnp.einsum("tu,sue->ste", before, chosen, preferred_element_type=jnp.float32)
    slot = jnp.sum(earlier * chosen, axis=2).astype(jnp.int32)
    places = jnp.arange(padded_capacity, dtype=jnp.int32)
    taken = ((slot[:, :, None] == places) & (places < capacity)).astype(jnp.float32)
    return [(chosen[:, :, k, None] * taken).astype(LOW) for k in range(expert_count)]


def hop(values, step):
    axis_name, distance = step
    size = lax.axis_size(axis_name)
    return lax.ppermute(values, axis_name, [(i, i ^ distance) for i in range(size)])


class Ring:
    def __init__(self, axis_name, stride, size):
        self.axis_name = axis_name
        self.stride = stride
        self.size = size
        self.place = lax.axis_index(axis_name) // stride % size

    def hop(self, values, distance=1):
        pairs = []
        for i in range(lax.axis_size(self.axis_name)):
            place = i // self.stride % self.size
            pairs.append((i, i + ((place + distance) % self.size - place) * self.stride))
        return lax.ppermute(values, self.axis_name, pairs)


def mesh_rings():
    dp_size, expert_size = lax.axis_size("dp"), lax.axis_size("expert")
    return [
        Ring("dp", 2, dp_size // 2),
        Ring("dp", 1, 2),
        Ring("expert", 2, expert_size // 2),
        Ring("expert", 1, 2),
    ]


def cubes():
    expert_size = lax.axis_size("expert")
    wide = 2 * expert_size
    return [
        [place * wide + i for i in range(wide)] for place in range(lax.axis_size("dp") // 2)
    ]


def far_gather(block):
    ring = mesh_rings()[0]
    blocks = [block[None]]
    for _ in range(ring.size - 1):
        blocks.append((yield ring.hop(blocks[-1])))
    line = jnp.concatenate(blocks[::-1] + blocks[:0:-1], axis=0)
    return lax.dynamic_slice_in_dim(line, ring.size - 1 - ring.place, ring.size, axis=0)


def cube_gather(block):
    return lax.all_gather(block, BOTH, axis=0, tiled=True, axis_index_groups=cubes())


def cube_scatter(total):
    return lax.psum_scatter(
        total, BOTH, scatter_dimension=0, tiled=True, axis_index_groups=cubes()
    )


def block_of(values, place, axis):
    return lax.dynamic_index_in_dim(values, place, axis, keepdims=True)


def far_and_pair(block):
    pair = mesh_rings()[1]
    blocks = yield from far_gather(block)
    blocks = blocks.reshape((-1, 2) + block.shape)
    moved = yield pair.hop(block_of(blocks, 1 - pair.place, 1))
    kept = block_of(blocks, pair.place, 1)
    return jnp.where(
        pair.place == 0,
        jnp.concatenate([kept, moved], axis=1),
        jnp.concatenate([moved, kept], axis=1),
    )


def far_and_pair_sum(blocks):
    pair = mesh_rings()[1]
    moved = yield pair.hop(block_of(blocks, 1 - pair.place, 1))
    kept = block_of(blocks, pair.place, 1)
    values = jnp.where(
        pair.place == 0,
        jnp.concatenate([kept, moved], axis=1),
        jnp.concatenate([moved, kept], axis=1),
    )
    values = values.reshape((-1,) + blocks.shape[2:])
    return (yield from far_sum(values))


def cube_stages_gather(block):
    for ring in mesh_rings()[:0:-1]:
        blocks = [block[None]]
        for _ in range(ring.size - 1):
            blocks.append((yield ring.hop(blocks[-1])))
        line = jnp.concatenate(blocks[::-1] + blocks[:0:-1], axis=0)
        block = lax.dynamic_slice_in_dim(line, ring.size - 1 - ring.place, ring.size, axis=0)
        block = block.reshape((-1,) + block.shape[2:])
    return block


def small_gather(block):
    block = yield from far_and_pair(block)
    return (yield from cube_stages_gather(block.reshape(-1, block.shape[-1])))


def add_low(kept, moved):
    return (kept.astype(jnp.float32) + moved.astype(jnp.float32)).astype(LOW)


def far_sum(blocks, more=None):
    ring = mesh_rings()[0]

    def block(distance):
        place = (ring.place + distance) % ring.size
        if more is None:
            return block_of(blocks, place, 0)[0]
        middle = ring.size // 2
        return jnp.where(
            place < middle,
            block_of(blocks, place % middle, 0)[0],
            block_of(more, place % middle, 0)[0],
        )

    moved = yield tuple(ring.hop(block(distance), distance) for distance in range(1, ring.size))
    total = block(0).astype(jnp.float32)
    for part in moved:
        total = total + part.astype(jnp.float32)
    return total.astype(LOW)


def ring_sum(blocks):
    ring = mesh_rings()[0]
    count = len(blocks)
    travelling = blocks[1 % count]
    for step in range(2, count + 1):
        travelling = yield travelling.astype(LOW)
        moved = yield ring.hop(travelling)
        travelling = blocks[step % count].astype(jnp.float32) + moved.astype(jnp.float32)
    return travelling


def butterfly(values, axis_name, first, last):
    distance = first
    while distance < last:
        values = values + (yield hop(values, (axis_name, distance)))
        distance *= 2
    return values


def near_sum(values):
    values = yield from butterfly(values, "expert", 1, lax.axis_size("expert"))
    return (yield from butterfly(values, "dp", 1, 2))


def shared_rows(values):
    rings = mesh_rings()
    gathered = values
    for ring in rings[2:]:
        blocks = [gathered[None]]
        for _ in range(ring.size - 1):
            blocks.append((yield ring.hop(blocks[-1])))
        line = jnp.concatenate(blocks[::-1] + blocks[:0:-1], axis=0)
        gathered = lax.dynamic_slice_in_dim(line, ring.size - 1 - ring.place, ring.size, axis=0)
    parts, rows, width = values.shape
    return gathered.transpose(2, 1, 0, 3, 4).reshape(parts, -1, width)


class Streams:
    def __init__(self):
        self.under_way = {}
        self.done = {}
        self.started = set()
        self.blocks = []

    def _take(self, name, stages, value):
        try:
            self.under_way[name] = (stages, stages.send(value))
        except StopIteration as end:
            self.under_way.pop(name, None)
            self.done[name] = end.value

    def start(self, name, stages):
        self.started.add(name)
        self._take(name, stages, None)

    def advance(self, names, *anchors):
        names = [name for name in names if name in self.under_way]
        values = [self.under_way[name][1] for name in names]
        values, anchors = lax.optimization_barrier((values, anchors))
        for name, value in zip(names, values):
            self._take(name, self.under_way[name][0], value)
        return anchors[0] if len(anchors) == 1 else anchors

    def finish(self, names):
        while any(name in self.under_way for name in names):
            self.advance(names)


def part_rows(weight, start, rows):
    return lax.dynamic_slice_in_dim(weight, start, rows, axis=0)


def on_device(
    layer_input,
    segments,
    routes,
    cotangent,
    norm1_gain,
    in_weight,
    conv_weight,
    conv_bias,
    xproj_weight,
    dtproj_weight,
    dt_bias,
    a_log,
    skip_gain,
    out_weight,
    norm2_gain,
    router_weight,
    up_weight,
    down_weight,
):
    seq_len, model_width = layer_input.shape[2:]
    sequences = layer_input.shape[0] * layer_input.shape[1]
    tokens = sequences * seq_len
    expert_devices = lax.axis_size("expert")
    dp_devices = lax.axis_size("dp")
    devices = dp_devices * expert_devices
    assert up_weight.shape[0] == 1
    expert_count = expert_devices
    capacity = seq_len * 5 // (4 * expert_count)
    padded_capacity = -(-capacity // 16) * 16
    slots = sequences * padded_capacity
    taps = conv_weight.shape[0]
    rank = dtproj_weight.shape[0]
    states = a_log.shape[0]
    channels = skip_gain.shape[0]
    inner_width = channels * devices
    steps = dp_devices // 2
    expert_index = lax.axis_index("expert")
    small = jnp.concatenate(
        [
            xproj_weight,
            dtproj_weight.T,
            a_log.T,
            conv_weight.T,
            conv_bias[:, None],
            dt_bias[:, None],
            skip_gain[:, None],
        ],
        axis=1,
    )
    streams = Streams()

    def ring_blocks(block):
        ring = mesh_rings()[0]
        blocks = streams.blocks
        blocks.append(block)
        for _ in range(steps - 1):
            blocks.append((yield ring.hop(blocks[-1])))
        return blocks

    in_block = lax.dynamic_index_in_dim(
        in_weight.reshape(2, expert_devices, channels, model_width), expert_index, 1, keepdims=False
    ).reshape(2 * channels, model_width)
    streams.start("in", far_gather(in_block))
    streams.start("small", small_gather(small))
    for _ in range(steps - 1):
        streams.advance(("in", "small"))
    in_blocks = streams.done["in"].reshape(2, -1, model_width)
    with jax.named_scope("fetch_in"):
        in_cube = cube_gather(jnp.concatenate([in_blocks[0], in_blocks[1]], axis=1))
    expert_block = jnp.concatenate([up_weight[0], down_weight[0]], axis=0)
    expert_block = lax.optimization_barrier((expert_block, in_blocks))[0]
    streams.start("expert", ring_blocks(expert_block))
    for _ in range(3):
        streams.advance(("small",))
    out_block = part_rows(out_weight, expert_index * channels, channels)
    out_block = streams.advance(("small", "expert"), out_block)
    streams.start("out", far_and_pair(out_block))
    streams.finish(("small",))
    small_full = streams.done["small"]
    xproj_width = rank + 2 * states
    xproj_full = small_full[:, :xproj_width]
    across = small_full[:, xproj_width:].T
    dtproj_full = across[:rank]
    across = across[rank:].astype(jnp.float32)
    log_rates = across[:states]
    conv_full = across[states : states + taps]
    convb_full = across[states + taps]
    dtb_full = across[states + taps + 1]
    skip_full = across[states + taps + 2]
    conv_rows = jnp.concatenate(
        [
            conv_full,
            convb_full[None],
            skip_full[None],
            jnp.zeros((ROWS - taps - 2, inner_width), jnp.float32),
        ],
        axis=0,
    )
    segment_rows = segments.reshape(sequences, seq_len)
    masks = [same_document(segment_rows, offset)[:, :, None] for offset in range(taps)]
    mask_columns = jnp.concatenate([mask.reshape(tokens, 1) for mask in masks], axis=1)
    rate = -jnp.exp(log_rates)
    rate_two = rate * LOG2E
    route_rows = routes.reshape(sequences, seq_len)
    placed = dispatch_matrices(
        route_rows ^ expert_index.astype(jnp.int32), expert_count, capacity, padded_capacity
    )
    conv_rows, mask_columns, xproj_full, dtproj_full, rate_two, placed, dtb_full = streams.advance(
        ("out",), conv_rows, mask_columns, xproj_full, dtproj_full, rate_two, placed, dtb_full
    )
    streams.finish(("out",))
    with jax.named_scope("fetch_out"):
        out_full = cube_gather(streams.done["out"].reshape(-1, model_width))
    gain_one = norm1_gain.astype(jnp.float32)
    gain_two = norm2_gain.astype(jnp.float32)
    router_full = router_weight.astype(jnp.float32)

    def split(values):
        return values.reshape(sequences, seq_len, values.shape[-1])

    def flat(values):
        return values.reshape(tokens, values.shape[-1])

    rows_in = layer_input.reshape(tokens, model_width).astype(jnp.float32)
    cot_rows = cotangent.reshape(tokens, model_width).astype(jnp.float32)
    normed_one, norm_pull = jax.vjp(rms_scale, rows_in, gain_one)
    normed_low = normed_one.astype(LOW)
    inner, gate_in, conv_out, projected = run_conv_forward(
        normed_low, in_cube, mask_columns, conv_rows, xproj_full
    )
    gate_in, conv_out = split(gate_in), split(conv_out)
    dt_low = projected[:, :rank].astype(LOW)
    b_wide = jnp.broadcast_to(
        split(projected[:, rank : rank + states])[..., None], (sequences, seq_len, states, LANES)
    )
    c_wide = jnp.broadcast_to(
        split(projected[:, rank + states :])[..., None], (sequences, seq_len, states, LANES)
    )
    dt_sum = split(dot(dt_low, dtproj_full, ((1,), (0,)))) + dtb_full
    delta = jax.nn.softplus(dt_sum)
    decay = jnp.where(masks[1] > 0, delta, FAR)
    drive = delta * conv_out
    scanned = run_forward(decay, drive, b_wide, c_wide, rate_two)
    scanned = streams.advance(("expert",), scanned)
    mixed = scanned + skip_full * conv_out
    gate_silu = jax.nn.silu(gate_in)
    mixed_low = flat(mixed * gate_silu).astype(LOW)
    residual = rows_in + dot(mixed_low, out_full, ((1,), (0,)))

    chosen_rows = (
        route_rows.reshape(tokens, 1) == jnp.arange(expert_count, dtype=jnp.int32)[None]
    ).astype(jnp.float32)

    def route_piece(resid_value, gain_value, router_value):
        return norm_route(resid_value, gain_value, router_value, chosen_rows)

    (normed_two, gate_row), route_pull = jax.vjp(route_piece, residual, gain_two, router_full)
    sending = split(
        jnp.concatenate(
            [normed_two.astype(LOW), (cot_rows * gate_row[:, None]).astype(LOW)], axis=1
        )
    )

    def partners(cross, k):
        place = lambda d, e: d * expert_devices + e
        return [
            (place(d, e), place(d ^ cross, e ^ k))
            for d in range(dp_devices)
            for e in range(expert_devices)
        ]

    def exchange(piece, cross, k):
        if not cross and not k:
            return piece
        return lax.ppermute(piece, BOTH, partners(cross, k))

    pieces = [
        jnp.einsum("stk,std->skd", matrix, sending, preferred_element_type=jnp.float32).astype(LOW)
        for matrix in placed
    ]
    with jax.named_scope("send_rows"):
        received = [
            [exchange(pieces[k], cross, k).reshape(slots, -1) for k in range(expert_count)]
            for cross in (0, 1)
        ]

    units = up_weight.shape[1]
    while len(streams.blocks) < steps - 1:
        streams.advance(("expert",))
    early = streams.blocks[: steps - 1]
    own_rows, own_active, own_d_hidden, own_total = run_expert_first(received[0], early)
    cross_rows, cross_active, cross_d_hidden, cross_total = run_expert_first(received[1], early)
    own_total, cross_total = streams.advance(("expert",), own_total, cross_total)
    results, last_active, last_d_hidden = run_expert_last(
        expert_count,
        [own_rows, cross_rows],
        [own_total, cross_total],
        streams.done["expert"][steps - 1],
    )
    results = [
        [piece.reshape(sequences, padded_capacity, 2 * model_width) for piece in group]
        for group in results
    ]
    extent = own_rows.shape[0]
    kept = [
        (own_rows, own_active, own_d_hidden, last_active[:extent], last_d_hidden[:extent]),
        (cross_rows, cross_active, cross_d_hidden, last_active[extent:], last_d_hidden[extent:]),
    ]
    kept, results = lax.optimization_barrier((kept, results))
    with jax.named_scope("send_results"):
        arrived = [
            [exchange(results[cross][k], cross, k) for k in range(expert_count)]
            for cross in (0, 1)
        ]
    kept, arrived[0] = lax.optimization_barrier((kept, arrived[0]))
    up_terms = [0.0] * steps
    down_terms = [0.0] * steps
    for rows, active_rows, d_hidden_rows, last_active, last_d_hidden in kept:
        for k in range(steps):
            part = slice(k * units, (k + 1) * units)
            active_k = active_rows[:, part] if k < steps - 1 else last_active
            d_hidden_k = d_hidden_rows[:, part] if k < steps - 1 else last_d_hidden
            up_terms[k] = up_terms[k] + dot(d_hidden_k, rows[:, :model_width], ((0,), (0,)))
            down_terms[k] = down_terms[k] + dot(active_k, rows[:, model_width:], ((0,), (0,)))
    terms = [
        jnp.concatenate([up.astype(LOW), down.astype(LOW)], axis=0)
        for up, down in zip(up_terms, down_terms)
    ]
    terms, arrived[1] = lax.optimization_barrier((terms, arrived[1]))
    streams.start("expert_grad", ring_sum(terms))
    streams.advance(("expert_grad",))
    gathered_both = 0.0
    for k in range(expert_count):
        total = (arrived[0][k].astype(jnp.float32) + arrived[1][k].astype(jnp.float32)).astype(LOW)
        gathered_both = gathered_both + jnp.einsum(
            "stk,skd->std", placed[k], total, preferred_element_type=jnp.float32
        )
    gathered_both = flat(gathered_both)
    gathered = gathered_both[:, :model_width]
    d_sent = gathered_both[:, model_width:]
    layer_output = (residual + gate_row[:, None] * gathered).astype(LOW)


    d_gate = jnp.sum(cot_rows * gathered, axis=1)
    d_resid_norm, d_gain_two, d_router = route_pull((d_sent, d_gate))
    d_residual = cot_rows + d_resid_norm
    d_branch_low = d_residual.astype(LOW)

    out_gate_term, d_gate_low, d_scanned = run_gate_backward(
        d_branch_low, normed_low, out_full, mixed_low, flat(mixed), flat(gate_in)
    )
    with jax.named_scope("reduce_out_gate"):
        out_gate_blocks = cube_scatter(out_gate_term)
    d_scanned = split(d_scanned)
    d_scan, d_dt_low, d_dt_rows, more_rows, d_b, d_c = run_backward(
        decay,
        drive,
        b_wide,
        c_wide,
        rate_two,
        d_scanned,
        delta,
        conv_out,
        dt_sum,
        skip_full[None],
        dtproj_full,
    )
    d_scan = streams.advance(("expert_grad",), d_scan)
    streams.advance(("expert_grad",))
    d_dt_low = flat(d_dt_low)
    d_proj_low = jnp.concatenate(
        [
            flat(d_dt_rows),
            d_b[:, 0].reshape(tokens, states),
            d_c[:, 0].reshape(tokens, states),
        ],
        axis=1,
    ).astype(LOW)
    more_rows = jnp.sum(more_rows, axis=0)
    inner_term, d_normed = run_conv_backward(
        flat(d_scan),
        inner,
        d_gate_low,
        d_proj_low,
        normed_low,
        mask_columns,
        conv_rows,
        xproj_full,
        in_cube,
        d_dt_low,
        dt_low,
        more_rows,
    )
    inner_term, d_normed, out_gate_blocks = streams.advance(
        ("expert_grad",), inner_term, d_normed, out_gate_blocks
    )
    with jax.named_scope("reduce_inner"):
        inner_blocks = cube_scatter(inner_term)
    out_blocks = out_gate_blocks[:, :model_width]
    gate_blocks = out_gate_blocks[:, model_width:]
    streams.start(
        "out_grad", far_and_pair_sum(out_blocks.reshape(-1, 2, channels, model_width))
    )
    d_rows_norm, d_gain_one = norm_pull(d_normed)
    input_grad = d_residual + d_rows_norm

    gains = jnp.concatenate([d_gain_one[None], d_gain_two[None], d_router.T], axis=0)
    streams.start("gains", near_sum(gains))
    streams.advance(("out_grad",))
    streams.finish(("out_grad",))
    out_part = streams.advance(("expert_grad",), streams.done["out_grad"])
    streams.finish(("gains",))
    gains = streams.done["gains"]
    inner_blocks = streams.advance(("expert_grad",), inner_blocks)
    half = (steps // 2, 2, channels, model_width)
    streams.start(
        "in_grad",
        far_sum(inner_blocks[:, :model_width].reshape(half), gate_blocks.reshape(half)),
    )
    small_blocks = inner_blocks[:, model_width:]
    streams.start(
        "small_grad",
        far_and_pair_sum(small_blocks.reshape(-1, 2, channels, small_blocks.shape[1])),
    )
    streams.advance(("small_grad",))
    streams.start("out_rows", shared_rows(out_part[None]))
    gains = streams.advance(("in_grad",), gains)
    streams.start("in_rows", shared_rows(streams.done["in_grad"]))
    streams.start("gains", butterfly(gains, "dp", 2, dp_devices))
    streams.advance(("in_rows", "out_rows", "gains"))
    streams.finish(("in_rows", "out_rows", "gains", "small_grad", "expert_grad"))
    gains = streams.done["gains"]
    in_grad = streams.done["in_rows"].reshape(in_weight.shape).astype(jnp.float32)
    out_grad = streams.done["out_rows"][0].astype(jnp.float32)
    expert_grad = streams.done["expert_grad"].astype(jnp.float32)
    up_grad, down_grad = expert_grad[:units], expert_grad[units:]
    small_grad = streams.done["small_grad"].astype(jnp.float32)
    xproj_grad = small_grad[:, :xproj_width]
    row_grads = small_grad[:, xproj_width:].T
    dtproj_grad = row_grads[:rank]
    row_grads = row_grads[rank:]
    conv_grad = row_grads[:taps]
    convb_grad = row_grads[taps]
    alog_grad = row_grads[ROWS : ROWS + states]
    dtb_grad, skip_grad = row_grads[ROWS + states], row_grads[ROWS + states + 1]

    return (
        layer_output.reshape(layer_input.shape),
        input_grad.reshape(layer_input.shape),
        gains[0],
        in_grad,
        conv_grad,
        convb_grad,
        xproj_grad,
        dtproj_grad,
        dtb_grad,
        alog_grad,
        skip_grad,
        out_grad,
        gains[1],
        gains[2:].T,
        up_grad[None],
        down_grad[None],
    )


def solution(mesh):
    placed = (
        P(None, ("dp", "expert"), None, None),
        P(None, ("dp", "expert"), None),
        P(None, ("dp", "expert"), None, None),
        P(None, ("dp", "expert"), None, None),
        P(),
        P("dp", None),
        P(None, ("dp", "expert")),
        P(("dp", "expert")),
        P(("dp", "expert"), None),
        P(None, ("dp", "expert")),
        P(("dp", "expert")),
        P(None, ("dp", "expert")),
        P(("dp", "expert")),
        P("dp", None),
        P(),
        P(),
        P("expert", "dp", None),
        P("expert", "dp", None),
    )
    return jax.shard_map(
        on_device,
        mesh=mesh,
        in_specs=placed,
        out_specs=(
            P(None, ("dp", "expert"), None, None),
            P(None, ("dp", "expert"), None, None),
            P(),
            P("dp", None),
            P(None, ("dp", "expert")),
            P(("dp", "expert")),
            P(("dp", "expert"), None),
            P(None, ("dp", "expert")),
            P(("dp", "expert")),
            P(None, ("dp", "expert")),
            P(("dp", "expert")),
            P("dp", None),
            P(),
            P(),
            P("expert", "dp", None),
            P("expert", "dp", None),
        ),
        check_vma=False,
    )
```
